256 devices in a mesh: group: 8 (over z), tok: 32 (over y, x, core).
Axes of the slice: x: 4, y: 4, z: 8, core: 2. Of those that a mesh axis runs over, the one named last changes fastest.
Arguments:
- tokens: bfloat16 [16384, 1792], P(('group', 'tok')), may hold values from -6 to 6
- norm_gains: float32 [2, 1792], replicated, may hold values from 0.25 to 1.75
- qk_weight: bfloat16 [2, 256, 1792], replicated, may hold values from -0.125 to 0.125
- mixer_weight: bfloat16 [3, 1792, 1792], P(None, 'tok'), may hold values from -0.125 to 0.125
- conv_weight: float32 [3, 1792], P(None, 'tok'), may hold values from -1 to 1
- out_weight: bfloat16 [2, 1792, 1792], P(None, 'tok'), may hold values from -0.09375 to 0.09375
- ffn_weight: bfloat16 [2, 4864, 1792], P(None, 'tok'), may hold values from -0.125 to 0.125
- down_weight: bfloat16 [4864, 1792], P('tok'), may hold values from -0.078125 to 0.078125
- cached_states: float32 [64, 273, 1792], P('group', None, 'tok'), may hold values from -8 to 8
- cached_norms: float32 [64, 273, 16], P('group'), as said below
- conv_cache: bfloat16 [64, 2, 1792], P('group', None, 'tok'), may hold values from -6 to 6
- cached_lengths: int32 [64], P('group'), may hold values from 0 to 31744
- new_lengths: int32 [8, 8], P('group'), may hold values from 1 to 1024, as said below
- state_source: int32 [64, 1], replicated, may hold values from 0 to 7; in each aligned block of 8 rows (0 to 7, 8 to 15, ...) at most 2 rows name the same one
Outputs:
- layer_out: bfloat16 [16384, 1792], P(('group', 'tok'))
- new_states: float32 [64, 273, 1792], P('group', None, 'tok')
- new_norms: float32 [64, 273, 16], P('group')
- new_cache: bfloat16 [64, 2, 1792], P('group', None, 'tok')
The draws below stay inside these ranges and needn't reach their ends.
Inputs may be any that keep to these rules, and one draw needn't show every extreme that they name: `new_lengths`: the 8 lengths of a group sum to 2048; in every group at least two requests have one new token and one has exactly 1024. `state_source`: among the 8 requests of one group, at most 2 name the same group. For every vector x of 16 entries and every slot and head, phi(x) . cached_norms[slot][:, head] is positive.
All inputs are finite; a program needn't handle non-finite values.
Results may differ from the reference program's by a relative error of at most 0.02.
Values may be sent and summed in bfloat16 or wider, within the bound.
No kernel may reach another device: no remote copies, remote signals or barrier semaphores. Data moves between devices by JAX's collectives and lax.ppermute only.
A program may use at most 128 MiB of HBM per device.

```python
import math
import jax
import jax.numpy as jnp
import numpy as np
from jax import lax

D = 1792
H = 16
FD = 16
FF = 4864
KER = 3
CAP = 2
SPAN = 1024
CONTEXT = 32768
REQ_G = 8
PHI = 273
TOKENS_G = 2048
TOKENS = 16384
REQS = 64
MOST_NEW = 1024
N_GROUP = 8
N_TOK = 32


quad_scale = 0.25 / math.sqrt(2.0)


def draw_cached_norms(key, part):
    key_one, key_two = jax.random.split(key)
    drawn = jax.random.normal(key_one, (REQS, 4, H, FD), jnp.float32)
    low_end = math.log(4.0)
    high_end = math.log(64.0)
    scales = jnp.exp(jax.random.uniform(key_two, (REQS, 4, 1, H), jnp.float32, low_end, high_end))
    ones_part = jnp.ones((REQS, 4, 1, H), jnp.float32)
    linear_part = 0.5 * jnp.transpose(drawn, (0, 1, 3, 2))
    outer_terms = drawn[:, :, :, :, None] * drawn[:, :, :, None, :]
    quad_part = quad_scale * jnp.transpose(outer_terms.reshape(REQS, 4, H, FD * FD), (0, 1, 3, 2))
    features = jnp.concatenate([ones_part, linear_part, quad_part], axis=2)
    return jnp.sum(scales * features, axis=1)


def draw_cached_lengths(key, part):
    key_one, key_two, key_three = jax.random.split(key, 3)
    category = jax.random.randint(key_one, (REQS,), 0, 6)
    long_lengths = jax.random.randint(key_two, (REQS,), 3, CONTEXT - SPAN + 1)
    lengths = jnp.where(category < 3, category, long_lengths)
    places = jax.random.permutation(key_three, REQS)
    lengths = lengths.at[places[0]].set(0)
    lengths = lengths.at[places[1]].set(CONTEXT - SPAN)
    return lengths.astype(jnp.int32)


def group_lengths(key):
    key_one, key_two, key_three = jax.random.split(key, 3)
    shuffled = jax.random.permutation(key_one, REQ_G).astype(jnp.int32)
    ranking = jnp.zeros((REQ_G,), jnp.int32).at[shuffled].set(jnp.arange(REQ_G, dtype=jnp.int32))
    decode_count = jax.random.randint(key_two, (), 2, 4).astype(jnp.int32)
    is_decode = ranking < decode_count
    is_longest = ranking == decode_count
    middle_rows = jnp.logical_not(is_decode | is_longest)
    middle_count = REQ_G - decode_count - 1
    spare_rows = TOKENS_G - decode_count - MOST_NEW - middle_count
    draw_weights = jnp.where(middle_rows, jax.random.randint(key_three, (REQ_G,), 1, 65), 0).astype(jnp.int32)
    extra_rows = (spare_rows * draw_weights // jnp.sum(draw_weights)).astype(jnp.int32)
    room_left = jnp.where(middle_rows, MOST_NEW - 1, 0).astype(jnp.int32)
    extra_rows = jnp.minimum(extra_rows, room_left)
    leftover = spare_rows - jnp.sum(extra_rows)
    free_room = room_left - extra_rows
    before = (jnp.cumsum(free_room) - free_room).astype(jnp.int32)
    extra_rows = extra_rows + jnp.clip(leftover - before, 0, free_room)
    lengths = jnp.where(is_decode, 1, jnp.where(is_longest, MOST_NEW, 1 + extra_rows))
    return lengths.astype(jnp.int32)


def draw_new_lengths(key, part):
    group_keys = jax.random.split(jax.random.fold_in(key, 17), N_GROUP)
    return jax.vmap(group_lengths)(group_keys).astype(jnp.int32)


def levels(rng, shape, pieces, low, largest):
    gain, own = 1.0, jax.random.fold_in(rng, 6)
    for dim, parts in pieces:
        draws = jnp.exp(jax.random.uniform(jax.random.fold_in(own, dim), (parts,), jnp.float32, low / len(pieces), largest / len(pieces)))
        gain = gain * jnp.repeat(draws, shape[dim] // parts).reshape([-1 if axis == dim else 1 for axis in range(len(shape))])
    return gain


def deal_out(own_key, own, number, rows, number_of, top, most, skew):
    order = jax.random.permutation(own_key, number_of)
    packed, common = load_shares(number_of, rows * top, most, skew, True), load_shares(number_of, rows * top, most, skew, False)
    places = jnp.arange(number_of)

    def named(tallies, rotation):
        used = int((tallies > 0).sum())
        fixed = max(1, used // 4)
        shifted = fixed + (places - fixed + rotation * (used - fixed)) % max(1, number_of - fixed)
        return jnp.zeros((number_of,), jnp.int32).at[order[jnp.where(places < fixed, places, shifted)]].set(jnp.asarray(tallies, jnp.int32))

    tallies = jnp.where(number % 4 == 0, named(packed, number // 4), named(common, number - number // 4 - 1))
    mixed = jax.random.permutation(jax.random.fold_in(own, 3), number_of)
    donor, sink = mixed[0:number_of // 2 * 2:2], mixed[1:number_of // 2 * 2:2]
    room = jnp.minimum(tallies[donor] - 1, most - tallies[sink]) // 2
    room = jnp.where((donor == order[0]) | (sink == order[0]) | (tallies[sink] == 0), 0, jnp.maximum(room, 0))
    shifted = jax.random.randint(jax.random.fold_in(own, 4), (number_of // 2,), 0, 1 << 20) % (room + 1)
    tallies = tallies.at[donor].add(-shifted).at[sink].add(shifted)
    items = jnp.searchsorted(jnp.cumsum(tallies), jnp.arange(rows * top), side="right").astype(jnp.int32)
    listing = items.reshape(top, rows).T
    listing = listing[jax.random.permutation(jax.random.fold_in(own, 1), rows)]
    rotation = jax.random.randint(jax.random.fold_in(own, 2), (rows, 1), 0, top)
    return jnp.take_along_axis(listing, (jnp.arange(top)[None, :] + rotation) % top, axis=1)


def load_shares(number_of, total, limit, skew, full):
    weights = [(1 << 20) // math.isqrt(standing ** skew) + 1 for standing in range(1, number_of + 1)]
    largest = limit if full else min(limit, max(-(-total // number_of), total * weights[0] // sum(weights)))
    least = 1 if total - largest >= number_of - 1 else 0
    holding, rest = [largest] + [least] * (number_of - 1), total - largest - least * (number_of - 1)
    while rest > 0:
        movable = [i for i in range(1, number_of) if holding[i] < largest] or [i for i in range(1, number_of) if holding[i] < limit]
        pool, budget = sum([weights[i] for i in movable]), rest
        for i in movable:
            extra = min(limit - holding[i], max(1, budget * weights[i] // pool), rest)
            holding[i] = holding[i] + extra
            rest = rest - extra
    return np.array(holding)


def gaussian(rng, extent, width, limit, shards=(), kind=jnp.bfloat16):
    entries = width * jax.random.normal(rng, extent, jnp.float32)
    if shards:
        entries = entries * levels(rng, extent, shards, -0.22, 0.18)
    return jnp.clip(entries, -limit, limit).astype(kind)


def setup_inputs(seed: int = 0) -> dict:
    streams_of = jax.random.split(jax.random.key(seed), 15)
    tokens = gaussian(streams_of[0], (TOKENS, D), 1.0, 6.0, ((0, 256),))
    norm_gains = jnp.clip(1.0 + 0.15 * jax.random.normal(streams_of[1], (2, D), jnp.float32), 0.25, 1.75)
    qk_weight = gaussian(streams_of[2], (2, H * FD, D), D ** -0.5, 0.125)
    mixer_weight = gaussian(streams_of[3], (3, D, D), D ** -0.5, 0.125, ((1, 32),))
    conv_weight = jnp.clip(jax.random.uniform(streams_of[4], (KER, D), jnp.float32, -1.0, 1.0) * levels(streams_of[4], (KER, D), ((1, 32),), -0.4, 0.0), -1.0, 1.0)
    out_weight = gaussian(streams_of[5], (2, D, D), (2 * D) ** -0.5, 0.09375, ((1, 32),))
    ffn_weight = gaussian(streams_of[6], (2, FF, D), D ** -0.5, 0.125, ((1, 32),))
    down_weight = gaussian(streams_of[7], (FF, D), FF ** -0.5, 0.078125, ((0, 32),))
    cached_states = gaussian(streams_of[8], (REQS, PHI, D), 2.0, 8.0, ((0, 8), (2, 32)), jnp.float32)
    cached_norms = draw_cached_norms(jax.random.fold_in(streams_of[14], 71), 0)
    conv_cache = gaussian(streams_of[10], (REQS, 2, D), 1.0, 6.0, ((0, 8), (2, 32)))
    cached_lengths = draw_cached_lengths(jax.random.fold_in(streams_of[14], 71), 0)
    new_lengths = draw_new_lengths(jax.random.fold_in(streams_of[14], 71), 0)
    state_source_keys = jax.random.split(jax.random.fold_in(streams_of[13], 1), REQS // REQ_G)
    state_source_turns = jax.random.permutation(jax.random.fold_in(streams_of[13], 3), REQS // REQ_G)
    state_source = jax.vmap(lambda own, number: deal_out(jax.random.fold_in(streams_of[13], 2), own, number, REQ_G, N_GROUP, 1, CAP, 2))(state_source_keys, state_source_turns).reshape((REQS, 1))
    return {"tokens": tokens, "norm_gains": norm_gains, "qk_weight": qk_weight, "mixer_weight": mixer_weight, "conv_weight": conv_weight, "out_weight": out_weight, "ffn_weight": ffn_weight, "down_weight": down_weight, "cached_states": cached_states, "cached_norms": cached_norms, "conv_cache": conv_cache, "cached_lengths": cached_lengths, "new_lengths": new_lengths, "state_source": state_source}


epsilon = 1e-05
quad_scale = 0.25 / math.sqrt(2.0)
highest = lax.Precision.HIGHEST

def rms_scale(inputs, gain_row):
    widened = inputs.astype(jnp.float32)
    mean_sq = lax.optimization_barrier(jnp.mean(widened * widened, axis=-1, keepdims=True))
    return widened * lax.rsqrt(mean_sq + epsilon) * gain_row

def taylor_features(vectors):
    row_count = vectors.shape[0]
    feat_count = vectors.shape[1]
    outer_terms = (vectors[:, :, None] * vectors[:, None, :]).reshape(row_count, feat_count * feat_count)
    return jnp.concatenate([jnp.ones((row_count, 1), jnp.float32), 0.5 * vectors, quad_scale * outer_terms], axis=1)

def segment_layout(lengths, all_rows):
    request_ends = jnp.cumsum(lengths).astype(jnp.int32)
    request_starts = (request_ends - lengths).astype(jnp.int32)
    position = jnp.arange(all_rows, dtype=jnp.int32)
    segment = lax.optimization_barrier(jnp.sum((position[:, None] >= request_ends[None, :]).astype(jnp.int32), axis=1)).astype(jnp.int32)
    member = segment[:, None] == jnp.arange(lengths.shape[0], dtype=jnp.int32)[None, :]
    offset = (position - lax.optimization_barrier(jnp.sum(jnp.where(member, request_starts[None, :], 0), axis=1))).astype(jnp.int32)
    return (request_ends, segment, member, offset)

def head_attention(queries, keys_head, values_head, state_head, norm_head, segment, member, query_block):
    all_rows = queries.shape[0]
    requests, phi_size, value_width = state_head.shape
    state_flat = jnp.transpose(state_head, (1, 0, 2)).reshape(phi_size, requests * value_width)
    position = jnp.arange(all_rows, dtype=jnp.int32)
    pieces_out = []
    for first_row in range(0, all_rows, query_block):
        query_rows = queries[first_row:first_row + query_block]
        scores = lax.dot_general(query_rows, keys_head, (((1,), (1,)), ((), ())), precision=highest)
        kernel = 1.0 + 0.25 * scores + scores * scores / 32.0
        allowed = (segment[first_row:first_row + query_block, None] == segment[None, :]) & (position[None, :] <= position[first_row:first_row + query_block, None])
        kernel = jnp.where(allowed, kernel, 0.0)
        local_den = lax.optimization_barrier(jnp.sum(kernel, axis=1))
        local_num = jnp.dot(kernel.astype(jnp.bfloat16), values_head, preferred_element_type=jnp.float32)
        features = taylor_features(query_rows)
        carried = jnp.dot(features, state_flat, precision=highest).reshape(query_block, requests, value_width)
        owner = member[first_row:first_row + query_block]
        carried_num = lax.optimization_barrier(jnp.sum(jnp.where(owner[:, :, None], carried, 0.0), axis=1))
        carried_den = lax.optimization_barrier(jnp.sum(jnp.where(owner, jnp.dot(features, norm_head.T, precision=highest), 0.0), axis=1))
        pieces_out.append((local_num + carried_num) / (local_den + carried_den)[:, None])
    return jnp.concatenate(pieces_out, axis=0).astype(jnp.bfloat16)

def state_update(keys_head, values_head, member, state_head, norm_head):
    all_rows = keys_head.shape[0]
    requests, phi_size, value_width = state_head.shape
    features = taylor_features(keys_head)
    weights = member.astype(jnp.float32)
    spread = (weights[:, :, None] * values_head.astype(jnp.float32)[:, None, :]).reshape(all_rows, requests * value_width)
    added_state = lax.dot_general(features, spread, (((0,), (0,)), ((), ())), precision=highest)
    added_state = jnp.transpose(added_state.reshape(phi_size, requests, value_width), (1, 0, 2))
    norm_added = lax.dot_general(weights, features, (((0,), (0,)), ((), ())), precision=highest)
    return (state_head + added_state, norm_head + norm_added)

def short_conv(inputs, conv_gate, conv_taps, conv_state, cached_length, lengths, request_ends, member, offset):
    all_rows = inputs.shape[0]
    channels = inputs.shape[1]
    cached = conv_state.astype(jnp.float32)
    last_cached = cached[:, 1] * (cached_length >= 1).astype(jnp.float32)[:, None]
    second_cached = cached[:, 0] * (cached_length >= 2).astype(jnp.float32)[:, None]
    last_rows = lax.optimization_barrier(jnp.sum(jnp.where(member[:, :, None], last_cached[None], 0.0), axis=1))
    second_rows = lax.optimization_barrier(jnp.sum(jnp.where(member[:, :, None], second_cached[None], 0.0), axis=1))
    shift_one = jnp.concatenate([jnp.zeros((1, channels), jnp.float32), inputs[:-1]], axis=0)
    shift_two = jnp.concatenate([jnp.zeros((2, channels), jnp.float32), inputs[:-2]], axis=0)
    within = offset[:, None]
    prev_one = jnp.where(within >= 1, shift_one, last_rows)
    prev_two = jnp.where(within >= 2, shift_two, jnp.where(within == 1, last_rows, second_rows))
    convolved = conv_taps[0] * inputs + conv_taps[1] * prev_one + conv_taps[2] * prev_two
    conv_out = (convolved * conv_gate).astype(jnp.bfloat16)
    position = jnp.arange(all_rows, dtype=jnp.int32)
    at_end = position[None, :] == (request_ends - 1)[:, None]
    before_end = position[None, :] == (request_ends - 2)[:, None]
    final_rows = lax.optimization_barrier(jnp.sum(jnp.where(at_end[:, :, None], inputs[None], 0.0), axis=1))
    penultimate = lax.optimization_barrier(jnp.sum(jnp.where(before_end[:, :, None], inputs[None], 0.0), axis=1))
    penultimate = jnp.where((lengths >= 2)[:, None], penultimate, last_cached)
    return (conv_out, jnp.stack([penultimate, final_rows], axis=1).astype(jnp.bfloat16))

def shard_sum(left_rows, right_rows, shard_count):
    shard_width = left_rows.shape[1] // shard_count

    def add_shard(shard_index, running):
        begin = (shard_index * shard_width).astype(jnp.int32)
        left_part = lax.dynamic_slice_in_dim(left_rows, begin, shard_width, 1)
        right_part = lax.dynamic_slice_in_dim(right_rows, begin, shard_width, 0)
        partial_value = jnp.dot(left_part, right_part, preferred_element_type=jnp.float32)
        return running + lax.optimization_barrier(partial_value.astype(jnp.bfloat16)).astype(jnp.float32)
    blank = jnp.zeros((left_rows.shape[0], right_rows.shape[1]), jnp.float32)
    return lax.fori_loop(0, shard_count, add_shard, blank)

def reference(tokens, norm_gains, qk_weight, mixer_weight, conv_weight, out_weight, ffn_weight, down_weight, cached_states, cached_norms, conv_cache, cached_lengths, new_lengths, state_source):
    head_width = D // H
    query_block = math.gcd(TOKENS_G, 512)
    request_slot = (jnp.arange(REQS, dtype=jnp.int32) % REQ_G).astype(jnp.int32)
    slots = (state_source[:, 0] * REQ_G + request_slot).astype(jnp.int32)
    has_state = (cached_lengths > 0).astype(jnp.float32)[:, None, None]
    start_states = cached_states[slots] * has_state
    start_norms = cached_norms[slots] * has_state
    start_cache = conv_cache[slots]
    out_rows = jnp.transpose(out_weight.reshape(2, N_TOK, D // N_TOK, D), (1, 0, 2, 3)).reshape(2 * D, D)
    layer_parts = []
    state_parts = []
    norm_parts = []
    cache_parts = []
    for group_id in range(N_GROUP):
        rows_low = group_id * TOKENS_G
        group_rows = tokens[rows_low:rows_low + TOKENS_G]
        req_low = group_id * REQ_G
        lengths = new_lengths[group_id]
        request_ends, segment, member, offset = segment_layout(lengths, TOKENS_G)
        normed = rms_scale(group_rows, norm_gains[0]).astype(jnp.bfloat16)
        values = jnp.dot(normed, mixer_weight[0].T, preferred_element_type=jnp.float32).astype(jnp.bfloat16)
        conv_in = jnp.dot(normed, mixer_weight[1].T, preferred_element_type=jnp.float32)
        conv_gate = jnp.dot(normed, mixer_weight[2].T, preferred_element_type=jnp.float32)
        queries = jnp.dot(normed, qk_weight[0].T, preferred_element_type=jnp.float32)
        keys_all = jnp.dot(normed, qk_weight[1].T, preferred_element_type=jnp.float32)
        head_queries = jnp.transpose(queries.reshape(TOKENS_G, H, FD), (1, 0, 2))
        head_keys = jnp.transpose(keys_all.reshape(TOKENS_G, H, FD), (1, 0, 2))
        head_values = jnp.transpose(values.reshape(TOKENS_G, H, head_width), (1, 0, 2))
        group_states = start_states[req_low:req_low + REQ_G]
        head_states = jnp.transpose(group_states.reshape(REQ_G, PHI, H, head_width), (2, 0, 1, 3))
        head_norms = jnp.transpose(start_norms[req_low:req_low + REQ_G], (2, 0, 1))

        def one_head(operands):
            query_part, key_part, value_part, state_part, norm_part = operands
            attended_head = head_attention(query_part, key_part, value_part, state_part, norm_part, segment, member, query_block)
            state_next, norm_next = state_update(key_part, value_part, member, state_part, norm_part)
            return (attended_head, state_next, norm_next)
        attended, state_next, norm_next = lax.map(one_head, (head_queries, head_keys, head_values, head_states, head_norms))
        attended = jnp.transpose(attended, (1, 0, 2)).reshape(TOKENS_G, D)
        state_parts.append(jnp.transpose(state_next, (1, 2, 0, 3)).reshape(REQ_G, PHI, D))
        norm_parts.append(jnp.transpose(norm_next, (1, 2, 0)))
        conv_out, cache_next = short_conv(conv_in, conv_gate, conv_weight, start_cache[req_low:req_low + REQ_G], cached_lengths[req_low:req_low + REQ_G], lengths, request_ends, member, offset)
        cache_parts.append(cache_next)
        mixer_in = jnp.stack([attended.reshape(TOKENS_G, N_TOK, D // N_TOK), conv_out.reshape(TOKENS_G, N_TOK, D // N_TOK)], axis=2).reshape(TOKENS_G, 2 * D)
        residual = group_rows.astype(jnp.float32) + shard_sum(mixer_in, out_rows, N_TOK)
        normed_ffn = rms_scale(residual, norm_gains[1]).astype(jnp.bfloat16)
        gate_part = jnp.dot(normed_ffn, ffn_weight[0].T, preferred_element_type=jnp.float32)
        up_part = jnp.dot(normed_ffn, ffn_weight[1].T, preferred_element_type=jnp.float32)
        hidden = (jax.nn.silu(gate_part) * up_part).astype(jnp.bfloat16)
        layer_parts.append((residual + shard_sum(hidden, down_weight, N_TOK)).astype(jnp.bfloat16))
    return (jnp.concatenate(layer_parts, axis=0), jnp.concatenate(state_parts, axis=0), jnp.concatenate(norm_parts, axis=0), jnp.concatenate(cache_parts, axis=0))
```

```python
import math

import jax
import jax.numpy as jnp
from jax import lax
from jax.sharding import PartitionSpec as P

epsilon = 1e-05
quad_scale = 0.25 / math.sqrt(2.0)
SIDE_Y = 4
SIDE_X = 4
CORES = 2
CHIPS = SIDE_Y * SIDE_X
f32 = jnp.float32
bf16 = jnp.bfloat16


def tok_perm(move):
    pairs = []
    for y in range(SIDE_Y):
        for x in range(SIDE_X):
            for c in range(CORES):
                ty, tx, tc = move(y, x, c)
                source = (y * SIDE_X + x) * CORES + c
                target = (ty % SIDE_Y * SIDE_X + tx % SIDE_X) * CORES + tc % CORES
                pairs.append((source, target))
    return pairs


def permute(array, move):
    return lax.ppermute(array, "tok", tok_perm(move))


def swap_cores(array):
    return permute(array, lambda y, x, c: (y, x, 1 - c))


def shift(array, axis, step):
    if axis == "x":
        return permute(array, lambda y, x, c: (y, x + step, c))
    return permute(array, lambda y, x, c: (y + step, x, c))


def ring_gather(own, axis):
    half = own.shape[0] // 2
    from_next = shift(own, axis, -1)
    from_prev = shift(own, axis, 1)
    far_low = shift(from_next[:half], axis, -1)
    far_high = shift(from_prev[half:], axis, 1)
    return [own, from_next, jnp.concatenate([far_low, far_high], axis=0), from_prev]


def gather_chips(own):
    rows, width = own.shape
    half = rows // 2
    first = own[:half]
    second = own[half:]
    row_a = jnp.stack(ring_gather(first, "x"), axis=0)
    col_b = jnp.stack(ring_gather(second, "y"), axis=0)
    whole_a = jnp.stack(ring_gather(row_a, "y"), axis=0)
    whole_b = jnp.stack(ring_gather(col_b, "x"), axis=0)
    return whole_a, whole_b


def ring_reduce(parts, axis):
    half = parts[0].shape[0] // 2
    far_up = shift(parts[2][:half], axis, 1)
    far_down = shift(parts[2][half:], axis, -1)
    up = jnp.concatenate([(parts[1][:half].astype(f32) + far_up.astype(f32)).astype(bf16), parts[1][half:]], axis=0)
    down = jnp.concatenate([parts[3][:half], (parts[3][half:].astype(f32) + far_down.astype(f32)).astype(bf16)], axis=0)
    got_up = shift(up, axis, 1)
    got_down = shift(down, axis, -1)
    return parts[0].astype(f32) + got_up.astype(f32) + got_down.astype(f32)


def scatter_chips(partial_a, partial_b):
    across_a = ring_reduce([partial_a[k] for k in range(4)], "y").astype(bf16)
    across_b = ring_reduce([partial_b[k] for k in range(4)], "x").astype(bf16)
    own_a = ring_reduce([across_a[k] for k in range(4)], "x")
    own_b = ring_reduce([across_b[k] for k in range(4)], "y")
    return jnp.concatenate([own_a, own_b], axis=0)


def rms_scale(inputs, gain_row):
    widened = inputs.astype(f32)
    mean_sq = jnp.mean(widened * widened, axis=-1, keepdims=True)
    return widened * lax.rsqrt(mean_sq + epsilon) * gain_row


def taylor_features(vectors):
    count, feat = vectors.shape
    column = jnp.arange(feat * feat, dtype=jnp.int32)
    entry = jnp.arange(feat, dtype=jnp.int32)[:, None]
    pick_a = (column[None, :] // feat == entry).astype(bf16)
    pick_b = (column[None, :] % feat == entry).astype(bf16)
    left = jnp.dot(vectors, pick_a, preferred_element_type=f32)
    right = jnp.dot(vectors, pick_b, preferred_element_type=f32)
    outer = (quad_scale * left * right).astype(bf16)
    linear = (0.5 * vectors.astype(f32)).astype(bf16)
    return jnp.concatenate(
        [jnp.ones((count, 1), bf16), linear, outer, jnp.zeros((count, 15), bf16)], axis=1
    )


def on_device(
    tokens,
    norm_gains,
    qk_weight,
    mixer_weight,
    conv_weight,
    out_weight,
    ffn_weight,
    down_weight,
    cached_states,
    cached_norms,
    conv_cache,
    cached_lengths,
    new_lengths,
    state_source,
):
    tok_rows, width = tokens.shape
    requests, phi_size, columns = cached_states.shape
    head_count = cached_norms.shape[2]
    feature = qk_weight.shape[1] // head_count
    units = ffn_weight.shape[1]
    channels = CORES * columns
    half_rows = tok_rows // 2
    rows_here = CHIPS * tok_rows
    group_now = lax.axis_index("group")
    tok_now = lax.axis_index("tok")
    core = tok_now % CORES
    chip = tok_now // CORES
    chip_y = chip // SIDE_X
    chip_x = chip % SIDE_X
    first_core = core == 0

    def both(own, other, axis):
        return jnp.where(
            first_core,
            jnp.concatenate([own, other], axis=axis),
            jnp.concatenate([other, own], axis=axis),
        )

    normed_own = rms_scale(tokens, norm_gains[0]).astype(bf16)
    normed_a, normed_b = gather_chips(normed_own)
    normed = jnp.concatenate(
        [normed_a.reshape(rows_here // 2, width), normed_b.reshape(rows_here // 2, width)], axis=0
    )

    mixer_rows = both(mixer_weight, swap_cores(mixer_weight), 1)
    out_rows = both(out_weight, swap_cores(out_weight), 1)
    taps = both(conv_weight, swap_cores(conv_weight), 1)
    ffn_other = swap_cores(ffn_weight)
    down_other = swap_cores(down_weight)
    head_qk = lax.dynamic_slice_in_dim(qk_weight, chip * feature, feature, 1)
    blank16 = jnp.zeros((16, width), bf16)
    in_rows = jnp.concatenate(
        [mixer_rows[0], head_qk[1], mixer_rows[1], head_qk[0], mixer_rows[2], blank16], axis=0
    )
    out_wide = jnp.concatenate([out_rows[0], blank16, out_rows[1], blank16], axis=0)
    pad_units = -(-CORES * units // 128) * 128 - CORES * units
    blank_units = jnp.zeros((pad_units, width), bf16)
    ffn_wide = jnp.concatenate(
        [ffn_weight[0], ffn_other[0], blank_units, ffn_weight[1], ffn_other[1], blank_units], axis=0
    )
    down_wide = jnp.concatenate([down_weight, down_other, blank_units], axis=0)

    split = 144
    rest = phi_size - split
    norm_col = lax.dynamic_slice_in_dim(cached_norms, chip, 1, 2)
    upper = jnp.concatenate(
        [
            cached_states[:, split:],
            jnp.zeros((requests, 136 - rest, columns), f32),
            conv_cache.astype(f32),
            jnp.zeros((requests, split - 138, columns), f32),
        ],
        axis=1,
    )
    norm_upper = jnp.concatenate(
        [norm_col[:, split:], jnp.zeros((requests, split - rest, 1), f32)], axis=1
    )
    packed = jnp.concatenate(
        [cached_states[:, :split], upper, norm_col[:, :split], norm_upper, jnp.zeros((requests, split, 14), f32)],
        axis=2,
    ).astype(bf16)
    gathered = lax.all_gather(packed, "group", axis=0, tiled=True)
    own_sources = lax.dynamic_slice_in_dim(state_source[:, 0], group_now * requests, requests)
    wanted = own_sources * requests + jnp.arange(requests, dtype=jnp.int32)
    slots = gathered[jnp.clip(wanted, 0, gathered.shape[0] - 1)]
    slots_other = swap_cores(slots)
    low = jnp.where(first_core, slots, slots_other)
    high = jnp.where(first_core, slots_other, slots)
    blank15 = jnp.zeros((requests, split, 15), bf16)
    top = jnp.concatenate([low[..., :columns], high[..., :columns], low[..., 112:113], blank15], axis=2)
    bottom = jnp.concatenate(
        [low[..., columns : 2 * columns], high[..., columns : 2 * columns], low[..., 113:114], blank15], axis=2
    )
    live = (cached_lengths > 0)[:, None, None]
    start_wide = jnp.where(live, jnp.concatenate([top, bottom], axis=1), 0)
    live_f = live.astype(f32)
    start_states = (
        jnp.concatenate([slots[..., :columns], slots[:, :rest, columns : 2 * columns]], axis=1).astype(f32) * live_f
    )
    start_norm = (
        jnp.concatenate([slots[..., 112], slots[:, :rest, 113]], axis=1).astype(f32) * live_f[:, :, 0]
    )
    conv_slots = jnp.concatenate([low[:, 136:138, columns : 2 * columns], high[:, 136:138, columns : 2 * columns]], axis=2)
    cached_one = jnp.where((cached_lengths >= 1)[:, None], conv_slots[:, 1], 0)
    cached_two = jnp.where((cached_lengths >= 2)[:, None], conv_slots[:, 0], 0)

    lengths = new_lengths[0]
    request_ends = jnp.cumsum(lengths)
    request_starts = request_ends - lengths
    row = jnp.arange(rows_here, dtype=jnp.int32)
    part = row // (rows_here // 2)
    major = row // (4 * half_rows) % 4
    minor = row // half_rows % 4
    dy = jnp.where(part == 0, major, minor)
    dx = jnp.where(part == 0, minor, major)
    inner = row % half_rows
    block = (chip_y + dy) % SIDE_Y * SIDE_X + (chip_x + dx) % SIDE_X
    pos_base = block * (CORES * tok_rows) + part * half_rows + inner
    pos_own = pos_base + core * tok_rows
    pos_other = pos_base + (1 - core) * tok_rows
    pos_all = jnp.concatenate([pos_own, pos_other], axis=0)

    def locate(position):
        at = position[:, None]
        return (at >= request_starts[None, :]) & (at < request_ends[None, :])

    member = locate(pos_own)
    member_all = locate(pos_all)
    row_start = jnp.sum(jnp.where(member, request_starts[None, :], 0), axis=1)

    projected = lax.dot_general(normed, in_rows, (((1,), (1,)), ((), ())), preferred_element_type=f32)
    value_key = projected[:, :128].astype(bf16)
    conv_in = projected[:, 128 : 128 + channels]
    queries = projected[:, 128 + channels : 256].astype(bf16)
    conv_gate = projected[:, 256 : 256 + channels]
    value_key_all = jnp.concatenate([value_key, swap_cores(value_key)], axis=0)
    keys_all = value_key_all[:, channels:]
    lane = jnp.arange(128, dtype=jnp.int32)[None, :]
    values_one = jnp.where(lane < channels, value_key_all, (lane == channels).astype(bf16))

    scores = lax.dot_general(queries, keys_all, (((1,), (1,)), ((), ())), preferred_element_type=f32)
    kernel = 1.0 + scores * (0.25 + scores * 0.03125)
    allowed = (pos_all[None, :] <= pos_own[:, None]) & (pos_all[None, :] >= row_start[:, None])
    weights = jnp.where(allowed, kernel, 0.0).astype(bf16)
    local = jnp.dot(weights, values_one, preferred_element_type=f32)
    query_features = taylor_features(queries)
    carried = lax.dot_general(
        jnp.broadcast_to(query_features[None], (requests,) + query_features.shape),
        start_wide,
        (((2,), (1,)), ((0,), (0,))),
        preferred_element_type=f32,
    )
    carried = jnp.sum(jnp.where(member.T[:, :, None], carried, 0.0), axis=0)
    total = local + carried
    attended = (total / total[:, channels : channels + 1]).astype(bf16)

    bound = conv_in.reshape(2, CHIPS, half_rows, channels)[1, :, half_rows - 2 :]
    bound_other = swap_cores(bound.reshape(CHIPS, 2 * channels))
    spot = jnp.arange(CHIPS, dtype=jnp.int32)
    spot_block = (chip_y + spot // SIDE_X) % SIDE_Y * SIDE_X + (chip_x + spot % SIDE_X) % SIDE_X
    before = spot_block - (1 - core)
    before = before % CHIPS
    spot_before = (before % SIDE_X - chip_x) % SIDE_X * SIDE_Y + (before // SIDE_X - chip_y) % SIDE_Y
    bound_pick = (spot_before[:, None] == spot[None, :]).astype(f32)
    bound_prev = jnp.dot(bound_pick, bound_other, precision=lax.Precision.HIGHEST).reshape(CHIPS, 2, channels)
    bound_first = conv_in.reshape(2, SIDE_Y, SIDE_X, half_rows, channels)[0, :, :, half_rows - 2 :]
    bound_first = jnp.swapaxes(bound_first, 0, 1).reshape(CHIPS, 2, channels)
    heads = jnp.stack([bound_prev, bound_first], axis=0)
    extended = jnp.concatenate([heads, conv_in.reshape(2, CHIPS, half_rows, channels)], axis=2)
    shift_one = extended[:, :, 1 : half_rows + 1].reshape(rows_here, channels)
    shift_two = extended[:, :, :half_rows].reshape(rows_here, channels)
    member_b = member.astype(bf16)
    last_rows = jnp.dot(member_b, cached_one, preferred_element_type=f32)
    second_rows = jnp.dot(member_b, cached_two, preferred_element_type=f32)
    within = (pos_own - row_start)[:, None]
    prev_one = jnp.where(within >= 1, shift_one, last_rows)
    prev_two = jnp.where(within >= 2, shift_two, jnp.where(within == 1, last_rows, second_rows))
    conv_out = ((taps[0] * conv_in + taps[1] * prev_one + taps[2] * prev_two) * conv_gate).astype(bf16)

    blank_lanes = jnp.zeros((rows_here, 128 - channels), bf16)
    mixer_in = jnp.concatenate([attended, conv_out, blank_lanes], axis=1)
    partial = jnp.dot(mixer_in, out_wide, preferred_element_type=f32).astype(bf16)
    partial = partial.reshape(2, 4, 4, half_rows, width)
    residual = tokens.astype(f32) + scatter_chips(partial[0], partial[1])

    normed_ffn_own = rms_scale(residual, norm_gains[1]).astype(bf16)
    ffn_a, ffn_b = gather_chips(normed_ffn_own)
    normed_ffn = jnp.concatenate(
        [ffn_a.reshape(rows_here // 2, width), ffn_b.reshape(rows_here // 2, width)], axis=0
    )
    both_parts = lax.dot_general(normed_ffn, ffn_wide, (((1,), (1,)), ((), ())), preferred_element_type=f32)
    wide_units = CORES * units + pad_units
    hidden = (jax.nn.silu(both_parts[:, :wide_units]) * both_parts[:, wide_units:]).astype(bf16)
    ffn_partial = jnp.dot(hidden, down_wide, preferred_element_type=f32).astype(bf16)
    ffn_partial = ffn_partial.reshape(2, SIDE_Y, SIDE_X, half_rows, width)
    layer_out = (residual + scatter_chips(ffn_partial[0], ffn_partial[1])).astype(bf16)

    key_features = taylor_features(keys_all)
    values_own = jnp.where(first_core, value_key_all[:, :columns], value_key_all[:, columns:channels])
    ones = jnp.ones((values_own.shape[0], 1), bf16)
    slab = jnp.concatenate([values_own, ones, jnp.zeros((values_own.shape[0], 64 - columns - 1), bf16)], axis=1)
    owner = jnp.repeat(member_all.astype(bf16), 64, axis=1)
    spread = jnp.tile(slab, (1, requests)) * owner
    added = lax.dot_general(key_features, spread, (((0,), (0,)), ((), ())), preferred_element_type=f32)
    added = added[:phi_size].reshape(phi_size, requests, 64)
    new_states = start_states + jnp.transpose(added[:, :, :columns], (1, 0, 2))
    norm_here = (start_norm + added[:, :, columns].T).astype(bf16)
    stage = norm_here[None]
    for move in (
        lambda y, x, c: (y, x ^ 1, c),
        lambda y, x, c: (y, x ^ 2, c),
        lambda y, x, c: (y ^ 1, x, c),
        lambda y, x, c: (y ^ 2, x, c),
    ):
        stage = jnp.concatenate([stage, permute(stage, move)], axis=0)
    head_index = jnp.arange(head_count, dtype=jnp.int32)
    head_spot = (head_index // SIDE_X ^ chip_y) * SIDE_X + (head_index % SIDE_X ^ chip_x)
    head_pick = (head_spot[:, None] == jnp.arange(CHIPS, dtype=jnp.int32)[None, :]).astype(bf16)
    new_norms = lax.dot_general(
        stage.reshape(CHIPS, requests * phi_size), head_pick, (((0,), (1,)), ((), ())), preferred_element_type=f32
    ).reshape(requests, phi_size, head_count)

    at_end = pos_own[None, :] == (request_ends - 1)[:, None]
    before_end = (pos_own[None, :] == (request_ends - 2)[:, None]) & (lengths >= 2)[:, None]
    chosen = jnp.concatenate([before_end, at_end], axis=0).astype(bf16)
    tail = jnp.dot(chosen, conv_in.astype(bf16), preferred_element_type=f32)
    tail = tail + swap_cores(tail)
    tail = tail.reshape(2, requests, channels)
    penultimate = jnp.where((lengths >= 2)[:, None], tail[0], cached_one.astype(f32))
    cache = jnp.stack([penultimate, tail[1]], axis=1).astype(bf16)
    new_cache = jnp.where(first_core, cache[..., :columns], cache[..., columns:])
    return (layer_out, new_states, new_norms, new_cache)


def solution(mesh):
    in_specs = (
        P(("group", "tok"), None),
        P(),
        P(),
        P(None, "tok", None),
        P(None, "tok"),
        P(None, "tok", None),
        P(None, "tok", None),
        P("tok", None),
        P("group", None, "tok"),
        P("group", None, None),
        P("group", None, "tok"),
        P("group"),
        P("group", None),
        P(),
    )
    out_specs = (
        P(("group", "tok"), None),
        P("group", None, "tok"),
        P("group", None, None),
        P("group", None, "tok"),
    )
    return jax.shard_map(
        on_device, mesh=mesh, in_specs=in_specs, out_specs=out_specs, check_vma=False
    )
```

```python
import math

import jax
import jax.numpy as jnp
import numpy as np
from jax import lax
from jax.experimental import pallas as pl
from jax.experimental.pallas import tpu as pltpu
from jax.sharding import PartitionSpec as P

epsilon = 1e-05
quad_scale = 0.25 / math.sqrt(2.0)
SIDE_Y = 4
SIDE_X = 4
CORES = 2
CHIPS = SIDE_Y * SIDE_X
f32 = jnp.float32
bf16 = jnp.bfloat16


def tok_perm(move):
    pairs = []
    for y in range(SIDE_Y):
        for x in range(SIDE_X):
            for c in range(CORES):
                ty, tx, tc = move(y, x, c)
                source = (y * SIDE_X + x) * CORES + c
                target = (ty % SIDE_Y * SIDE_X + tx % SIDE_X) * CORES + tc % CORES
                pairs.append((source, target))
    return pairs


def permute(array, move):
    return lax.ppermute(array, "tok", tok_perm(move))


def swap_cores(array):
    return permute(array, lambda y, x, c: (y, x, 1 - c))


def shift(array, stage, step):
    def move(y, x, c):
        if c == stage:
            return (y, x + step, c)
        return (y + step, x, c)

    return permute(array, move)


def ring_gather(own, stage):
    half = own.shape[0] // 2
    from_next = shift(own, stage, -1)
    from_prev = shift(own, stage, 1)
    far_low = shift(from_next[:half], stage, -1)
    far_high = shift(from_prev[half:], stage, 1)
    return [own, from_next, jnp.concatenate([far_low, far_high], axis=0), from_prev]


def gather_line(own):
    return jnp.concatenate(ring_gather(own, 0), axis=0)


def gather_plane(line):
    return ring_gather(line, 1)


def ring_reduce(parts, stage):
    half = parts[0].shape[0] // 2
    far_up = shift(parts[2][:half], stage, 1)
    far_down = shift(parts[2][half:], stage, -1)
    up = jnp.concatenate([(parts[1][:half].astype(f32) + far_up.astype(f32)).astype(bf16), parts[1][half:]], axis=0)
    down = jnp.concatenate([parts[3][:half], (parts[3][half:].astype(f32) + far_down.astype(f32)).astype(bf16)], axis=0)
    got_up = shift(up, stage, 1)
    got_down = shift(down, stage, -1)
    return parts[0].astype(f32) + got_up.astype(f32) + got_down.astype(f32)


def scatter_chips(partials):
    line = ring_reduce(partials, 1).astype(bf16)
    rows = line.shape[0] // 4
    return ring_reduce([line[k * rows : (k + 1) * rows] for k in range(4)], 0)


def rms_scale(inputs, gain_row):
    widened = inputs.astype(f32)
    mean_sq = jnp.mean(widened * widened, axis=-1, keepdims=True)
    return widened * lax.rsqrt(mean_sq + epsilon) * gain_row


WIDE = 288
HALF = 144
LANES = 128
smem = pl.BlockSpec(memory_space=pltpu.SMEM)
vmem = pl.BlockSpec(memory_space=pltpu.VMEM)
params = pltpu.CompilerParams(vmem_limit_bytes=40 * 1024 * 1024)


def feature_tables(feature, first_lane):
    left = np.zeros((LANES, WIDE), np.float32)
    right = np.zeros((LANES, WIDE), np.float32)
    bias = np.zeros((8, WIDE), np.float32)
    bias[:3, 0] = 1.0
    for a in range(feature):
        left[first_lane + a, 1 + a] = 1.0
        bias[1, 1 + a] = 1.0
        bias[2, 1 + a] = 0.5
        for b in range(feature):
            column = 1 + feature + a * feature + b
            left[first_lane + a, column] = 1.0
            right[first_lane + b, column] = 1.0
            bias[2, column] = quad_scale
    return jnp.asarray(left, bf16), jnp.asarray(right, bf16), jnp.asarray(bias)


def features_of(rows, left, right, bias):
    first = jnp.dot(rows, left, preferred_element_type=f32) + bias[0:1]
    second = jnp.dot(rows, right, preferred_element_type=f32) + bias[1:2]
    return (first * second * bias[2:3]).astype(bf16)


def pack_slots(chip, states, norms, conv):
    requests, columns, phi_size = states.shape

    def body(chip_ref, states_ref, norms_ref, conv_ref, out_ref):
        head = chip_ref[0]
        for q in range(requests):
            whole = jnp.concatenate(
                [
                    states_ref[q],
                    jnp.broadcast_to(norms_ref[q, pl.ds(head, 1), :], (8, phi_size)),
                ],
                axis=0,
            )
            whole = jnp.concatenate([whole, jnp.zeros((64, 384 - phi_size), f32)], axis=1)
            turned = whole.T
            turned = jnp.concatenate([turned, jnp.zeros((384, 64), f32)], axis=1)
            upper = turned[HALF : 2 * HALF]
            packed = turned[:HALF] + pltpu.roll(upper, 64, axis=1)
            row = lax.broadcasted_iota(jnp.int32, (HALF, LANES), 0)
            lane = lax.broadcasted_iota(jnp.int32, (HALF, LANES), 1)
            slots = jnp.concatenate(
                [jnp.zeros((2, 64), f32), conv_ref[q].astype(f32), jnp.zeros((2, 64 - columns), f32)], axis=1
            )
            for k in range(2):
                packed = jnp.where((row == 136 + k) & (lane >= 64), slots[k : k + 1], packed)
            out_ref[q] = packed.astype(bf16)

    return pl.pallas_call(
        body,
        out_shape=jax.ShapeDtypeStruct((requests, HALF, LANES), bf16),
        in_specs=[smem, vmem, vmem, vmem],
        out_specs=vmem,
        compiler_params=params,
        name="pack_slots",
    )(chip, states, norms, conv)


def unpack_slots(scalars, own, other, columns):
    requests = own.shape[0]

    def body(scalar_ref, own_ref, other_ref, start_ref, turned_ref):
        first = scalar_ref[56] == 0
        lane = lax.broadcasted_iota(jnp.int32, (HALF, LANES), 1)
        for q in range(requests):
            live = scalar_ref[16 + q] > 0
            mine = jnp.where(live, own_ref[q].astype(f32), 0.0)
            theirs = jnp.where(live, other_ref[q].astype(f32), 0.0)
            low = jnp.where(first, mine, theirs)
            high = jnp.where(first, theirs, mine)
            norm = lane == 2 * columns
            top = jnp.where(
                lane < columns,
                low,
                jnp.where(
                    lane < 2 * columns, pltpu.roll(high, columns, axis=1), jnp.where(norm, pltpu.roll(low, columns, axis=1), 0.0)
                ),
            )
            bottom = jnp.where(
                lane < columns,
                pltpu.roll(low, 64, axis=1),
                jnp.where(
                    lane < 2 * columns, pltpu.roll(high, 120, axis=1), jnp.where(norm, pltpu.roll(low, 120, axis=1), 0.0)
                ),
            )
            start_ref[q] = jnp.concatenate([top, bottom], axis=0).astype(bf16)
            natural = jnp.concatenate([mine, pltpu.roll(mine, 64, axis=1)], axis=0)
            turned_ref[q] = natural.T[:64]

    return pl.pallas_call(
        body,
        out_shape=(
            jax.ShapeDtypeStruct((requests, WIDE, LANES), bf16),
            jax.ShapeDtypeStruct((requests, 64, WIDE), f32),
        ),
        in_specs=[smem, vmem, vmem],
        out_specs=(vmem, vmem),
        compiler_params=params,
        name="unpack_slots",
    )(scalars, own, other)


def mix_rows(scalars, projected, value_key, pos_row, start, bound, taps, targets, tables, out_wide, part, channels):
    count = projected.shape[0]
    every = value_key.shape[0]
    requests = start.shape[0]
    width = out_wide.shape[1]
    blocks = count // 64
    chunk = 512

    def body(
        scalar_ref, proj_ref, vk_ref, pos_ref, start_ref, bound_ref, taps_ref, target_ref,
        left_ref, right_ref, bias_ref, out_w_ref, out_ref, tail_ref, acc_ref, one_ref, two_ref,
    ):
        lane = lax.broadcasted_iota(jnp.int32, (1, LANES), 1)
        conv_in = proj_ref[:, LANES : 2 * LANES]
        gate = proj_ref[:, 2 * LANES :]
        query = jnp.where(lane >= channels, conv_in, 0.0).astype(bf16)
        row = lax.broadcasted_iota(jnp.int32, (count, 1), 0)
        bases = [scalar_ref[24 + part * blocks + j] for j in range(blocks)]
        pos = row % 64
        for j in range(blocks):
            pos = pos + jnp.where(row // 64 == j, bases[j], 0)
        first_pos = jnp.zeros((count, 1), jnp.int32)
        for q in range(requests):
            low, high = scalar_ref[q], scalar_ref[8 + q]
            first_pos = jnp.where((pos >= low) & (pos < high), low, first_pos)

        keep = (lane < channels).astype(f32).astype(bf16)
        one_lane = (lane == channels).astype(f32).astype(bf16)
        total = jnp.zeros((count, LANES), f32)
        for k in range(every // chunk):
            keys = vk_ref[k * chunk : (k + 1) * chunk]
            at = pos_ref[:, k * chunk : (k + 1) * chunk]
            scores = lax.dot_general(query, keys, (((1,), (1,)), ((), ())), preferred_element_type=f32)
            kernel = 1.0 + scores * (0.25 + scores * 0.03125)
            weights = jnp.where((at <= pos) & (at >= first_pos), kernel, 0.0).astype(bf16)
            total = total + jnp.dot(weights, keys * keep + one_lane, preferred_element_type=f32)
        acc_ref[...] = total
        one_ref[...] = jnp.zeros((count, LANES), f32)
        two_ref[...] = jnp.zeros((count, LANES), f32)
        phi = features_of(query, left_ref[...], right_ref[...], bias_ref[...])
        for q in range(requests):
            low, high = scalar_ref[q], scalar_ref[8 + q]
            here = (bases[0] < high) & (bases[0] + 64 > low)
            for j in range(1, blocks):
                here = here | ((bases[j] < high) & (bases[j] + 64 > low))

            @pl.when(here)
            def _():
                member = (pos >= low) & (pos < high)
                carried = jnp.dot(phi, start_ref[q], preferred_element_type=f32)
                acc_ref[...] = acc_ref[...] + jnp.where(member, carried, 0.0)
                slots = start_ref[q, 272:288, :].astype(f32)
                newest = slots[9:10]
                older = jnp.where(scalar_ref[16 + q] >= 2, slots[8:9], 0.0)
                one_ref[...] = jnp.where(member, newest, one_ref[...])
                two_ref[...] = jnp.where(member, older, two_ref[...])

        attended = acc_ref[...] / acc_ref[:, channels : channels + 1]
        back_one = pltpu.roll(conv_in, 1, axis=0)
        back_two = pltpu.roll(conv_in, 2, axis=0)
        inner = row % 64
        for j in range(blocks):
            spot = scalar_ref[40 + part * blocks + j]
            older = bound_ref[pl.ds(2 * spot, 1), :]
            newest = bound_ref[pl.ds(2 * spot + 1, 1), :]
            mine = row // 64 == j
            back_one = jnp.where(mine & (inner == 0), newest, back_one)
            back_two = jnp.where(mine & (inner == 0), older, jnp.where(mine & (inner == 1), newest, back_two))
        within = pos - first_pos
        prev_one = jnp.where(within >= 1, back_one, one_ref[...])
        prev_two = jnp.where(within >= 2, back_two, jnp.where(within == 1, one_ref[...], two_ref[...]))
        conv_out = (taps_ref[0:1] * conv_in + taps_ref[1:2] * prev_one + taps_ref[2:3] * prev_two) * gate
        mixed = jnp.concatenate([attended.astype(bf16), conv_out.astype(bf16)], axis=1)
        out_ref[...] = jnp.dot(mixed, out_w_ref[...], preferred_element_type=f32).astype(bf16)
        own_at = pos_ref[:, part * count : (part + 1) * count]
        chosen = (target_ref[:, 0:1] == own_at).astype(f32).astype(bf16)
        tail_ref[...] = jnp.dot(chosen, conv_in.astype(bf16), preferred_element_type=f32)

    return pl.pallas_call(
        body,
        out_shape=(
            jax.ShapeDtypeStruct((count, width), bf16),
            jax.ShapeDtypeStruct((2 * requests, LANES), f32),
        ),
        in_specs=[smem] + [vmem] * 11,
        out_specs=(vmem, vmem),
        scratch_shapes=[pltpu.VMEM((count, LANES), f32)] * 3,
        compiler_params=params,
        name="mix_rows",
    )(scalars, projected, value_key, pos_row, start, bound, taps, targets, *tables, out_wide)


def grow_states(scalars, value_key, pos_row, tables, requests, columns):
    every = value_key.shape[0]
    chunk = 512

    def body(scalar_ref, vk_ref, pos_ref, left_ref, right_ref, bias_ref, out_ref):
        first_lane = scalar_ref[56] * columns
        row = lax.broadcasted_iota(jnp.int32, (64, LANES), 0)
        lane = lax.broadcasted_iota(jnp.int32, (64, LANES), 1)
        pick = ((lane == row + first_lane) & (row < columns)).astype(f32).astype(bf16)
        ones_row = (lax.broadcasted_iota(jnp.int32, (64, 1), 0) == columns).astype(f32)
        total = jnp.zeros((requests * 64, WIDE), f32)
        for k in range(every // chunk):
            rows = vk_ref[k * chunk : (k + 1) * chunk]
            at = pos_ref[:, k * chunk : (k + 1) * chunk]
            phi = features_of(rows, left_ref[...], right_ref[...], bias_ref[...])
            turned = lax.dot_general(pick, rows, (((1,), (1,)), ((), ())), preferred_element_type=f32) + ones_row
            parts = []
            for q in range(requests):
                member = (at >= scalar_ref[q]) & (at < scalar_ref[8 + q])
                parts.append(jnp.where(member, turned, 0.0).astype(bf16))
            total = total + jnp.dot(jnp.concatenate(parts, axis=0), phi, preferred_element_type=f32)
        for q in range(requests):
            out_ref[q] = total[q * 64 : (q + 1) * 64]

    return pl.pallas_call(
        body,
        out_shape=jax.ShapeDtypeStruct((requests, 64, WIDE), f32),
        in_specs=[smem] + [vmem] * 5,
        out_specs=vmem,
        compiler_params=params,
        name="grow_states",
    )(scalars, value_key, pos_row, *tables)


def on_device(
    tokens,
    norm_gains,
    qk_weight,
    mixer_weight,
    conv_weight,
    out_weight,
    ffn_weight,
    down_weight,
    cached_states,
    cached_norms,
    conv_cache,
    cached_lengths,
    new_lengths,
    state_source,
):
    tok_rows, width = tokens.shape
    requests, phi_size, columns = cached_states.shape
    head_count = cached_norms.shape[2]
    feature = qk_weight.shape[1] // head_count
    units = ffn_weight.shape[1]
    channels = CORES * columns
    rows_here = CHIPS * tok_rows
    group_now = lax.axis_index("group")
    tok_now = lax.axis_index("tok")
    core = tok_now % CORES
    chip = tok_now // CORES
    chip_y = chip // SIDE_X
    chip_x = chip % SIDE_X
    first_core = core == 0

    def both(own, other, axis):
        return jnp.where(
            first_core,
            jnp.concatenate([own, other], axis=axis),
            jnp.concatenate([other, own], axis=axis),
        )

    packed = pack_slots(
        chip[None].astype(jnp.int32), jnp.swapaxes(cached_states, 1, 2), jnp.swapaxes(cached_norms, 1, 2), conv_cache
    )
    gathered = lax.all_gather(packed, "group", axis=0, tiled=True)

    normed_own = rms_scale(tokens, norm_gains[0]).astype(bf16)
    normed_line = gather_line(normed_own)
    normed_parts = gather_plane(normed_line)

    mixer_rows = both(mixer_weight, swap_cores(mixer_weight), 1)
    out_rows = both(out_weight, swap_cores(out_weight), 1)
    taps = both(conv_weight, swap_cores(conv_weight), 1)
    ffn_other = swap_cores(ffn_weight)
    down_other = swap_cores(down_weight)
    head_qk = lax.dynamic_slice_in_dim(qk_weight, chip * feature, feature, 1)
    blank16 = jnp.zeros((16, width), bf16)
    in_rows = jnp.concatenate(
        [mixer_rows[0], head_qk[1], mixer_rows[1], head_qk[0], mixer_rows[2], blank16], axis=0
    )
    out_wide = jnp.concatenate([out_rows[0], blank16, out_rows[1], blank16], axis=0)
    pad_units = -(-CORES * units // 128) * 128 - CORES * units
    blank_units = jnp.zeros((pad_units, width), bf16)
    ffn_wide = jnp.concatenate(
        [ffn_weight[0], ffn_other[0], blank_units, ffn_weight[1], ffn_other[1], blank_units], axis=0
    )
    down_wide = jnp.concatenate([down_weight, down_other, blank_units], axis=0)

    lengths = new_lengths[0]
    request_ends = jnp.cumsum(lengths)
    request_starts = request_ends - lengths
    row = jnp.arange(rows_here, dtype=jnp.int32)

    def place(core_of):
        major = row // (4 * tok_rows)
        minor = row // tok_rows % 4
        dy = jnp.where(core_of == 0, major, minor)
        dx = jnp.where(core_of == 0, minor, major)
        block = (chip_y + dy) % SIDE_Y * SIDE_X + (chip_x + dx) % SIDE_X
        return (block * CORES + core_of) * tok_rows + row % tok_rows

    pos_own = place(core)
    pos_other = place(1 - core)
    pos_all = jnp.concatenate([pos_own, pos_other], axis=0)

    pos_row = jnp.concatenate([pos_own, pos_other], axis=0)[None, :]
    own_bases = pos_own[::tok_rows]
    other_bases = pos_other[::tok_rows]
    before = own_bases[:, None] - tok_rows == other_bases[None, :]
    spot_before = jnp.sum(jnp.where(before, jnp.arange(CHIPS, dtype=jnp.int32)[None, :], 0), axis=1)
    scalars = jnp.concatenate(
        [
            request_starts,
            request_ends,
            cached_lengths,
            own_bases,
            spot_before,
            jnp.stack([core, chip]),
            jnp.zeros((6,), jnp.int32),
        ]
    ).astype(jnp.int32)
    targets = jnp.concatenate([jnp.where(lengths >= 2, request_ends - 2, -1), request_ends - 1])
    targets = jnp.broadcast_to(targets[:, None], (2 * requests, LANES)).astype(jnp.int32)
    tables = feature_tables(feature, channels)

    projected = [
        lax.dot_general(piece, in_rows, (((1,), (1,)), ((), ())), preferred_element_type=f32)
        for piece in normed_parts
    ]
    value_key = jnp.concatenate([piece[:, :LANES].astype(bf16) for piece in projected], axis=0)
    value_key_all = jnp.concatenate([value_key, swap_cores(value_key)], axis=0)
    bound = jnp.concatenate(
        [
            piece.reshape(-1, tok_rows, piece.shape[1])[:, tok_rows - 2 :, LANES : 2 * LANES].reshape(-1, LANES)
            for piece in projected
        ],
        axis=0,
    )
    bound = swap_cores(bound)
    added = grow_states(scalars, value_key_all, pos_row, tables, requests, columns)

    own_sources = lax.dynamic_slice_in_dim(state_source[:, 0], group_now * requests, requests)
    wanted = own_sources * requests + jnp.arange(requests, dtype=jnp.int32)
    slots = gathered[jnp.clip(wanted, 0, gathered.shape[0] - 1)]
    start, turned = unpack_slots(scalars, slots, swap_cores(slots), columns)

    taps_wide = jnp.concatenate([taps, jnp.zeros((taps.shape[0], LANES - channels), f32)], axis=1)
    mixed = [
        mix_rows(
            scalars, projected[k], value_key_all, pos_row, start, bound, taps_wide, targets, tables, out_wide, k, channels
        )
        for k in range(4)
    ]
    residual = tokens.astype(f32) + scatter_chips([out for out, _ in mixed])

    normed_ffn_own = rms_scale(residual, norm_gains[1]).astype(bf16)
    wide_units = CORES * units + pad_units

    def feed_forward(rows):
        both_parts = lax.dot_general(rows, ffn_wide, (((1,), (1,)), ((), ())), preferred_element_type=f32)
        hidden = (jax.nn.silu(both_parts[:, :wide_units]) * both_parts[:, wide_units:]).astype(bf16)
        return jnp.dot(hidden, down_wide, preferred_element_type=f32).astype(bf16)

    ffn_partials = [feed_forward(piece) for piece in gather_plane(gather_line(normed_ffn_own))]
    layer_out = (residual + scatter_chips(ffn_partials)).astype(bf16)

    grown = added + turned
    new_states = jnp.swapaxes(grown[:, :columns, :phi_size], 1, 2)
    stage = grown[:, columns, :phi_size].astype(bf16)[None]
    for move in (
        lambda y, x, c: (y, x ^ 1, c),
        lambda y, x, c: (y, x ^ 2, c),
        lambda y, x, c: (y ^ 1, x, c),
        lambda y, x, c: (y ^ 2, x, c),
    ):
        stage = jnp.concatenate([stage, permute(stage, move)], axis=0)
    head_index = jnp.arange(head_count, dtype=jnp.int32)
    head_spot = (head_index // SIDE_X ^ chip_y) * SIDE_X + (head_index % SIDE_X ^ chip_x)
    new_norms = jnp.transpose(stage[head_spot].astype(f32), (1, 2, 0))

    tail = sum(part for _, part in mixed)[:, :channels]
    tail = tail + swap_cores(tail)
    tail = tail.reshape(2, requests, channels)
    penultimate = jnp.where((lengths >= 2)[:, None], tail[0], start[:, 281, :channels].astype(f32))
    cache = jnp.stack([penultimate, tail[1]], axis=1).astype(bf16)
    new_cache = jnp.where(first_core, cache[..., :columns], cache[..., columns:])
    return (layer_out, new_states, new_norms, new_cache)


def solution(mesh):
    in_specs = (
        P(("group", "tok"), None),
        P(),
        P(),
        P(None, "tok", None),
        P(None, "tok"),
        P(None, "tok", None),
        P(None, "tok", None),
        P("tok", None),
        P("group", None, "tok"),
        P("group", None, None),
        P("group", None, "tok"),
        P("group"),
        P("group", None),
        P(),
    )
    out_specs = (
        P(("group", "tok"), None),
        P("group", None, "tok"),
        P("group", None, None),
        P("group", None, "tok"),
    )
    return jax.shard_map(
        on_device, mesh=mesh, in_specs=in_specs, out_specs=out_specs, check_vma=False
    )
```

```python
import math

import jax
import jax.numpy as jnp
import numpy as np
from jax import lax
from jax.experimental import pallas as pl
from jax.experimental.pallas import tpu as pltpu
from jax.sharding import PartitionSpec as P

epsilon = 1e-05
quad_scale = 0.25 / math.sqrt(2.0)
SIDE_Y = 4
SIDE_X = 4
CORES = 2
CHIPS = SIDE_Y * SIDE_X
f32 = jnp.float32
bf16 = jnp.bfloat16


def tok_perm(move):
    pairs = []
    for y in range(SIDE_Y):
        for x in range(SIDE_X):
            for c in range(CORES):
                ty, tx, tc = move(y, x, c)
                source = (y * SIDE_X + x) * CORES + c
                target = (ty % SIDE_Y * SIDE_X + tx % SIDE_X) * CORES + tc % CORES
                pairs.append((source, target))
    return pairs


def permute(array, move):
    return lax.ppermute(array, "tok", tok_perm(move))


def swap_cores(array):
    return permute(array, lambda y, x, c: (y, x, 1 - c))


def shift(array, stage, step):
    def move(y, x, c):
        if c == stage:
            return (y, x + step, c)
        return (y + step, x, c)

    return permute(array, move)


def line_gather(own, stage):
    far = shift(own, stage, 2)
    from_next = shift(own, stage, -1)
    from_prev = shift(own, stage, 1)
    return [own, from_next, far, from_prev]


def line_reduce(parts, stage):
    far = shift(parts[2], stage, 2)
    from_prev = shift(parts[1], stage, 1)
    from_next = shift(parts[3], stage, -1)
    return parts[0].astype(f32) + far.astype(f32) + from_prev.astype(f32) + from_next.astype(f32)


def scatter_chips(partials):
    line = line_reduce(partials, 1).astype(bf16)
    rows = line.shape[0] // 4
    return line_reduce([line[k * rows : (k + 1) * rows] for k in range(4)], 0)


def rms_scale(inputs, gain_row):
    widened = inputs.astype(f32)
    mean_sq = jnp.mean(widened * widened, axis=-1, keepdims=True)
    return widened * lax.rsqrt(mean_sq + epsilon) * gain_row


WIDE = 288
HALF = 144
LANES = 128
smem = pl.BlockSpec(memory_space=pltpu.SMEM)
vmem = pl.BlockSpec(memory_space=pltpu.VMEM)
tiny = pl.CostEstimate(flops=2_000_000_000, bytes_accessed=8_000_000, transcendentals=0)
params = pltpu.CompilerParams(vmem_limit_bytes=40 * 1024 * 1024)


def feature_tables(feature, first_lane):
    left = np.zeros((LANES, WIDE), np.float32)
    right = np.zeros((LANES, WIDE), np.float32)
    bias = np.zeros((8, WIDE), np.float32)
    bias[:3, 0] = 1.0
    for a in range(feature):
        left[first_lane + a, 1 + a] = 1.0
        bias[1, 1 + a] = 1.0
        bias[2, 1 + a] = 0.5
        for b in range(feature):
            column = 1 + feature + a * feature + b
            left[first_lane + a, column] = 1.0
            right[first_lane + b, column] = 1.0
            bias[2, column] = quad_scale
    return jnp.asarray(left, bf16), jnp.asarray(right, bf16), jnp.asarray(bias)


def features_of(rows, left, right, bias):
    first = jnp.dot(rows, left, preferred_element_type=f32) + bias[0:1]
    second = jnp.dot(rows, right, preferred_element_type=f32) + bias[1:2]
    return (first * second * bias[2:3]).astype(bf16)


def spans(length_ref, requests):
    lows, highs, at = [], [], 0
    for q in range(requests):
        lows.append(at)
        at = at + length_ref[0, q]
        highs.append(at)
    return lows, highs


def spot_of(tok):
    return tok & 1, (tok >> 3) & 3, (tok >> 1) & 3


def block_first(block, core, chip_y, chip_x):
    dy = jnp.where(core == 0, block >> 2, block & 3)
    dx = jnp.where(core == 0, block & 3, block >> 2)
    return (((chip_y + dy) & 3) * 4 + ((chip_x + dx) & 3)) * 128 + core * 64


def rows_at(first, count, core, chip_y, chip_x):
    index = lax.broadcasted_iota(jnp.int32, (1, count), 1) + first
    return block_first(index >> 6, core, chip_y, chip_x) + (index & 63)


def gather_slots(wanted, gathered):
    requests = wanted.shape[0]

    def body(wanted_ref, all_ref, out_ref, sems):
        copies = [
            pltpu.make_async_copy(all_ref.at[wanted_ref[q]], out_ref.at[q], sems.at[q]) for q in range(requests)
        ]
        for copy in copies:
            copy.start()
        for copy in copies:
            copy.wait()

    return pl.pallas_call(
        body,
        out_shape=jax.ShapeDtypeStruct((requests,) + gathered.shape[1:], gathered.dtype),
        in_specs=[smem, pl.BlockSpec(memory_space=pl.ANY)],
        out_specs=vmem,
        scratch_shapes=[pltpu.SemaphoreType.DMA((requests,))],
        compiler_params=params,
        name="gather_slots",
    )(wanted, gathered)


def pack_slots(tok, states, norms, conv):
    requests, columns, phi_size = states.shape

    def body(tok_ref, states_ref, norms_ref, conv_ref, out_ref):
        head = tok_ref[0] >> 1
        for q in range(requests):
            whole = jnp.concatenate(
                [
                    states_ref[q],
                    jnp.broadcast_to(norms_ref[q, pl.ds(head, 1), :], (8, phi_size)),
                ],
                axis=0,
            )
            whole = jnp.concatenate([whole, jnp.zeros((64, 384 - phi_size), f32)], axis=1)
            turned = whole.T
            turned = jnp.concatenate([turned, jnp.zeros((384, 64), f32)], axis=1)
            upper = turned[HALF : 2 * HALF]
            packed = turned[:HALF] + pltpu.roll(upper, 64, axis=1)
            row = lax.broadcasted_iota(jnp.int32, (HALF, LANES), 0)
            lane = lax.broadcasted_iota(jnp.int32, (HALF, LANES), 1)
            slots = jnp.concatenate(
                [jnp.zeros((2, 64), f32), conv_ref[q].astype(f32), jnp.zeros((2, 64 - columns), f32)], axis=1
            )
            for k in range(2):
                packed = jnp.where((row == 136 + k) & (lane >= 64), slots[k : k + 1], packed)
            out_ref[q] = packed.astype(bf16)

    return pl.pallas_call(
        body,
        out_shape=jax.ShapeDtypeStruct((requests, HALF, LANES), bf16),
        in_specs=[smem, vmem, vmem, vmem],
        out_specs=vmem,
        compiler_params=params,
        name="pack_slots",
    )(tok, states, norms, conv)


def unpack_slots(tok, cached, own, other, columns):
    requests = own.shape[0]

    def body(tok_ref, cached_ref, own_ref, other_ref, start_ref, turned_ref):
        first = (tok_ref[0] & 1) == 0
        lane = lax.broadcasted_iota(jnp.int32, (HALF, LANES), 1)
        for q in range(requests):
            live = cached_ref[q] > 0
            mine = jnp.where(live, own_ref[q].astype(f32), 0.0)
            theirs = jnp.where(live, other_ref[q].astype(f32), 0.0)
            low = jnp.where(first, mine, theirs)
            high = jnp.where(first, theirs, mine)
            norm = lane == 2 * columns
            top = jnp.where(
                lane < columns,
                low,
                jnp.where(
                    lane < 2 * columns, pltpu.roll(high, columns, axis=1), jnp.where(norm, pltpu.roll(low, columns, axis=1), 0.0)
                ),
            )
            bottom = jnp.where(
                lane < columns,
                pltpu.roll(low, 64, axis=1),
                jnp.where(
                    lane < 2 * columns, pltpu.roll(high, 120, axis=1), jnp.where(norm, pltpu.roll(low, 120, axis=1), 0.0)
                ),
            )
            start_ref[q] = jnp.concatenate([top, bottom], axis=0).astype(bf16)
            natural = jnp.concatenate([mine, pltpu.roll(mine, 64, axis=1)], axis=0)
            turned_ref[q] = natural.T[:64]

    return pl.pallas_call(
        body,
        out_shape=(
            jax.ShapeDtypeStruct((requests, WIDE, LANES), bf16),
            jax.ShapeDtypeStruct((requests, 64, WIDE), f32),
        ),
        in_specs=[smem, smem, vmem, vmem],
        out_specs=(vmem, vmem),
        compiler_params=params,
        cost_estimate=tiny,
        name="unpack_slots",
    )(tok, cached, own, other)


def stage_rows(tok, lengths, projected):
    count = projected[0].shape[0]
    parts = len(projected)
    blocks = count // 64
    rows = parts * count
    requests = lengths.shape[1]
    total = rows + 2 * parts * blocks + 2 * requests

    def body(tok_ref, length_ref, *refs):
        proj_refs = refs[:parts]
        out_ref = refs[parts]
        core, chip_y, chip_x = spot_of(tok_ref[0])
        lows, highs = spans(length_ref, requests)
        line = lax.broadcasted_iota(jnp.int32, (2 * requests, 1), 0)
        target = jnp.full((2 * requests, 1), -1, jnp.int32)
        for q in range(requests):
            before = jnp.where(highs[q] - lows[q] >= 2, highs[q] - 2, -1)
            target = jnp.where(line == q, before, jnp.where(line == requests + q, highs[q] - 1, target))
        tail = jnp.zeros((2 * requests, LANES), f32)
        bounds = []
        for p in range(parts):
            out_ref[p * count : (p + 1) * count] = proj_refs[p][:, :LANES].astype(bf16)
            conv_in = proj_refs[p][:, LANES : 2 * LANES]
            chosen = (target == rows_at(p * count, count, core, chip_y, chip_x)).astype(f32).astype(bf16)
            tail = tail + jnp.dot(chosen, conv_in.astype(bf16), preferred_element_type=f32)
            for j in range(blocks):
                bounds.append(conv_in[j * 64 + 62 : j * 64 + 64])
        out_ref[rows : rows + 2 * parts * blocks] = jnp.concatenate(bounds, axis=0).astype(bf16)
        out_ref[rows + 2 * parts * blocks :] = tail.astype(bf16)

    return pl.pallas_call(
        body,
        out_shape=jax.ShapeDtypeStruct((total, LANES), bf16),
        in_specs=[smem, smem] + [vmem] * parts,
        out_specs=vmem,
        compiler_params=params,
        cost_estimate=tiny,
        name="stage_rows",
    )(tok, lengths, *projected)


def mix_rows(tok, lengths, cached, projected, staged, staged_other, start, taps, tables, out_wide, part, channels):
    count = projected.shape[0]
    near = 4 * count
    every = 2 * near
    requests = start.shape[0]
    width = out_wide.shape[1]
    blocks = count // 64
    chunk = 512

    def body(
        tok_ref, length_ref, cached_ref, proj_ref, own_ref, other_ref, start_ref, taps_ref,
        left_ref, right_ref, bias_ref, out_w_ref, out_ref, tail_ref, acc_ref, one_ref, two_ref, bound_ref,
    ):
        lane = lax.broadcasted_iota(jnp.int32, (1, LANES), 1)
        conv_in = proj_ref[:, LANES : 2 * LANES]
        gate = proj_ref[:, 2 * LANES :]
        query = jnp.where(lane >= channels, conv_in, 0.0).astype(bf16)
        row = lax.broadcasted_iota(jnp.int32, (count, 1), 0)
        core, chip_y, chip_x = spot_of(tok_ref[0])
        lows, highs = spans(length_ref, requests)
        bases = [block_first(jnp.int32(part * blocks + j), core, chip_y, chip_x) for j in range(blocks)]
        pos = row % 64
        for j in range(blocks):
            pos = pos + jnp.where(row // 64 == j, bases[j], 0)
        first_pos = jnp.zeros((count, 1), jnp.int32)
        for q in range(requests):
            first_pos = jnp.where((pos >= lows[q]) & (pos < highs[q]), lows[q], first_pos)

        keep = (lane < channels).astype(f32).astype(bf16)
        one_lane = (lane == channels).astype(f32).astype(bf16)
        total = jnp.zeros((count, LANES), f32)
        for k in range(every // chunk):
            if k * chunk < near:
                keys = own_ref[k * chunk : (k + 1) * chunk]
                at = rows_at(k * chunk, chunk, core, chip_y, chip_x)
            else:
                keys = other_ref[k * chunk - near : (k + 1) * chunk - near]
                at = rows_at(k * chunk - near, chunk, 1 - core, chip_y, chip_x)
            scores = lax.dot_general(query, keys, (((1,), (1,)), ((), ())), preferred_element_type=f32)
            kernel = 1.0 + scores * (0.25 + scores * 0.03125)
            weights = jnp.where((at <= pos) & (at >= first_pos), kernel, 0.0).astype(bf16)
            total = total + jnp.dot(weights, keys * keep + one_lane, preferred_element_type=f32)
        acc_ref[...] = total
        one_ref[...] = jnp.zeros((count, LANES), f32)
        two_ref[...] = jnp.zeros((count, LANES), f32)
        phi = features_of(query, left_ref[...], right_ref[...], bias_ref[...])
        for q in range(requests):
            low, high = lows[q], highs[q]
            here = (bases[0] < high) & (bases[0] + 64 > low)
            for j in range(1, blocks):
                here = here | ((bases[j] < high) & (bases[j] + 64 > low))

            @pl.when(here)
            def _(q=q, low=low, high=high):
                member = (pos >= low) & (pos < high)
                carried = jnp.dot(phi, start_ref[q], preferred_element_type=f32)
                acc_ref[...] = acc_ref[...] + jnp.where(member, carried, 0.0)
                slots = start_ref[q, 272:288, :].astype(f32)
                newest = slots[9:10]
                older = jnp.where(cached_ref[q] >= 2, slots[8:9], 0.0)
                one_ref[...] = jnp.where(member, newest, one_ref[...])
                two_ref[...] = jnp.where(member, older, two_ref[...])

        attended = acc_ref[...] / acc_ref[:, channels : channels + 1]
        back_one = pltpu.roll(conv_in, 1, axis=0)
        back_two = pltpu.roll(conv_in, 2, axis=0)
        inner = row % 64
        bound_ref[...] = other_ref[near : near + 2 * CHIPS].astype(f32)
        for j in range(blocks):
            order = ((bases[j] >> 6) - 1) >> 1 & 15
            back_y = ((order >> 2) - chip_y) & 3
            back_x = ((order & 3) - chip_x) & 3
            spot = jnp.where(core == 1, back_y * 4 + back_x, back_x * 4 + back_y)
            older = bound_ref[pl.ds(2 * spot, 1), :]
            newest = bound_ref[pl.ds(2 * spot + 1, 1), :]
            mine = row // 64 == j
            back_one = jnp.where(mine & (inner == 0), newest, back_one)
            back_two = jnp.where(mine & (inner == 0), older, jnp.where(mine & (inner == 1), newest, back_two))
        within = pos - first_pos
        prev_one = jnp.where(within >= 1, back_one, one_ref[...])
        prev_two = jnp.where(within >= 2, back_two, jnp.where(within == 1, one_ref[...], two_ref[...]))
        conv_out = (taps_ref[0:1] * conv_in + taps_ref[1:2] * prev_one + taps_ref[2:3] * prev_two) * gate
        mixed = jnp.concatenate([attended.astype(bf16), conv_out.astype(bf16)], axis=1)
        out_ref[...] = jnp.dot(mixed, out_w_ref[...], preferred_element_type=f32).astype(bf16)
        line = lax.broadcasted_iota(jnp.int32, (2 * requests, 1), 0)
        target = jnp.full((2 * requests, 1), -1, jnp.int32)
        for q in range(requests):
            before = jnp.where(highs[q] - lows[q] >= 2, highs[q] - 2, -1)
            target = jnp.where(line == q, before, jnp.where(line == requests + q, highs[q] - 1, target))
        chosen = (target == rows_at(part * count, count, core, chip_y, chip_x)).astype(f32).astype(bf16)
        tail_ref[...] = jnp.dot(chosen, conv_in.astype(bf16), preferred_element_type=f32)

    return pl.pallas_call(
        body,
        out_shape=(
            jax.ShapeDtypeStruct((count, width), bf16),
            jax.ShapeDtypeStruct((2 * requests, LANES), f32),
        ),
        in_specs=[smem] * 3 + [vmem] * 9,
        out_specs=(vmem, vmem),
        cost_estimate=tiny,
        scratch_shapes=[pltpu.VMEM((count, LANES), f32)] * 3 + [pltpu.VMEM((2 * CHIPS, LANES), f32)],
        compiler_params=params,
        name="mix_rows",
    )(tok, lengths, cached, projected, staged, staged_other, start, taps, *tables, out_wide)


def grow_states(tok, lengths, staged, staged_other, tables, near, columns):
    every = 2 * near
    requests = lengths.shape[1]
    chunk = 512

    def body(tok_ref, length_ref, own_ref, other_ref, left_ref, right_ref, bias_ref, out_ref):
        core, chip_y, chip_x = spot_of(tok_ref[0])
        lows, highs = spans(length_ref, requests)
        first_lane = core * columns
        row = lax.broadcasted_iota(jnp.int32, (64, LANES), 0)
        lane = lax.broadcasted_iota(jnp.int32, (64, LANES), 1)
        pick = ((lane == row + first_lane) & (row < columns)).astype(f32).astype(bf16)
        ones_row = (lax.broadcasted_iota(jnp.int32, (64, 1), 0) == columns).astype(f32)
        total = jnp.zeros((requests * 64, WIDE), f32)
        for k in range(every // chunk):
            if k * chunk < near:
                rows = own_ref[k * chunk : (k + 1) * chunk]
                at = rows_at(k * chunk, chunk, core, chip_y, chip_x)
            else:
                rows = other_ref[k * chunk - near : (k + 1) * chunk - near]
                at = rows_at(k * chunk - near, chunk, 1 - core, chip_y, chip_x)
            phi = features_of(rows, left_ref[...], right_ref[...], bias_ref[...])
            turned = lax.dot_general(pick, rows, (((1,), (1,)), ((), ())), preferred_element_type=f32) + ones_row
            parts = []
            for q in range(requests):
                member = (at >= lows[q]) & (at < highs[q])
                parts.append(jnp.where(member, turned, 0.0).astype(bf16))
            total = total + jnp.dot(jnp.concatenate(parts, axis=0), phi, preferred_element_type=f32)
        for q in range(requests):
            out_ref[q] = total[q * 64 : (q + 1) * 64]

    return pl.pallas_call(
        body,
        out_shape=jax.ShapeDtypeStruct((requests, 64, WIDE), f32),
        in_specs=[smem] * 2 + [vmem] * 5,
        cost_estimate=tiny,
        out_specs=vmem,
        compiler_params=params,
        name="grow_states",
    )(tok, lengths, staged, staged_other, *tables)


def on_device(
    tokens,
    norm_gains,
    qk_weight,
    mixer_weight,
    conv_weight,
    out_weight,
    ffn_weight,
    down_weight,
    cached_states,
    cached_norms,
    conv_cache,
    cached_lengths,
    new_lengths,
    state_source,
):
    tok_rows, width = tokens.shape
    requests, phi_size, columns = cached_states.shape
    head_count = cached_norms.shape[2]
    feature = qk_weight.shape[1] // head_count
    units = ffn_weight.shape[1]
    channels = CORES * columns
    rows_here = CHIPS * tok_rows
    group_now = lax.axis_index("group")
    tok_now = lax.axis_index("tok")
    core = tok_now % CORES
    chip = tok_now // CORES
    chip_y = chip // SIDE_X
    chip_x = chip % SIDE_X
    first_core = core == 0

    def both(own, other, axis):
        return jnp.where(
            first_core,
            jnp.concatenate([own, other], axis=axis),
            jnp.concatenate([other, own], axis=axis),
        )

    tok_here = tok_now[None].astype(jnp.int32)

    packed = pack_slots(
        tok_here, jnp.swapaxes(cached_states, 1, 2), jnp.swapaxes(cached_norms, 1, 2), conv_cache
    )
    normed_own = rms_scale(tokens, norm_gains[0]).astype(bf16)
    normed_own, packed = lax.optimization_barrier((normed_own, packed))
    gathered = lax.all_gather(packed, "group", axis=0, tiled=True)
    normed_pieces = line_gather(normed_own, 0)

    taps_high = conv_weight.astype(bf16)
    taps_low = (conv_weight - taps_high.astype(f32)).astype(bf16)
    taps_rows = jnp.concatenate([taps_high, taps_low, jnp.zeros((2, columns), bf16)], axis=0)
    mixer_rows = mixer_weight.reshape(3 * columns, width)
    early = jnp.concatenate(
        [
            mixer_rows,
            out_weight.reshape(2 * columns, width),
            jnp.concatenate([taps_rows, jnp.zeros((8, width - columns), bf16)], axis=1),
        ],
        axis=0,
    )
    early_other = swap_cores(early)
    normed_pieces, early_other = lax.optimization_barrier((normed_pieces, early_other))
    normed_parts = line_gather(jnp.concatenate(normed_pieces, axis=0), 1)
    early_low = jnp.where(first_core, early, early_other)
    early_high = jnp.where(first_core, early_other, early)

    def chip_rows(k):
        return [early_low[k * columns : (k + 1) * columns], early_high[k * columns : (k + 1) * columns]]

    head_qk = lax.dynamic_slice_in_dim(qk_weight, chip * feature, feature, 1)
    blank16 = jnp.zeros((16, width), bf16)
    in_rows = jnp.concatenate(
        chip_rows(0) + [head_qk[1]] + chip_rows(1) + [head_qk[0]] + chip_rows(2) + [blank16], axis=0
    )
    out_wide = jnp.concatenate(chip_rows(3) + [blank16] + chip_rows(4) + [blank16], axis=0)
    taps_both = jnp.concatenate(
        [early_low[5 * columns :, :columns], early_high[5 * columns :, :columns]], axis=1
    ).astype(f32)
    taps_both = taps_both[:3] + taps_both[3:6]

    lengths = new_lengths[0]
    tables = feature_tables(feature, channels)

    projected = [
        lax.dot_general(piece, in_rows, (((1,), (1,)), ((), ())), preferred_element_type=f32)
        for piece in normed_parts
    ]
    staged = stage_rows(tok_here, new_lengths, projected)
    staged_other = swap_cores(staged)
    added = grow_states(tok_here, new_lengths, staged, staged_other, tables, rows_here, columns)

    staged_other, ffn_weight, down_weight = lax.optimization_barrier((staged_other, ffn_weight, down_weight))
    late = jnp.concatenate([ffn_weight.reshape(2 * units, width), down_weight], axis=0)
    late_other = swap_cores(late)
    pad_units = -(-CORES * units // 128) * 128 - CORES * units
    blank_units = jnp.zeros((pad_units, width), bf16)
    ffn_wide = jnp.concatenate(
        [late[:units], late_other[:units], blank_units, late[units : 2 * units], late_other[units : 2 * units], blank_units], axis=0
    )
    down_wide = jnp.concatenate([late[2 * units :], late_other[2 * units :], blank_units], axis=0)

    own_sources = lax.dynamic_slice_in_dim(state_source[:, 0], group_now * requests, requests)
    wanted = own_sources * requests + jnp.arange(requests, dtype=jnp.int32)
    slots = gather_slots(jnp.clip(wanted, 0, gathered.shape[0] - 1), gathered)
    start, turned = unpack_slots(tok_here, cached_lengths, slots, swap_cores(slots), columns)

    taps_wide = jnp.concatenate([taps_both, jnp.zeros((3, LANES - channels), f32)], axis=1)
    mixed = [
        mix_rows(
            tok_here, new_lengths, cached_lengths, projected[k], staged, staged_other, start, taps_wide, tables, out_wide, k, channels
        )
        for k in range(4)
    ]
    residual = tokens.astype(f32) + scatter_chips([out for out, _ in mixed])

    grown = added + turned
    new_states = jnp.swapaxes(grown[:, :columns, :phi_size], 1, 2)
    norm_rows = jnp.concatenate(
        [grown[:, columns, :phi_size].astype(bf16), jnp.zeros((requests, width - phi_size), bf16)], axis=1
    )

    normed_ffn_own = rms_scale(residual, norm_gains[1]).astype(bf16)
    line = line_gather(jnp.concatenate([normed_ffn_own, norm_rows], axis=0), 0)
    line = jnp.concatenate([piece[:tok_rows] for piece in line] + [piece[tok_rows:] for piece in line], axis=0)
    wide_units = CORES * units + pad_units
    quarter = 4 * tok_rows

    def feed_forward(rows):
        both_parts = lax.dot_general(rows, ffn_wide, (((1,), (1,)), ((), ())), preferred_element_type=f32)
        hidden = (jax.nn.silu(both_parts[:, :wide_units]) * both_parts[:, wide_units:]).astype(bf16)
        return jnp.dot(hidden, down_wide, preferred_element_type=f32).astype(bf16)

    ffn_parts = line_gather(line, 1)
    ffn_partials = [feed_forward(piece[:quarter]) for piece in ffn_parts]
    layer_out = (residual + scatter_chips(ffn_partials)).astype(bf16)
    stage = jnp.concatenate([piece[quarter:, :phi_size] for piece in ffn_parts], axis=0)
    stage = stage.reshape(CHIPS, requests, phi_size)
    head_index = jnp.arange(head_count, dtype=jnp.int32)
    head_dy = (head_index // SIDE_X - chip_y) % SIDE_Y
    head_dx = (head_index % SIDE_X - chip_x) % SIDE_X
    head_spot = jnp.where(first_core, head_dy * SIDE_X + head_dx, head_dx * SIDE_Y + head_dy)
    new_norms = jnp.transpose(stage[head_spot].astype(f32), (1, 2, 0))

    low_tail = rows_here + 2 * CHIPS
    tail = sum(own for _, own in mixed) + staged_other[low_tail:].astype(f32)
    tail = tail[:, :channels].reshape(2, requests, channels)
    penultimate = jnp.where((lengths >= 2)[:, None], tail[0], start[:, 281, :channels].astype(f32))
    cache = jnp.stack([penultimate, tail[1]], axis=1).astype(bf16)
    new_cache = jnp.where(first_core, cache[..., :columns], cache[..., columns:])
    return (layer_out, new_states, new_norms, new_cache)


def solution(mesh):
    in_specs = (
        P(("group", "tok"), None),
        P(),
        P(),
        P(None, "tok", None),
        P(None, "tok"),
        P(None, "tok", None),
        P(None, "tok", None),
        P("tok", None),
        P("group", None, "tok"),
        P("group", None, None),
        P("group", None, "tok"),
        P("group"),
        P("group", None),
        P(),
    )
    out_specs = (
        P(("group", "tok"), None),
        P("group", None, "tok"),
        P("group", None, None),
        P("group", None, "tok"),
    )
    return jax.shard_map(
        on_device, mesh=mesh, in_specs=in_specs, out_specs=out_specs, check_vma=False
    )
```

```python
import math

import jax
import jax.numpy as jnp
import numpy as np
from jax import lax
from jax.experimental import pallas as pl
from jax.experimental.pallas import tpu as pltpu
from jax.sharding import PartitionSpec as P

epsilon = 1e-05
quad_scale = 0.25 / math.sqrt(2.0)
SIDE_Y = 4
SIDE_X = 4
CORES = 2
CHIPS = SIDE_Y * SIDE_X
f32 = jnp.float32
bf16 = jnp.bfloat16


def tok_perm(move):
    pairs = []
    for y in range(SIDE_Y):
        for x in range(SIDE_X):
            for c in range(CORES):
                ty, tx, tc = move(y, x, c)
                source = (y * SIDE_X + x) * CORES + c
                target = (ty % SIDE_Y * SIDE_X + tx % SIDE_X) * CORES + tc % CORES
                pairs.append((source, target))
    return pairs


def permute(array, move):
    return lax.ppermute(array, "tok", tok_perm(move))


def swap_cores(array):
    return permute(array, lambda y, x, c: (y, x, 1 - c))


def shift(array, stage, step):
    def move(y, x, c):
        if c == stage:
            return (y, x + step, c)
        return (y + step, x, c)

    return permute(array, move)


def line_gather(own, stage):
    far = shift(own, stage, 2)
    from_next = shift(own, stage, -1)
    from_prev = shift(own, stage, 1)
    return [own, from_next, far, from_prev]


def line_reduce(parts, stage):
    far = shift(parts[2], stage, 2)
    from_prev = shift(parts[1], stage, 1)
    from_next = shift(parts[3], stage, -1)
    return parts[0].astype(f32) + far.astype(f32) + from_prev.astype(f32) + from_next.astype(f32)


def scatter_chips(partials):
    line = line_reduce(partials, 1).astype(bf16)
    rows = line.shape[0] // 4
    return line_reduce([line[k * rows : (k + 1) * rows] for k in range(4)], 0)


def rms_scale(inputs, gain_row):
    widened = inputs.astype(f32)
    mean_sq = jnp.mean(widened * widened, axis=-1, keepdims=True)
    return widened * lax.rsqrt(mean_sq + epsilon) * gain_row


WIDE = 288
HALF = 144
LANES = 128
smem = pl.BlockSpec(memory_space=pltpu.SMEM)
vmem = pl.BlockSpec(memory_space=pltpu.VMEM)
tiny = pl.CostEstimate(flops=2_000_000_000, bytes_accessed=8_000_000, transcendentals=0)
params = pltpu.CompilerParams(vmem_limit_bytes=40 * 1024 * 1024)


def feature_tables(feature, first_lane):
    left = np.zeros((LANES, WIDE), np.float32)
    right = np.zeros((LANES, WIDE), np.float32)
    bias = np.zeros((8, WIDE), np.float32)
    bias[:3, 0] = 1.0
    for a in range(feature):
        left[first_lane + a, 1 + a] = 1.0
        bias[1, 1 + a] = 1.0
        bias[2, 1 + a] = 0.5
        for b in range(feature):
            column = 1 + feature + a * feature + b
            left[first_lane + a, column] = 1.0
            right[first_lane + b, column] = 1.0
            bias[2, column] = quad_scale
    return jnp.asarray(left, bf16), jnp.asarray(right, bf16), jnp.asarray(bias)


def features_of(rows, left, right, bias):
    first = jnp.dot(rows, left, preferred_element_type=f32) + bias[0:1]
    second = jnp.dot(rows, right, preferred_element_type=f32) + bias[1:2]
    return (first * second * bias[2:3]).astype(bf16)


def spans(length_ref, requests):
    lows, highs, at = [], [], 0
    for q in range(requests):
        lows.append(at)
        at = at + length_ref[0, q]
        highs.append(at)
    return lows, highs


def spot_of(tok):
    return tok & 1, (tok >> 3) & 3, (tok >> 1) & 3


def block_first(block, core, chip_y, chip_x):
    dy = jnp.where(core == 0, block >> 2, block & 3)
    dx = jnp.where(core == 0, block & 3, block >> 2)
    return (((chip_y + dy) & 3) * 4 + ((chip_x + dx) & 3)) * 128 + core * 64


def rows_at(first, count, core, chip_y, chip_x):
    index = lax.broadcasted_iota(jnp.int32, (1, count), 1) + first
    return block_first(index >> 6, core, chip_y, chip_x) + (index & 63)


def gather_slots(wanted, gathered):
    requests = wanted.shape[0]

    def body(wanted_ref, all_ref, out_ref, sems):
        copies = [
            pltpu.make_async_copy(all_ref.at[wanted_ref[q]], out_ref.at[q], sems.at[q]) for q in range(requests)
        ]
        for copy in copies:
            copy.start()
        for copy in copies:
            copy.wait()

    return pl.pallas_call(
        body,
        out_shape=jax.ShapeDtypeStruct((requests,) + gathered.shape[1:], gathered.dtype),
        in_specs=[smem, pl.BlockSpec(memory_space=pltpu.HBM)],
        out_specs=vmem,
        scratch_shapes=[pltpu.SemaphoreType.DMA((requests,))],
        compiler_params=params,
        name="gather_slots",
    )(wanted, gathered)


def pack_slots(tok, states, norms, conv):
    requests, columns, phi_size = states.shape

    def body(tok_ref, states_ref, norms_ref, conv_ref, out_ref):
        head = tok_ref[0] >> 1
        for q in range(requests):
            whole = jnp.concatenate(
                [
                    states_ref[q],
                    jnp.broadcast_to(norms_ref[q, pl.ds(head, 1), :], (8, phi_size)),
                ],
                axis=0,
            )
            whole = jnp.concatenate([whole, jnp.zeros((64, 384 - phi_size), f32)], axis=1)
            turned = whole.T
            turned = jnp.concatenate([turned, jnp.zeros((384, 64), f32)], axis=1)
            upper = turned[HALF : 2 * HALF]
            packed = turned[:HALF] + pltpu.roll(upper, 64, axis=1)
            row = lax.broadcasted_iota(jnp.int32, (HALF, LANES), 0)
            lane = lax.broadcasted_iota(jnp.int32, (HALF, LANES), 1)
            slots = jnp.concatenate(
                [jnp.zeros((2, 64), f32), conv_ref[q].astype(f32), jnp.zeros((2, 64 - columns), f32)], axis=1
            )
            for k in range(2):
                packed = jnp.where((row == 136 + k) & (lane >= 64), slots[k : k + 1], packed)
            out_ref[q] = packed.astype(bf16)

    return pl.pallas_call(
        body,
        out_shape=jax.ShapeDtypeStruct((requests, HALF, LANES), bf16),
        in_specs=[smem, vmem, vmem, vmem],
        out_specs=vmem,
        compiler_params=params,
        name="pack_slots",
    )(tok, states, norms, conv)


def unpack_slots(tok, cached, own, other, columns):
    requests = own.shape[0]

    def body(tok_ref, cached_ref, own_ref, other_ref, start_ref):
        first = (tok_ref[0] & 1) == 0
        lane = lax.broadcasted_iota(jnp.int32, (HALF, LANES), 1)
        for q in range(requests):
            live = cached_ref[q] > 0
            mine = jnp.where(live, own_ref[q].astype(f32), 0.0)
            theirs = jnp.where(live, other_ref[q].astype(f32), 0.0)
            low = jnp.where(first, mine, theirs)
            high = jnp.where(first, theirs, mine)
            norm = lane == 2 * columns
            top = jnp.where(
                lane < columns,
                low,
                jnp.where(
                    lane < 2 * columns, pltpu.roll(high, columns, axis=1), jnp.where(norm, pltpu.roll(low, columns, axis=1), 0.0)
                ),
            )
            bottom = jnp.where(
                lane < columns,
                pltpu.roll(low, 64, axis=1),
                jnp.where(
                    lane < 2 * columns, pltpu.roll(high, 120, axis=1), jnp.where(norm, pltpu.roll(low, 120, axis=1), 0.0)
                ),
            )
            start_ref[q] = jnp.concatenate([top, bottom], axis=0).astype(bf16)

    return pl.pallas_call(
        body,
        out_shape=jax.ShapeDtypeStruct((requests, WIDE, LANES), bf16),
        in_specs=[smem, smem, vmem, vmem],
        out_specs=vmem,
        compiler_params=params,
        cost_estimate=tiny,
        name="unpack_slots",
    )(tok, cached, own, other)


def turn_slots(cached, own, added):
    requests = own.shape[0]

    def body(cached_ref, own_ref, added_ref, out_ref):
        for q in range(requests):
            mine = jnp.where(cached_ref[q] > 0, own_ref[q].astype(f32), 0.0)
            natural = jnp.concatenate([mine, pltpu.roll(mine, 64, axis=1)], axis=0)
            out_ref[q] = natural.T[:64] + added_ref[q]

    return pl.pallas_call(
        body,
        out_shape=jax.ShapeDtypeStruct((requests, 64, WIDE), f32),
        in_specs=[smem, vmem, vmem],
        out_specs=vmem,
        compiler_params=params,
        name="turn_slots",
    )(cached, own, added)


def stage_rows(tok, lengths, projected):
    count = projected[0].shape[0]
    parts = len(projected)
    blocks = count // 64
    rows = parts * count
    requests = lengths.shape[1]
    total = rows + 2 * parts * blocks + 2 * requests

    def body(tok_ref, length_ref, *refs):
        proj_refs = refs[:parts]
        out_ref = refs[parts]
        core, chip_y, chip_x = spot_of(tok_ref[0])
        lows, highs = spans(length_ref, requests)
        line = lax.broadcasted_iota(jnp.int32, (2 * requests, 1), 0)
        target = jnp.full((2 * requests, 1), -1, jnp.int32)
        for q in range(requests):
            before = jnp.where(highs[q] - lows[q] >= 2, highs[q] - 2, -1)
            target = jnp.where(line == q, before, jnp.where(line == requests + q, highs[q] - 1, target))
        tail = jnp.zeros((2 * requests, LANES), f32)
        bounds = []
        for p in range(parts):
            out_ref[p * count : (p + 1) * count] = proj_refs[p][:, :LANES].astype(bf16)
            conv_in = proj_refs[p][:, LANES : 2 * LANES]
            chosen = (target == rows_at(p * count, count, core, chip_y, chip_x)).astype(f32).astype(bf16)
            tail = tail + jnp.dot(chosen, conv_in.astype(bf16), preferred_element_type=f32)
            for j in range(blocks):
                bounds.append(conv_in[j * 64 + 62 : j * 64 + 64])
        out_ref[rows : rows + 2 * parts * blocks] = jnp.concatenate(bounds, axis=0).astype(bf16)
        out_ref[rows + 2 * parts * blocks :] = tail.astype(bf16)

    return pl.pallas_call(
        body,
        out_shape=jax.ShapeDtypeStruct((total, LANES), bf16),
        in_specs=[smem, smem] + [vmem] * parts,
        out_specs=vmem,
        compiler_params=params,
        cost_estimate=tiny,
        name="stage_rows",
    )(tok, lengths, *projected)


def attend_rows(tok, lengths, projected, staged, staged_other, channels):
    count = projected[0].shape[0]
    parts = len(projected)
    near = parts * count
    requests = lengths.shape[1]
    chunk = 512

    def body(tok_ref, length_ref, *refs):
        proj_refs = refs[:parts]
        own_ref, other_ref, out_ref = refs[parts:]
        core, chip_y, chip_x = spot_of(tok_ref[0])
        lows, highs = spans(length_ref, requests)
        lane = lax.broadcasted_iota(jnp.int32, (1, LANES), 1)
        keep = (lane < channels).astype(f32).astype(bf16)
        one_lane = (lane == channels).astype(f32).astype(bf16)
        for p in range(parts):
            query = jnp.where(lane >= channels, proj_refs[p][:, LANES : 2 * LANES], 0.0).astype(bf16)
            row = lax.broadcasted_iota(jnp.int32, (count, 1), 0) + p * count
            pos = block_first(row >> 6, core, chip_y, chip_x) + (row & 63)
            first_pos = jnp.zeros((count, 1), jnp.int32)
            for q in range(requests):
                first_pos = jnp.where((pos >= lows[q]) & (pos < highs[q]), lows[q], first_pos)
            total = jnp.zeros((count, LANES), f32)
            for k in range(2 * near // chunk):
                if k * chunk < near:
                    keys = own_ref[k * chunk : (k + 1) * chunk]
                    at = rows_at(k * chunk, chunk, core, chip_y, chip_x)
                else:
                    keys = other_ref[k * chunk - near : (k + 1) * chunk - near]
                    at = rows_at(k * chunk - near, chunk, 1 - core, chip_y, chip_x)
                scores = lax.dot_general(query, keys, (((1,), (1,)), ((), ())), preferred_element_type=f32)
                kernel = 1.0 + scores * (0.25 + scores * 0.03125)
                weights = jnp.where((at <= pos) & (at >= first_pos), kernel, 0.0).astype(bf16)
                total = total + jnp.dot(weights, keys * keep + one_lane, preferred_element_type=f32)
            out_ref[p * count : (p + 1) * count] = total

    return pl.pallas_call(
        body,
        out_shape=jax.ShapeDtypeStruct((near, LANES), f32),
        in_specs=[smem] * 2 + [vmem] * (parts + 2),
        out_specs=vmem,
        compiler_params=params,
        name="attend_rows",
    )(tok, lengths, *projected, staged, staged_other)


def mix_rows(tok, lengths, cached, projected, local, staged_other, start, taps, tables, out_wide, part, channels):
    count = projected.shape[0]
    near = 4 * count
    requests = start.shape[0]
    width = out_wide.shape[1]
    blocks = count // 64

    def body(
        tok_ref, length_ref, cached_ref, proj_ref, local_ref, other_ref, start_ref, taps_ref,
        left_ref, right_ref, bias_ref, out_w_ref, out_ref, tail_ref, acc_ref, one_ref, two_ref, bound_ref,
    ):
        lane = lax.broadcasted_iota(jnp.int32, (1, LANES), 1)
        conv_in = proj_ref[:, LANES : 2 * LANES]
        gate = proj_ref[:, 2 * LANES :]
        query = jnp.where(lane >= channels, conv_in, 0.0).astype(bf16)
        row = lax.broadcasted_iota(jnp.int32, (count, 1), 0)
        core, chip_y, chip_x = spot_of(tok_ref[0])
        lows, highs = spans(length_ref, requests)
        bases = [block_first(jnp.int32(part * blocks + j), core, chip_y, chip_x) for j in range(blocks)]
        pos = row % 64
        for j in range(blocks):
            pos = pos + jnp.where(row // 64 == j, bases[j], 0)
        first_pos = jnp.zeros((count, 1), jnp.int32)
        for q in range(requests):
            first_pos = jnp.where((pos >= lows[q]) & (pos < highs[q]), lows[q], first_pos)

        acc_ref[...] = local_ref[part * count : (part + 1) * count]
        one_ref[...] = jnp.zeros((count, LANES), f32)
        two_ref[...] = jnp.zeros((count, LANES), f32)
        phi = features_of(query, left_ref[...], right_ref[...], bias_ref[...])
        for q in range(requests):
            low, high = lows[q], highs[q]
            here = (bases[0] < high) & (bases[0] + 64 > low)
            for j in range(1, blocks):
                here = here | ((bases[j] < high) & (bases[j] + 64 > low))

            @pl.when(here)
            def _(q=q, low=low, high=high):
                member = (pos >= low) & (pos < high)
                carried = jnp.dot(phi, start_ref[q], preferred_element_type=f32)
                acc_ref[...] = acc_ref[...] + jnp.where(member, carried, 0.0)
                slots = start_ref[q, 272:288, :].astype(f32)
                newest = slots[9:10]
                older = jnp.where(cached_ref[q] >= 2, slots[8:9], 0.0)
                one_ref[...] = jnp.where(member, newest, one_ref[...])
                two_ref[...] = jnp.where(member, older, two_ref[...])

        attended = acc_ref[...] / acc_ref[:, channels : channels + 1]
        back_one = pltpu.roll(conv_in, 1, axis=0)
        back_two = pltpu.roll(conv_in, 2, axis=0)
        inner = row % 64
        bound_ref[...] = other_ref[near : near + 2 * CHIPS].astype(f32)
        for j in range(blocks):
            order = ((bases[j] >> 6) - 1) >> 1 & 15
            back_y = ((order >> 2) - chip_y) & 3
            back_x = ((order & 3) - chip_x) & 3
            spot = jnp.where(core == 1, back_y * 4 + back_x, back_x * 4 + back_y)
            older = bound_ref[pl.ds(2 * spot, 1), :]
            newest = bound_ref[pl.ds(2 * spot + 1, 1), :]
            mine = row // 64 == j
            back_one = jnp.where(mine & (inner == 0), newest, back_one)
            back_two = jnp.where(mine & (inner == 0), older, jnp.where(mine & (inner == 1), newest, back_two))
        within = pos - first_pos
        prev_one = jnp.where(within >= 1, back_one, one_ref[...])
        prev_two = jnp.where(within >= 2, back_two, jnp.where(within == 1, one_ref[...], two_ref[...]))
        conv_out = (taps_ref[0:1] * conv_in + taps_ref[1:2] * prev_one + taps_ref[2:3] * prev_two) * gate
        mixed = jnp.concatenate([attended.astype(bf16), conv_out.astype(bf16)], axis=1)
        out_ref[...] = jnp.dot(mixed, out_w_ref[...], preferred_element_type=f32).astype(bf16)
        line = lax.broadcasted_iota(jnp.int32, (2 * requests, 1), 0)
        target = jnp.full((2 * requests, 1), -1, jnp.int32)
        for q in range(requests):
            before = jnp.where(highs[q] - lows[q] >= 2, highs[q] - 2, -1)
            target = jnp.where(line == q, before, jnp.where(line == requests + q, highs[q] - 1, target))
        chosen = (target == rows_at(part * count, count, core, chip_y, chip_x)).astype(f32).astype(bf16)
        tail_ref[...] = jnp.dot(chosen, conv_in.astype(bf16), preferred_element_type=f32)

    return pl.pallas_call(
        body,
        out_shape=(
            jax.ShapeDtypeStruct((count, width), bf16),
            jax.ShapeDtypeStruct((2 * requests, LANES), f32),
        ),
        in_specs=[smem] * 3 + [vmem] * 9,
        out_specs=(vmem, vmem),
        cost_estimate=tiny,
        scratch_shapes=[pltpu.VMEM((count, LANES), f32)] * 3 + [pltpu.VMEM((2 * CHIPS, LANES), f32)],
        compiler_params=params,
        name="mix_rows",
    )(tok, lengths, cached, projected, local, staged_other, start, taps, *tables, out_wide)


def grow_states(tok, lengths, staged, staged_other, tables, near, columns):
    every = 2 * near
    requests = lengths.shape[1]
    chunk = 512

    def body(tok_ref, length_ref, own_ref, other_ref, left_ref, right_ref, bias_ref, out_ref):
        core, chip_y, chip_x = spot_of(tok_ref[0])
        lows, highs = spans(length_ref, requests)
        first_lane = core * columns
        row = lax.broadcasted_iota(jnp.int32, (64, LANES), 0)
        lane = lax.broadcasted_iota(jnp.int32, (64, LANES), 1)
        pick = ((lane == row + first_lane) & (row < columns)).astype(f32).astype(bf16)
        ones_row = (lax.broadcasted_iota(jnp.int32, (64, 1), 0) == columns).astype(f32)
        total = jnp.zeros((requests * 64, WIDE), f32)
        for k in range(every // chunk):
            if k * chunk < near:
                rows = own_ref[k * chunk : (k + 1) * chunk]
                at = rows_at(k * chunk, chunk, core, chip_y, chip_x)
            else:
                rows = other_ref[k * chunk - near : (k + 1) * chunk - near]
                at = rows_at(k * chunk - near, chunk, 1 - core, chip_y, chip_x)
            phi = features_of(rows, left_ref[...], right_ref[...], bias_ref[...])
            turned = lax.dot_general(pick, rows, (((1,), (1,)), ((), ())), preferred_element_type=f32) + ones_row
            parts = []
            for q in range(requests):
                member = (at >= lows[q]) & (at < highs[q])
                parts.append(jnp.where(member, turned, 0.0).astype(bf16))
            total = total + jnp.dot(jnp.concatenate(parts, axis=0), phi, preferred_element_type=f32)
        for q in range(requests):
            out_ref[q] = total[q * 64 : (q + 1) * 64]

    return pl.pallas_call(
        body,
        out_shape=jax.ShapeDtypeStruct((requests, 64, WIDE), f32),
        in_specs=[smem] * 2 + [vmem] * 5,
        cost_estimate=tiny,
        out_specs=vmem,
        compiler_params=params,
        name="grow_states",
    )(tok, lengths, staged, staged_other, *tables)


def on_device(
    tokens,
    norm_gains,
    qk_weight,
    mixer_weight,
    conv_weight,
    out_weight,
    ffn_weight,
    down_weight,
    cached_states,
    cached_norms,
    conv_cache,
    cached_lengths,
    new_lengths,
    state_source,
):
    tok_rows, width = tokens.shape
    requests, phi_size, columns = cached_states.shape
    head_count = cached_norms.shape[2]
    feature = qk_weight.shape[1] // head_count
    units = ffn_weight.shape[1]
    channels = CORES * columns
    rows_here = CHIPS * tok_rows
    group_now = lax.axis_index("group")
    tok_now = lax.axis_index("tok")
    core = tok_now % CORES
    chip = tok_now // CORES
    chip_y = chip // SIDE_X
    chip_x = chip % SIDE_X
    first_core = core == 0

    def both(own, other, axis):
        return jnp.where(
            first_core,
            jnp.concatenate([own, other], axis=axis),
            jnp.concatenate([other, own], axis=axis),
        )

    tok_here = tok_now[None].astype(jnp.int32)

    packed = pack_slots(
        tok_here, jnp.swapaxes(cached_states, 1, 2), jnp.swapaxes(cached_norms, 1, 2), conv_cache
    )
    tokens, packed, mixer_weight, out_weight, conv_weight = lax.optimization_barrier(
        (tokens, packed, mixer_weight, out_weight, conv_weight)
    )
    normed_own = rms_scale(tokens, norm_gains[0]).astype(bf16)
    gathered = lax.all_gather(packed, "group", axis=0, tiled=True)
    normed_pieces = line_gather(normed_own, 0)

    taps_high = conv_weight.astype(bf16)
    taps_low = (conv_weight - taps_high.astype(f32)).astype(bf16)
    taps_rows = jnp.concatenate([taps_high, taps_low, jnp.zeros((2, columns), bf16)], axis=0)
    mixer_rows = mixer_weight.reshape(3 * columns, width)
    early = jnp.concatenate(
        [
            mixer_rows,
            out_weight.reshape(2 * columns, width),
            jnp.concatenate([taps_rows, jnp.zeros((8, width - columns), bf16)], axis=1),
        ],
        axis=0,
    )
    early_other = swap_cores(early)
    normed_pieces, early_other = lax.optimization_barrier((normed_pieces, early_other))
    normed_parts = line_gather(jnp.concatenate(normed_pieces, axis=0), 1)
    early_low = jnp.where(first_core, early, early_other)
    early_high = jnp.where(first_core, early_other, early)

    def chip_rows(k):
        return [early_low[k * columns : (k + 1) * columns], early_high[k * columns : (k + 1) * columns]]

    head_qk = lax.dynamic_slice_in_dim(qk_weight, chip * feature, feature, 1)
    blank16 = jnp.zeros((16, width), bf16)
    in_rows = jnp.concatenate(
        chip_rows(0) + [head_qk[1]] + chip_rows(1) + [head_qk[0]] + chip_rows(2) + [blank16], axis=0
    )
    out_wide = jnp.concatenate(chip_rows(3) + [blank16] + chip_rows(4) + [blank16], axis=0)
    taps_both = jnp.concatenate(
        [early_low[5 * columns :, :columns], early_high[5 * columns :, :columns]], axis=1
    ).astype(f32)
    taps_both = taps_both[:3] + taps_both[3:6]

    lengths = new_lengths[0]
    tables = feature_tables(feature, channels)

    projected = [
        lax.dot_general(piece, in_rows, (((1,), (1,)), ((), ())), preferred_element_type=f32)
        for piece in normed_parts
    ]
    staged = stage_rows(tok_here, new_lengths, projected)
    staged_other = swap_cores(staged)
    added = grow_states(tok_here, new_lengths, staged, staged_other, tables, rows_here, columns)

    staged_other, ffn_weight, down_weight = lax.optimization_barrier((staged_other, ffn_weight, down_weight))
    late = jnp.concatenate([ffn_weight.reshape(2 * units, width), down_weight], axis=0)
    late_other = swap_cores(late)
    pad_units = -(-CORES * units // 128) * 128 - CORES * units
    blank_units = jnp.zeros((pad_units, width), bf16)
    ffn_wide = jnp.concatenate(
        [late[:units], late_other[:units], blank_units, late[units : 2 * units], late_other[units : 2 * units], blank_units], axis=0
    )
    down_wide = jnp.concatenate([late[2 * units :], late_other[2 * units :], blank_units], axis=0)

    local = attend_rows(tok_here, new_lengths, projected, staged, staged_other, channels)
    gathered, local = lax.optimization_barrier((gathered, local))
    own_sources = lax.dynamic_slice_in_dim(state_source[:, 0], group_now * requests, requests)
    wanted = own_sources * requests + jnp.arange(requests, dtype=jnp.int32)
    slots = gather_slots(jnp.clip(wanted, 0, gathered.shape[0] - 1), gathered)
    start = unpack_slots(tok_here, cached_lengths, slots, swap_cores(slots), columns)

    taps_wide = jnp.concatenate([taps_both, jnp.zeros((3, LANES - channels), f32)], axis=1)
    mixed = [None] * 4
    last = None
    for k in (2, 1, 3, 0):
        rows = projected[k]
        if last is not None:
            rows = lax.optimization_barrier((rows, last))[0]
        last = mixed[k] = mix_rows(
            tok_here, new_lengths, cached_lengths, rows, local, staged_other, start, taps_wide, tables, out_wide, k, channels
        )
    residual = tokens.astype(f32) + scatter_chips([out for out, _ in mixed])

    grown = turn_slots(cached_lengths, slots, added)
    new_states = jnp.swapaxes(grown[:, :columns, :phi_size], 1, 2)
    norm_rows = jnp.concatenate(
        [grown[:, columns, :phi_size].astype(bf16), jnp.zeros((requests, width - phi_size), bf16)], axis=1
    )

    normed_ffn_own = rms_scale(residual, norm_gains[1]).astype(bf16)
    line = line_gather(jnp.concatenate([normed_ffn_own, norm_rows], axis=0), 0)
    line = jnp.concatenate([piece[:tok_rows] for piece in line] + [piece[tok_rows:] for piece in line], axis=0)
    wide_units = CORES * units + pad_units
    quarter = 4 * tok_rows

    def feed_forward(rows):
        both_parts = lax.dot_general(rows, ffn_wide, (((1,), (1,)), ((), ())), preferred_element_type=f32)
        hidden = (jax.nn.silu(both_parts[:, :wide_units]) * both_parts[:, wide_units:]).astype(bf16)
        return jnp.dot(hidden, down_wide, preferred_element_type=f32).astype(bf16)

    ffn_parts = line_gather(line, 1)
    ffn_partials = [feed_forward(line[:quarter]), None, None, None]
    last = ffn_partials[0]
    for k in (2, 1, 3):
        rows = lax.optimization_barrier((ffn_parts[k], last))[0]
        last = ffn_partials[k] = feed_forward(rows[:quarter])
    layer_out = (residual + scatter_chips(ffn_partials)).astype(bf16)
    stage = jnp.concatenate([piece[quarter:, :phi_size] for piece in ffn_parts], axis=0)
    stage = stage.reshape(CHIPS, requests, phi_size)
    head_index = jnp.arange(head_count, dtype=jnp.int32)
    head_dy = (head_index // SIDE_X - chip_y) % SIDE_Y
    head_dx = (head_index % SIDE_X - chip_x) % SIDE_X
    head_spot = jnp.where(first_core, head_dy * SIDE_X + head_dx, head_dx * SIDE_Y + head_dy)
    new_norms = jnp.transpose(stage[head_spot].astype(f32), (1, 2, 0))

    low_tail = rows_here + 2 * CHIPS
    tail = sum(own for _, own in mixed) + staged_other[low_tail:].astype(f32)
    tail = tail[:, :channels].reshape(2, requests, channels)
    penultimate = jnp.where((lengths >= 2)[:, None], tail[0], start[:, 281, :channels].astype(f32))
    cache = jnp.stack([penultimate, tail[1]], axis=1).astype(bf16)
    new_cache = jnp.where(first_core, cache[..., :columns], cache[..., columns:])
    return (layer_out, new_states, new_norms, new_cache)


def solution(mesh):
    in_specs = (
        P(("group", "tok"), None),
        P(),
        P(),
        P(None, "tok", None),
        P(None, "tok"),
        P(None, "tok", None),
        P(None, "tok", None),
        P("tok", None),
        P("group", None, "tok"),
        P("group", None, None),
        P("group", None, "tok"),
        P("group"),
        P("group", None),
        P(),
    )
    out_specs = (
        P(("group", "tok"), None),
        P("group", None, "tok"),
        P("group", None, None),
        P("group", None, "tok"),
    )
    return jax.shard_map(
        on_device, mesh=mesh, in_specs=in_specs, out_specs=out_specs, check_vma=False
    )
```

```python
import math

import jax
import jax.numpy as jnp
import numpy as np
from jax import lax
from jax.experimental import pallas as pl
from jax.experimental.pallas import tpu as pltpu
from jax.sharding import PartitionSpec as P

epsilon = 1e-05
quad_scale = 0.25 / math.sqrt(2.0)
SIDE_Y = 4
SIDE_X = 4
CORES = 2
CHIPS = SIDE_Y * SIDE_X
f32 = jnp.float32
bf16 = jnp.bfloat16


def tok_perm(move):
    pairs = []
    for y in range(SIDE_Y):
        for x in range(SIDE_X):
            for c in range(CORES):
                ty, tx, tc = move(y, x, c)
                source = (y * SIDE_X + x) * CORES + c
                target = (ty % SIDE_Y * SIDE_X + tx % SIDE_X) * CORES + tc % CORES
                pairs.append((source, target))
    return pairs


def permute(array, move):
    return lax.ppermute(array, "tok", tok_perm(move))


def swap_cores(array):
    return permute(array, lambda y, x, c: (y, x, 1 - c))


def shift(array, stage, step):
    def move(y, x, c):
        if c == stage:
            return (y, x + step, c)
        return (y + step, x, c)

    return permute(array, move)


def line_gather(own, stage):
    far = shift(own, stage, 2)
    from_next = shift(own, stage, -1)
    from_prev = shift(own, stage, 1)
    return [own, from_next, far, from_prev]


def line_reduce(parts, stage):
    far = shift(parts[2], stage, 2)
    from_prev = shift(parts[1], stage, 1)
    from_next = shift(parts[3], stage, -1)
    return parts[0].astype(f32) + far.astype(f32) + from_prev.astype(f32) + from_next.astype(f32)


def scatter_chips(partials):
    line = line_reduce(partials, 1).astype(bf16)
    rows = line.shape[0] // 4
    return line_reduce([line[k * rows : (k + 1) * rows] for k in range(4)], 0)


def rms_scale(inputs, gain_row):
    widened = inputs.astype(f32)
    mean_sq = jnp.mean(widened * widened, axis=-1, keepdims=True)
    return widened * lax.rsqrt(mean_sq + epsilon) * gain_row


WIDE = 288
HALF = 144
LANES = 128
smem = pl.BlockSpec(memory_space=pltpu.SMEM)
vmem = pl.BlockSpec(memory_space=pltpu.VMEM)
tiny = pl.CostEstimate(flops=2_000_000_000, bytes_accessed=8_000_000, transcendentals=0)
params = pltpu.CompilerParams(vmem_limit_bytes=40 * 1024 * 1024)


def feature_tables(feature, first_lane):
    left = np.zeros((LANES, WIDE), np.float32)
    right = np.zeros((LANES, WIDE), np.float32)
    bias = np.zeros((8, WIDE), np.float32)
    bias[:3, 0] = 1.0
    for a in range(feature):
        left[first_lane + a, 1 + a] = 1.0
        bias[1, 1 + a] = 1.0
        bias[2, 1 + a] = 0.5
        for b in range(feature):
            column = 1 + feature + a * feature + b
            left[first_lane + a, column] = 1.0
            right[first_lane + b, column] = 1.0
            bias[2, column] = quad_scale
    return jnp.asarray(left, bf16), jnp.asarray(right, bf16), jnp.asarray(bias)


def features_of(rows, left, right, bias):
    first = jnp.dot(rows, left, preferred_element_type=f32) + bias[0:1]
    second = jnp.dot(rows, right, preferred_element_type=f32) + bias[1:2]
    return (first * second * bias[2:3]).astype(bf16)


def spans(length_ref, requests):
    lows, highs, at = [], [], 0
    for q in range(requests):
        lows.append(at)
        at = at + length_ref[0, q]
        highs.append(at)
    return lows, highs


def spot_of(tok):
    return tok & 1, (tok >> 3) & 3, (tok >> 1) & 3


def block_first(block, core, chip_y, chip_x):
    dy = jnp.where(core == 0, block >> 2, block & 3)
    dx = jnp.where(core == 0, block & 3, block >> 2)
    return (((chip_y + dy) & 3) * 4 + ((chip_x + dx) & 3)) * 128 + core * 64


def rows_at(first, count, core, chip_y, chip_x):
    index = lax.broadcasted_iota(jnp.int32, (1, count), 1) + first
    return block_first(index >> 6, core, chip_y, chip_x) + (index & 63)


def gather_slots(wanted, gathered):
    requests = wanted.shape[0]

    def body(wanted_ref, all_ref, out_ref, sems):
        copies = [
            pltpu.make_async_copy(all_ref.at[wanted_ref[q]], out_ref.at[q], sems.at[q]) for q in range(requests)
        ]
        for copy in copies:
            copy.start()
        for copy in copies:
            copy.wait()

    return pl.pallas_call(
        body,
        out_shape=jax.ShapeDtypeStruct((requests,) + gathered.shape[1:], gathered.dtype),
        in_specs=[smem, pl.BlockSpec(memory_space=pltpu.HBM)],
        out_specs=vmem,
        scratch_shapes=[pltpu.SemaphoreType.DMA((requests,))],
        compiler_params=params,
        name="gather_slots",
    )(wanted, gathered)


def pack_slots(tok, states, norms, conv):
    requests, columns, phi_size = states.shape

    def body(tok_ref, states_ref, norms_ref, conv_ref, out_ref):
        head = tok_ref[0] >> 1
        for q in range(requests):
            whole = jnp.concatenate(
                [
                    states_ref[q],
                    jnp.broadcast_to(norms_ref[q, pl.ds(head, 1), :], (8, phi_size)),
                ],
                axis=0,
            )
            whole = jnp.concatenate([whole, jnp.zeros((64, 384 - phi_size), f32)], axis=1)
            turned = whole.T
            turned = jnp.concatenate([turned, jnp.zeros((384, 64), f32)], axis=1)
            upper = turned[HALF : 2 * HALF]
            packed = turned[:HALF] + pltpu.roll(upper, 64, axis=1)
            row = lax.broadcasted_iota(jnp.int32, (HALF, LANES), 0)
            lane = lax.broadcasted_iota(jnp.int32, (HALF, LANES), 1)
            slots = jnp.concatenate(
                [jnp.zeros((2, 64), f32), conv_ref[q].astype(f32), jnp.zeros((2, 64 - columns), f32)], axis=1
            )
            for k in range(2):
                packed = jnp.where((row == 136 + k) & (lane >= 64), slots[k : k + 1], packed)
            out_ref[q] = packed.astype(bf16)

    return pl.pallas_call(
        body,
        out_shape=jax.ShapeDtypeStruct((requests, HALF, LANES), bf16),
        in_specs=[smem, vmem, vmem, vmem],
        out_specs=vmem,
        compiler_params=params,
        name="pack_slots",
    )(tok, states, norms, conv)


def unpack_slots(tok, cached, own, other, columns):
    requests = own.shape[0]

    def body(tok_ref, cached_ref, own_ref, other_ref, start_ref):
        first = (tok_ref[0] & 1) == 0
        lane = lax.broadcasted_iota(jnp.int32, (HALF, LANES), 1)
        for q in range(requests):
            live = cached_ref[q] > 0
            mine = jnp.where(live, own_ref[q].astype(f32), 0.0)
            theirs = jnp.where(live, other_ref[q].astype(f32), 0.0)
            low = jnp.where(first, mine, theirs)
            high = jnp.where(first, theirs, mine)
            norm = lane == 2 * columns
            top = jnp.where(
                lane < columns,
                low,
                jnp.where(
                    lane < 2 * columns, pltpu.roll(high, columns, axis=1), jnp.where(norm, pltpu.roll(low, columns, axis=1), 0.0)
                ),
            )
            bottom = jnp.where(
                lane < columns,
                pltpu.roll(low, 64, axis=1),
                jnp.where(
                    lane < 2 * columns, pltpu.roll(high, 120, axis=1), jnp.where(norm, pltpu.roll(low, 120, axis=1), 0.0)
                ),
            )
            start_ref[q] = jnp.concatenate([top, bottom], axis=0).astype(bf16)

    return pl.pallas_call(
        body,
        out_shape=jax.ShapeDtypeStruct((requests, WIDE, LANES), bf16),
        in_specs=[smem, smem, vmem, vmem],
        out_specs=vmem,
        compiler_params=params,
        cost_estimate=tiny,
        name="unpack_slots",
    )(tok, cached, own, other)


def turn_slots(cached, own, added):
    requests = own.shape[0]

    def body(cached_ref, own_ref, added_ref, out_ref):
        for q in range(requests):
            mine = jnp.where(cached_ref[q] > 0, own_ref[q].astype(f32), 0.0)
            natural = jnp.concatenate([mine, pltpu.roll(mine, 64, axis=1)], axis=0)
            out_ref[q] = natural.T[:64] + added_ref[q]

    return pl.pallas_call(
        body,
        out_shape=jax.ShapeDtypeStruct((requests, 64, WIDE), f32),
        in_specs=[smem, vmem, vmem],
        out_specs=vmem,
        compiler_params=params,
        name="turn_slots",
    )(cached, own, added)


def stage_rows(tok, lengths, projected):
    count = projected[0].shape[0]
    parts = len(projected)
    blocks = count // 64
    rows = parts * count
    requests = lengths.shape[1]
    total = rows + 2 * parts * blocks + 2 * requests

    def body(tok_ref, length_ref, *refs):
        proj_refs = refs[:parts]
        out_ref = refs[parts]
        core, chip_y, chip_x = spot_of(tok_ref[0])
        lows, highs = spans(length_ref, requests)
        line = lax.broadcasted_iota(jnp.int32, (2 * requests, 1), 0)
        target = jnp.full((2 * requests, 1), -1, jnp.int32)
        for q in range(requests):
            before = jnp.where(highs[q] - lows[q] >= 2, highs[q] - 2, -1)
            target = jnp.where(line == q, before, jnp.where(line == requests + q, highs[q] - 1, target))
        tail = jnp.zeros((2 * requests, LANES), f32)
        bounds = []
        for p in range(parts):
            out_ref[p * count : (p + 1) * count] = proj_refs[p][:, :LANES].astype(bf16)
            conv_in = proj_refs[p][:, LANES : 2 * LANES]
            chosen = (target == rows_at(p * count, count, core, chip_y, chip_x)).astype(f32).astype(bf16)
            tail = tail + jnp.dot(chosen, conv_in.astype(bf16), preferred_element_type=f32)
            for j in range(blocks):
                bounds.append(conv_in[j * 64 + 62 : j * 64 + 64])
        out_ref[rows : rows + 2 * parts * blocks] = jnp.concatenate(bounds, axis=0).astype(bf16)
        out_ref[rows + 2 * parts * blocks :] = tail.astype(bf16)

    return pl.pallas_call(
        body,
        out_shape=jax.ShapeDtypeStruct((total, LANES), bf16),
        in_specs=[smem, smem] + [vmem] * parts,
        out_specs=vmem,
        compiler_params=params,
        cost_estimate=tiny,
        name="stage_rows",
    )(tok, lengths, *projected)


def attend_rows(tok, lengths, projected, staged, staged_other, channels):
    count = projected[0].shape[0]
    parts = len(projected)
    near = parts * count
    requests = lengths.shape[1]
    chunk = 512

    def body(tok_ref, length_ref, *refs):
        proj_refs = refs[:parts]
        own_ref, other_ref, out_ref = refs[parts:]
        core, chip_y, chip_x = spot_of(tok_ref[0])
        lows, highs = spans(length_ref, requests)
        lane = lax.broadcasted_iota(jnp.int32, (1, LANES), 1)
        keep = (lane < channels).astype(f32).astype(bf16)
        one_lane = (lane == channels).astype(f32).astype(bf16)
        for p in range(parts):
            query = jnp.where(lane >= channels, proj_refs[p][:, LANES : 2 * LANES], 0.0).astype(bf16)
            row = lax.broadcasted_iota(jnp.int32, (count, 1), 0) + p * count
            pos = block_first(row >> 6, core, chip_y, chip_x) + (row & 63)
            first_pos = jnp.zeros((count, 1), jnp.int32)
            for q in range(requests):
                first_pos = jnp.where((pos >= lows[q]) & (pos < highs[q]), lows[q], first_pos)
            total = jnp.zeros((count, LANES), f32)
            for k in range(2 * near // chunk):
                if k * chunk < near:
                    keys = own_ref[k * chunk : (k + 1) * chunk]
                    at = rows_at(k * chunk, chunk, core, chip_y, chip_x)
                else:
                    keys = other_ref[k * chunk - near : (k + 1) * chunk - near]
                    at = rows_at(k * chunk - near, chunk, 1 - core, chip_y, chip_x)
                scores = lax.dot_general(query, keys, (((1,), (1,)), ((), ())), preferred_element_type=f32)
                kernel = 1.0 + scores * (0.25 + scores * 0.03125)
                weights = jnp.where((at <= pos) & (at >= first_pos), kernel, 0.0).astype(bf16)
                total = total + jnp.dot(weights, keys * keep + one_lane, preferred_element_type=f32)
            out_ref[p * count : (p + 1) * count] = total

    return pl.pallas_call(
        body,
        out_shape=jax.ShapeDtypeStruct((near, LANES), f32),
        in_specs=[smem] * 2 + [vmem] * (parts + 2),
        out_specs=vmem,
        compiler_params=params,
        name="attend_rows",
    )(tok, lengths, *projected, staged, staged_other)


def mix_rows(tok, lengths, cached, projected, local, staged_other, start, taps, tables, out_wide, part, channels):
    count = projected.shape[0]
    near = 4 * count
    requests = start.shape[0]
    width = out_wide.shape[1]
    blocks = count // 64

    def body(
        tok_ref, length_ref, cached_ref, proj_ref, local_ref, other_ref, start_ref, taps_ref,
        left_ref, right_ref, bias_ref, out_w_ref, out_ref, tail_ref, acc_ref, one_ref, two_ref, bound_ref,
    ):
        lane = lax.broadcasted_iota(jnp.int32, (1, LANES), 1)
        conv_in = proj_ref[:, LANES : 2 * LANES]
        gate = proj_ref[:, 2 * LANES :]
        query = jnp.where(lane >= channels, conv_in, 0.0).astype(bf16)
        row = lax.broadcasted_iota(jnp.int32, (count, 1), 0)
        core, chip_y, chip_x = spot_of(tok_ref[0])
        lows, highs = spans(length_ref, requests)
        bases = [block_first(jnp.int32(part * blocks + j), core, chip_y, chip_x) for j in range(blocks)]
        pos = row % 64
        for j in range(blocks):
            pos = pos + jnp.where(row // 64 == j, bases[j], 0)
        first_pos = jnp.zeros((count, 1), jnp.int32)
        for q in range(requests):
            first_pos = jnp.where((pos >= lows[q]) & (pos < highs[q]), lows[q], first_pos)

        acc_ref[...] = local_ref[part * count : (part + 1) * count]
        one_ref[...] = jnp.zeros((count, LANES), f32)
        two_ref[...] = jnp.zeros((count, LANES), f32)
        phi = features_of(query, left_ref[...], right_ref[...], bias_ref[...])
        for q in range(requests):
            low, high = lows[q], highs[q]
            here = (bases[0] < high) & (bases[0] + 64 > low)
            for j in range(1, blocks):
                here = here | ((bases[j] < high) & (bases[j] + 64 > low))

            @pl.when(here)
            def _(q=q, low=low, high=high):
                member = (pos >= low) & (pos < high)
                carried = jnp.dot(phi, start_ref[q], preferred_element_type=f32)
                acc_ref[...] = acc_ref[...] + jnp.where(member, carried, 0.0)
                slots = start_ref[q, 272:288, :].astype(f32)
                newest = slots[9:10]
                older = jnp.where(cached_ref[q] >= 2, slots[8:9], 0.0)
                one_ref[...] = jnp.where(member, newest, one_ref[...])
                two_ref[...] = jnp.where(member, older, two_ref[...])

        attended = acc_ref[...] / acc_ref[:, channels : channels + 1]
        back_one = pltpu.roll(conv_in, 1, axis=0)
        back_two = pltpu.roll(conv_in, 2, axis=0)
        inner = row % 64
        bound_ref[...] = other_ref[near : near + 2 * CHIPS].astype(f32)
        for j in range(blocks):
            order = ((bases[j] >> 6) - 1) >> 1 & 15
            back_y = ((order >> 2) - chip_y) & 3
            back_x = ((order & 3) - chip_x) & 3
            spot = jnp.where(core == 1, back_y * 4 + back_x, back_x * 4 + back_y)
            older = bound_ref[pl.ds(2 * spot, 1), :]
            newest = bound_ref[pl.ds(2 * spot + 1, 1), :]
            mine = row // 64 == j
            back_one = jnp.where(mine & (inner == 0), newest, back_one)
            back_two = jnp.where(mine & (inner == 0), older, jnp.where(mine & (inner == 1), newest, back_two))
        within = pos - first_pos
        prev_one = jnp.where(within >= 1, back_one, one_ref[...])
        prev_two = jnp.where(within >= 2, back_two, jnp.where(within == 1, one_ref[...], two_ref[...]))
        conv_out = (taps_ref[0:1] * conv_in + taps_ref[1:2] * prev_one + taps_ref[2:3] * prev_two) * gate
        mixed = jnp.concatenate([attended.astype(bf16), conv_out.astype(bf16)], axis=1)
        out_ref[...] = jnp.dot(mixed, out_w_ref[...], preferred_element_type=f32).astype(bf16)
        line = lax.broadcasted_iota(jnp.int32, (2 * requests, 1), 0)
        target = jnp.full((2 * requests, 1), -1, jnp.int32)
        for q in range(requests):
            before = jnp.where(highs[q] - lows[q] >= 2, highs[q] - 2, -1)
            target = jnp.where(line == q, before, jnp.where(line == requests + q, highs[q] - 1, target))
        chosen = (target == rows_at(part * count, count, core, chip_y, chip_x)).astype(f32).astype(bf16)
        tail_ref[...] = jnp.dot(chosen, conv_in.astype(bf16), preferred_element_type=f32)

    return pl.pallas_call(
        body,
        out_shape=(
            jax.ShapeDtypeStruct((count, width), bf16),
            jax.ShapeDtypeStruct((2 * requests, LANES), f32),
        ),
        in_specs=[smem] * 3 + [vmem] * 9,
        out_specs=(vmem, vmem),
        cost_estimate=tiny,
        scratch_shapes=[pltpu.VMEM((count, LANES), f32)] * 3 + [pltpu.VMEM((2 * CHIPS, LANES), f32)],
        compiler_params=params,
        name="mix_rows",
    )(tok, lengths, cached, projected, local, staged_other, start, taps, *tables, out_wide)


def grow_states(tok, lengths, staged, staged_other, tables, near, columns):
    every = 2 * near
    requests = lengths.shape[1]
    chunk = 512

    def body(tok_ref, length_ref, own_ref, other_ref, left_ref, right_ref, bias_ref, out_ref):
        core, chip_y, chip_x = spot_of(tok_ref[0])
        lows, highs = spans(length_ref, requests)
        first_lane = core * columns
        row = lax.broadcasted_iota(jnp.int32, (64, LANES), 0)
        lane = lax.broadcasted_iota(jnp.int32, (64, LANES), 1)
        pick = ((lane == row + first_lane) & (row < columns)).astype(f32).astype(bf16)
        ones_row = (lax.broadcasted_iota(jnp.int32, (64, 1), 0) == columns).astype(f32)
        total = jnp.zeros((requests * 64, WIDE), f32)
        for k in range(every // chunk):
            if k * chunk < near:
                rows = own_ref[k * chunk : (k + 1) * chunk]
                at = rows_at(k * chunk, chunk, core, chip_y, chip_x)
            else:
                rows = other_ref[k * chunk - near : (k + 1) * chunk - near]
                at = rows_at(k * chunk - near, chunk, 1 - core, chip_y, chip_x)
            phi = features_of(rows, left_ref[...], right_ref[...], bias_ref[...])
            turned = lax.dot_general(pick, rows, (((1,), (1,)), ((), ())), preferred_element_type=f32) + ones_row
            parts = []
            for q in range(requests):
                member = (at >= lows[q]) & (at < highs[q])
                parts.append(jnp.where(member, turned, 0.0).astype(bf16))
            total = total + jnp.dot(jnp.concatenate(parts, axis=0), phi, preferred_element_type=f32)
        for q in range(requests):
            out_ref[q] = total[q * 64 : (q + 1) * 64]

    return pl.pallas_call(
        body,
        out_shape=jax.ShapeDtypeStruct((requests, 64, WIDE), f32),
        in_specs=[smem] * 2 + [vmem] * 5,
        cost_estimate=tiny,
        out_specs=vmem,
        compiler_params=params,
        name="grow_states",
    )(tok, lengths, staged, staged_other, *tables)


def on_device(
    tokens,
    norm_gains,
    qk_weight,
    mixer_weight,
    conv_weight,
    out_weight,
    ffn_weight,
    down_weight,
    cached_states,
    cached_norms,
    conv_cache,
    cached_lengths,
    new_lengths,
    state_source,
):
    tok_rows, width = tokens.shape
    requests, phi_size, columns = cached_states.shape
    head_count = cached_norms.shape[2]
    feature = qk_weight.shape[1] // head_count
    units = ffn_weight.shape[1]
    channels = CORES * columns
    rows_here = CHIPS * tok_rows
    group_now = lax.axis_index("group")
    tok_now = lax.axis_index("tok")
    core = tok_now % CORES
    chip = tok_now // CORES
    chip_y = chip // SIDE_X
    chip_x = chip % SIDE_X
    first_core = core == 0

    def both(own, other, axis):
        return jnp.where(
            first_core,
            jnp.concatenate([own, other], axis=axis),
            jnp.concatenate([other, own], axis=axis),
        )

    tok_here = tok_now[None].astype(jnp.int32)

    packed = pack_slots(
        tok_here, jnp.swapaxes(cached_states, 1, 2), jnp.swapaxes(cached_norms, 1, 2), conv_cache
    )
    tokens, packed, mixer_weight, out_weight, conv_weight = lax.optimization_barrier(
        (tokens, packed, mixer_weight, out_weight, conv_weight)
    )
    normed_own = rms_scale(tokens, norm_gains[0]).astype(bf16)
    gathered = lax.all_gather(packed, "group", axis=0, tiled=True)
    normed_pieces = line_gather(normed_own, 0)

    taps_high = conv_weight.astype(bf16)
    taps_low = (conv_weight - taps_high.astype(f32)).astype(bf16)
    taps_rows = jnp.concatenate([taps_high, taps_low, jnp.zeros((2, columns), bf16)], axis=0)
    mixer_rows = mixer_weight.reshape(3 * columns, width)
    early = jnp.concatenate(
        [
            mixer_rows,
            out_weight.reshape(2 * columns, width),
            jnp.concatenate([taps_rows, jnp.zeros((8, width - columns), bf16)], axis=1),
        ],
        axis=0,
    )
    early_other = swap_cores(early)
    normed_pieces, early_other = lax.optimization_barrier((normed_pieces, early_other))
    normed_parts = line_gather(jnp.concatenate(normed_pieces, axis=0), 1)
    early_low = jnp.where(first_core, early, early_other)
    early_high = jnp.where(first_core, early_other, early)

    def chip_rows(k):
        return [early_low[k * columns : (k + 1) * columns], early_high[k * columns : (k + 1) * columns]]

    head_qk = lax.dynamic_slice_in_dim(qk_weight, chip * feature, feature, 1)
    blank16 = jnp.zeros((16, width), bf16)
    in_rows = jnp.concatenate(
        chip_rows(0) + [head_qk[1]] + chip_rows(1) + [head_qk[0]] + chip_rows(2) + [blank16], axis=0
    )
    out_wide = jnp.concatenate(chip_rows(3) + [blank16] + chip_rows(4) + [blank16], axis=0)
    taps_both = jnp.concatenate(
        [early_low[5 * columns :, :columns], early_high[5 * columns :, :columns]], axis=1
    ).astype(f32)
    taps_both = taps_both[:3] + taps_both[3:6]

    lengths = new_lengths[0]
    tables = feature_tables(feature, channels)

    projected = [
        lax.dot_general(piece, in_rows, (((1,), (1,)), ((), ())), preferred_element_type=f32)
        for piece in normed_parts
    ]
    staged = stage_rows(tok_here, new_lengths, projected)
    staged_other = swap_cores(staged)
    added = grow_states(tok_here, new_lengths, staged, staged_other, tables, rows_here, columns)

    staged_other, ffn_weight, down_weight = lax.optimization_barrier((staged_other, ffn_weight, down_weight))
    late = jnp.concatenate([ffn_weight.reshape(2 * units, width), down_weight], axis=0)
    late_other = swap_cores(late)
    pad_units = -(-CORES * units // 128) * 128 - CORES * units
    blank_units = jnp.zeros((pad_units, width), bf16)
    ffn_wide = jnp.concatenate(
        [late[:units], late_other[:units], blank_units, late[units : 2 * units], late_other[units : 2 * units], blank_units], axis=0
    )
    down_wide = jnp.concatenate([late[2 * units :], late_other[2 * units :], blank_units], axis=0)

    local = attend_rows(tok_here, new_lengths, projected, staged, staged_other, channels)
    gathered, local = lax.optimization_barrier((gathered, local))
    own_sources = lax.dynamic_slice_in_dim(state_source[:, 0], group_now * requests, requests)
    wanted = own_sources * requests + jnp.arange(requests, dtype=jnp.int32)
    gathered = pltpu.with_memory_space_constraint(gathered, pltpu.HBM)
    slots = gather_slots(jnp.clip(wanted, 0, gathered.shape[0] - 1), gathered)
    start = unpack_slots(tok_here, cached_lengths, slots, swap_cores(slots), columns)

    taps_wide = jnp.concatenate([taps_both, jnp.zeros((3, LANES - channels), f32)], axis=1)
    mixed = [None] * 4
    last = None
    for k in (2, 1, 3, 0):
        rows = projected[k]
        if last is not None:
            rows = lax.optimization_barrier((rows, last))[0]
        last = mixed[k] = mix_rows(
            tok_here, new_lengths, cached_lengths, rows, local, staged_other, start, taps_wide, tables, out_wide, k, channels
        )
    residual = tokens.astype(f32) + scatter_chips([out for out, _ in mixed])

    grown = turn_slots(cached_lengths, slots, added)
    new_states = jnp.swapaxes(grown[:, :columns, :phi_size], 1, 2)
    norm_rows = jnp.concatenate(
        [grown[:, columns, :phi_size].astype(bf16), jnp.zeros((requests, width - phi_size), bf16)], axis=1
    )

    normed_ffn_own = rms_scale(residual, norm_gains[1]).astype(bf16)
    line = line_gather(jnp.concatenate([normed_ffn_own, norm_rows], axis=0), 0)
    line = jnp.concatenate([piece[:tok_rows] for piece in line] + [piece[tok_rows:] for piece in line], axis=0)
    wide_units = CORES * units + pad_units
    quarter = 4 * tok_rows

    def feed_forward(rows):
        both_parts = lax.dot_general(rows, ffn_wide, (((1,), (1,)), ((), ())), preferred_element_type=f32)
        hidden = (jax.nn.silu(both_parts[:, :wide_units]) * both_parts[:, wide_units:]).astype(bf16)
        return jnp.dot(hidden, down_wide, preferred_element_type=f32).astype(bf16)

    ffn_parts = line_gather(line, 1)
    ffn_partials = [feed_forward(line[:quarter]), None, None, None]
    ffn_parts[2] = lax.optimization_barrier((ffn_parts[2], ffn_partials[0]))[0]
    for k in (1, 2, 3):
        ffn_partials[k] = feed_forward(ffn_parts[k][:quarter])
    layer_out = (residual + scatter_chips(ffn_partials)).astype(bf16)
    stage = jnp.concatenate([piece[quarter:, :phi_size] for piece in ffn_parts], axis=0)
    stage = stage.reshape(CHIPS, requests, phi_size)
    head_index = jnp.arange(head_count, dtype=jnp.int32)
    head_dy = (head_index // SIDE_X - chip_y) % SIDE_Y
    head_dx = (head_index % SIDE_X - chip_x) % SIDE_X
    head_spot = jnp.where(first_core, head_dy * SIDE_X + head_dx, head_dx * SIDE_Y + head_dy)
    new_norms = jnp.transpose(stage[head_spot].astype(f32), (1, 2, 0))

    low_tail = rows_here + 2 * CHIPS
    tail = sum(own for _, own in mixed) + staged_other[low_tail:].astype(f32)
    tail = tail[:, :channels].reshape(2, requests, channels)
    penultimate = jnp.where((lengths >= 2)[:, None], tail[0], start[:, 281, :channels].astype(f32))
    cache = jnp.stack([penultimate, tail[1]], axis=1).astype(bf16)
    new_cache = jnp.where(first_core, cache[..., :columns], cache[..., columns:])
    return (layer_out, new_states, new_norms, new_cache)


def solution(mesh):
    in_specs = (
        P(("group", "tok"), None),
        P(),
        P(),
        P(None, "tok", None),
        P(None, "tok"),
        P(None, "tok", None),
        P(None, "tok", None),
        P("tok", None),
        P("group", None, "tok"),
        P("group", None, None),
        P("group", None, "tok"),
        P("group"),
        P("group", None),
        P(),
    )
    out_specs = (
        P(("group", "tok"), None),
        P("group", None, "tok"),
        P("group", None, None),
        P("group", None, "tok"),
    )
    return jax.shard_map(
        on_device, mesh=mesh, in_specs=in_specs, out_specs=out_specs, check_vma=False
    )
```

```python
import math

import jax
import jax.numpy as jnp
import numpy as np
from jax import lax
from jax.experimental import pallas as pl
from jax.experimental.pallas import tpu as pltpu
from jax.sharding import PartitionSpec as P

epsilon = 1e-05
quad_scale = 0.25 / math.sqrt(2.0)
SIDE_Y = 4
SIDE_X = 4
CORES = 2
CHIPS = SIDE_Y * SIDE_X
f32 = jnp.float32
bf16 = jnp.bfloat16


def tok_perm(move):
    pairs = []
    for y in range(SIDE_Y):
        for x in range(SIDE_X):
            for c in range(CORES):
                ty, tx, tc = move(y, x, c)
                source = (y * SIDE_X + x) * CORES + c
                target = (ty % SIDE_Y * SIDE_X + tx % SIDE_X) * CORES + tc % CORES
                pairs.append((source, target))
    return pairs


def permute(array, move):
    return lax.ppermute(array, "tok", tok_perm(move))


def swap_cores(array):
    return permute(array, lambda y, x, c: (y, x, 1 - c))


def shift(array, stage, step):
    def move(y, x, c):
        if c == stage:
            return (y, x + step, c)
        return (y + step, x, c)

    return permute(array, move)


def line_gather(own, stage):
    far = shift(own, stage, 2)
    from_next = shift(own, stage, -1)
    from_prev = shift(own, stage, 1)
    return [own, from_next, far, from_prev]


def line_reduce(parts, stage):
    far = shift(parts[2], stage, 2)
    from_prev = shift(parts[1], stage, 1)
    from_next = shift(parts[3], stage, -1)
    return parts[0].astype(f32) + far.astype(f32) + from_prev.astype(f32) + from_next.astype(f32)


def scatter_chips(partials):
    line = line_reduce(partials, 1).astype(bf16)
    rows = line.shape[0] // 4
    return line_reduce([line[k * rows : (k + 1) * rows] for k in range(4)], 0)


def rms_scale(inputs, gain_row):
    widened = inputs.astype(f32)
    mean_sq = jnp.mean(widened * widened, axis=-1, keepdims=True)
    return widened * lax.rsqrt(mean_sq + epsilon) * gain_row


WIDE = 288
HALF = 144
LANES = 128
smem = pl.BlockSpec(memory_space=pltpu.SMEM)
vmem = pl.BlockSpec(memory_space=pltpu.VMEM)
tiny = pl.CostEstimate(flops=2_000_000_000, bytes_accessed=8_000_000, transcendentals=0)
params = pltpu.CompilerParams(vmem_limit_bytes=40 * 1024 * 1024)


def feature_tables(feature, first_lane):
    left = np.zeros((LANES, WIDE), np.float32)
    right = np.zeros((LANES, WIDE), np.float32)
    bias = np.zeros((8, WIDE), np.float32)
    bias[:3, 0] = 1.0
    for a in range(feature):
        left[first_lane + a, 1 + a] = 1.0
        bias[1, 1 + a] = 1.0
        bias[2, 1 + a] = 0.5
        for b in range(feature):
            column = 1 + feature + a * feature + b
            left[first_lane + a, column] = 1.0
            right[first_lane + b, column] = 1.0
            bias[2, column] = quad_scale
    return jnp.asarray(left, bf16), jnp.asarray(right, bf16), jnp.asarray(bias)


def features_of(rows, left, right, bias):
    first = jnp.dot(rows, left, preferred_element_type=f32) + bias[0:1]
    second = jnp.dot(rows, right, preferred_element_type=f32) + bias[1:2]
    return (first * second * bias[2:3]).astype(bf16)


def spans(length_ref, requests):
    lows, highs, at = [], [], 0
    for q in range(requests):
        lows.append(at)
        at = at + length_ref[0, q]
        highs.append(at)
    return lows, highs


def spot_of(tok):
    return tok & 1, (tok >> 3) & 3, (tok >> 1) & 3


def block_first(block, core, chip_y, chip_x):
    dy = jnp.where(core == 0, block >> 2, block & 3)
    dx = jnp.where(core == 0, block & 3, block >> 2)
    return (((chip_y + dy) & 3) * 4 + ((chip_x + dx) & 3)) * 128 + core * 64


def rows_at(first, count, core, chip_y, chip_x):
    index = lax.broadcasted_iota(jnp.int32, (1, count), 1) + first
    return block_first(index >> 6, core, chip_y, chip_x) + (index & 63)


def gather_slots(wanted, gathered):
    requests = wanted.shape[0]

    def body(wanted_ref, all_ref, out_ref, sems):
        copies = [
            pltpu.make_async_copy(all_ref.at[wanted_ref[q]], out_ref.at[q], sems.at[q]) for q in range(requests)
        ]
        for copy in copies:
            copy.start()
        for copy in copies:
            copy.wait()

    return pl.pallas_call(
        body,
        out_shape=jax.ShapeDtypeStruct((requests,) + gathered.shape[1:], gathered.dtype),
        in_specs=[smem, pl.BlockSpec(memory_space=pltpu.HBM)],
        out_specs=vmem,
        scratch_shapes=[pltpu.SemaphoreType.DMA((requests,))],
        compiler_params=params,
        name="gather_slots",
    )(wanted, gathered)


def pack_slots(tok, states, norms, conv):
    requests, columns, phi_size = states.shape

    def body(tok_ref, states_ref, norms_ref, conv_ref, out_ref):
        head = tok_ref[0] >> 1
        for q in range(requests):
            whole = jnp.concatenate(
                [
                    states_ref[q],
                    jnp.broadcast_to(norms_ref[q, pl.ds(head, 1), :], (8, phi_size)),
                ],
                axis=0,
            )
            whole = jnp.concatenate([whole, jnp.zeros((64, 384 - phi_size), f32)], axis=1)
            turned = whole.T
            turned = jnp.concatenate([turned, jnp.zeros((384, 64), f32)], axis=1)
            upper = turned[HALF : 2 * HALF]
            packed = turned[:HALF] + pltpu.roll(upper, 64, axis=1)
            row = lax.broadcasted_iota(jnp.int32, (HALF, LANES), 0)
            lane = lax.broadcasted_iota(jnp.int32, (HALF, LANES), 1)
            slots = jnp.concatenate(
                [jnp.zeros((2, 64), f32), conv_ref[q].astype(f32), jnp.zeros((2, 64 - columns), f32)], axis=1
            )
            for k in range(2):
                packed = jnp.where((row == 136 + k) & (lane >= 64), slots[k : k + 1], packed)
            out_ref[q] = packed.astype(bf16)

    return pl.pallas_call(
        body,
        out_shape=jax.ShapeDtypeStruct((requests, HALF, LANES), bf16),
        in_specs=[smem, vmem, vmem, vmem],
        out_specs=vmem,
        compiler_params=params,
        name="pack_slots",
    )(tok, states, norms, conv)


def unpack_slots(tok, cached, own, other, columns):
    requests = own.shape[0]

    def body(tok_ref, cached_ref, own_ref, other_ref, start_ref):
        first = (tok_ref[0] & 1) == 0
        lane = lax.broadcasted_iota(jnp.int32, (HALF, LANES), 1)
        for q in range(requests):
            live = cached_ref[q] > 0
            mine = jnp.where(live, own_ref[q].astype(f32), 0.0)
            theirs = jnp.where(live, other_ref[q].astype(f32), 0.0)
            low = jnp.where(first, mine, theirs)
            high = jnp.where(first, theirs, mine)
            norm = lane == 2 * columns
            top = jnp.where(
                lane < columns,
                low,
                jnp.where(
                    lane < 2 * columns, pltpu.roll(high, columns, axis=1), jnp.where(norm, pltpu.roll(low, columns, axis=1), 0.0)
                ),
            )
            bottom = jnp.where(
                lane < columns,
                pltpu.roll(low, 64, axis=1),
                jnp.where(
                    lane < 2 * columns, pltpu.roll(high, 120, axis=1), jnp.where(norm, pltpu.roll(low, 120, axis=1), 0.0)
                ),
            )
            start_ref[q] = jnp.concatenate([top, bottom], axis=0).astype(bf16)

    return pl.pallas_call(
        body,
        out_shape=jax.ShapeDtypeStruct((requests, WIDE, LANES), bf16),
        in_specs=[smem, smem, vmem, vmem],
        out_specs=vmem,
        compiler_params=params,
        cost_estimate=tiny,
        name="unpack_slots",
    )(tok, cached, own, other)


def turn_slots(cached, own, added):
    requests = own.shape[0]

    def body(cached_ref, own_ref, added_ref, out_ref):
        for q in range(requests):
            mine = jnp.where(cached_ref[q] > 0, own_ref[q].astype(f32), 0.0)
            natural = jnp.concatenate([mine, pltpu.roll(mine, 64, axis=1)], axis=0)
            out_ref[q] = natural.T[:64] + added_ref[q]

    return pl.pallas_call(
        body,
        out_shape=jax.ShapeDtypeStruct((requests, 64, WIDE), f32),
        in_specs=[smem, vmem, vmem],
        out_specs=vmem,
        compiler_params=params,
        name="turn_slots",
    )(cached, own, added)


def stage_rows(tok, lengths, projected):
    count = projected[0].shape[0]
    parts = len(projected)
    blocks = count // 64
    rows = parts * count
    requests = lengths.shape[1]
    total = rows + 2 * parts * blocks + 2 * requests

    def body(tok_ref, length_ref, *refs):
        proj_refs = refs[:parts]
        out_ref = refs[parts]
        core, chip_y, chip_x = spot_of(tok_ref[0])
        lows, highs = spans(length_ref, requests)
        line = lax.broadcasted_iota(jnp.int32, (2 * requests, 1), 0)
        target = jnp.full((2 * requests, 1), -1, jnp.int32)
        for q in range(requests):
            before = jnp.where(highs[q] - lows[q] >= 2, highs[q] - 2, -1)
            target = jnp.where(line == q, before, jnp.where(line == requests + q, highs[q] - 1, target))
        tail = jnp.zeros((2 * requests, LANES), f32)
        bounds = []
        for p in range(parts):
            out_ref[p * count : (p + 1) * count] = proj_refs[p][:, :LANES].astype(bf16)
            conv_in = proj_refs[p][:, LANES : 2 * LANES]
            chosen = (target == rows_at(p * count, count, core, chip_y, chip_x)).astype(f32).astype(bf16)
            tail = tail + jnp.dot(chosen, conv_in.astype(bf16), preferred_element_type=f32)
            for j in range(blocks):
                bounds.append(conv_in[j * 64 + 62 : j * 64 + 64])
        out_ref[rows : rows + 2 * parts * blocks] = jnp.concatenate(bounds, axis=0).astype(bf16)
        out_ref[rows + 2 * parts * blocks :] = tail.astype(bf16)

    return pl.pallas_call(
        body,
        out_shape=jax.ShapeDtypeStruct((total, LANES), bf16),
        in_specs=[smem, smem] + [vmem] * parts,
        out_specs=vmem,
        compiler_params=params,
        cost_estimate=tiny,
        name="stage_rows",
    )(tok, lengths, *projected)


def attend_rows(tok, lengths, projected, staged, staged_other, channels):
    count = projected[0].shape[0]
    parts = len(projected)
    near = parts * count
    requests = lengths.shape[1]
    chunk = 512

    def body(tok_ref, length_ref, *refs):
        proj_refs = refs[:parts]
        own_ref, other_ref, out_ref = refs[parts:]
        core, chip_y, chip_x = spot_of(tok_ref[0])
        lows, highs = spans(length_ref, requests)
        lane = lax.broadcasted_iota(jnp.int32, (1, LANES), 1)
        keep = (lane < channels).astype(f32).astype(bf16)
        one_lane = (lane == channels).astype(f32).astype(bf16)
        for p in range(parts):
            query = jnp.where(lane >= channels, proj_refs[p][:, LANES : 2 * LANES], 0.0).astype(bf16)
            row = lax.broadcasted_iota(jnp.int32, (count, 1), 0) + p * count
            pos = block_first(row >> 6, core, chip_y, chip_x) + (row & 63)
            first_pos = jnp.zeros((count, 1), jnp.int32)
            for q in range(requests):
                first_pos = jnp.where((pos >= lows[q]) & (pos < highs[q]), lows[q], first_pos)
            total = jnp.zeros((count, LANES), f32)
            for k in range(2 * near // chunk):
                if k * chunk < near:
                    keys = own_ref[k * chunk : (k + 1) * chunk]
                    at = rows_at(k * chunk, chunk, core, chip_y, chip_x)
                else:
                    keys = other_ref[k * chunk - near : (k + 1) * chunk - near]
                    at = rows_at(k * chunk - near, chunk, 1 - core, chip_y, chip_x)
                scores = lax.dot_general(query, keys, (((1,), (1,)), ((), ())), preferred_element_type=f32)
                kernel = 1.0 + scores * (0.25 + scores * 0.03125)
                weights = jnp.where((at <= pos) & (at >= first_pos), kernel, 0.0).astype(bf16)
                total = total + jnp.dot(weights, keys * keep + one_lane, preferred_element_type=f32)
            out_ref[p * count : (p + 1) * count] = total

    return pl.pallas_call(
        body,
        out_shape=jax.ShapeDtypeStruct((near, LANES), f32),
        in_specs=[smem] * 2 + [vmem] * (parts + 2),
        out_specs=vmem,
        compiler_params=params,
        name="attend_rows",
    )(tok, lengths, *projected, staged, staged_other)


def mix_rows(tok, lengths, cached, projected, local, staged_other, start, taps, tables, out_wide, part, channels):
    count = projected.shape[0]
    near = 4 * count
    requests = start.shape[0]
    width = out_wide.shape[1]
    blocks = count // 64

    def body(
        tok_ref, length_ref, cached_ref, proj_ref, local_ref, other_ref, start_ref, taps_ref,
        left_ref, right_ref, bias_ref, out_w_ref, out_ref, tail_ref, acc_ref, one_ref, two_ref, bound_ref,
    ):
        lane = lax.broadcasted_iota(jnp.int32, (1, LANES), 1)
        conv_in = proj_ref[:, LANES : 2 * LANES]
        gate = proj_ref[:, 2 * LANES :]
        query = jnp.where(lane >= channels, conv_in, 0.0).astype(bf16)
        row = lax.broadcasted_iota(jnp.int32, (count, 1), 0)
        core, chip_y, chip_x = spot_of(tok_ref[0])
        lows, highs = spans(length_ref, requests)
        bases = [block_first(jnp.int32(part * blocks + j), core, chip_y, chip_x) for j in range(blocks)]
        pos = row % 64
        for j in range(blocks):
            pos = pos + jnp.where(row // 64 == j, bases[j], 0)
        first_pos = jnp.zeros((count, 1), jnp.int32)
        for q in range(requests):
            first_pos = jnp.where((pos >= lows[q]) & (pos < highs[q]), lows[q], first_pos)

        acc_ref[...] = local_ref[part * count : (part + 1) * count]
        one_ref[...] = jnp.zeros((count, LANES), f32)
        two_ref[...] = jnp.zeros((count, LANES), f32)
        phi = features_of(query, left_ref[...], right_ref[...], bias_ref[...])
        for q in range(requests):
            low, high = lows[q], highs[q]
            here = (bases[0] < high) & (bases[0] + 64 > low)
            for j in range(1, blocks):
                here = here | ((bases[j] < high) & (bases[j] + 64 > low))

            @pl.when(here)
            def _(q=q, low=low, high=high):
                member = (pos >= low) & (pos < high)
                carried = jnp.dot(phi, start_ref[q], preferred_element_type=f32)
                acc_ref[...] = acc_ref[...] + jnp.where(member, carried, 0.0)
                slots = start_ref[q, 272:288, :].astype(f32)
                newest = slots[9:10]
                older = jnp.where(cached_ref[q] >= 2, slots[8:9], 0.0)
                one_ref[...] = jnp.where(member, newest, one_ref[...])
                two_ref[...] = jnp.where(member, older, two_ref[...])

        attended = acc_ref[...] / acc_ref[:, channels : channels + 1]
        back_one = pltpu.roll(conv_in, 1, axis=0)
        back_two = pltpu.roll(conv_in, 2, axis=0)
        inner = row % 64
        bound_ref[...] = other_ref[near : near + 2 * CHIPS].astype(f32)
        for j in range(blocks):
            order = ((bases[j] >> 6) - 1) >> 1 & 15
            back_y = ((order >> 2) - chip_y) & 3
            back_x = ((order & 3) - chip_x) & 3
            spot = jnp.where(core == 1, back_y * 4 + back_x, back_x * 4 + back_y)
            older = bound_ref[pl.ds(2 * spot, 1), :]
            newest = bound_ref[pl.ds(2 * spot + 1, 1), :]
            mine = row // 64 == j
            back_one = jnp.where(mine & (inner == 0), newest, back_one)
            back_two = jnp.where(mine & (inner == 0), older, jnp.where(mine & (inner == 1), newest, back_two))
        within = pos - first_pos
        prev_one = jnp.where(within >= 1, back_one, one_ref[...])
        prev_two = jnp.where(within >= 2, back_two, jnp.where(within == 1, one_ref[...], two_ref[...]))
        conv_out = (taps_ref[0:1] * conv_in + taps_ref[1:2] * prev_one + taps_ref[2:3] * prev_two) * gate
        mixed = jnp.concatenate([attended.astype(bf16), conv_out.astype(bf16)], axis=1)
        out_ref[...] = jnp.dot(mixed, out_w_ref[...], preferred_element_type=f32).astype(bf16)
        line = lax.broadcasted_iota(jnp.int32, (2 * requests, 1), 0)
        target = jnp.full((2 * requests, 1), -1, jnp.int32)
        for q in range(requests):
            before = jnp.where(highs[q] - lows[q] >= 2, highs[q] - 2, -1)
            target = jnp.where(line == q, before, jnp.where(line == requests + q, highs[q] - 1, target))
        chosen = (target == rows_at(part * count, count, core, chip_y, chip_x)).astype(f32).astype(bf16)
        tail_ref[...] = jnp.dot(chosen, conv_in.astype(bf16), preferred_element_type=f32)

    return pl.pallas_call(
        body,
        out_shape=(
            jax.ShapeDtypeStruct((count, width), bf16),
            jax.ShapeDtypeStruct((2 * requests, LANES), f32),
        ),
        in_specs=[smem] * 3 + [vmem] * 9,
        out_specs=(vmem, vmem),
        cost_estimate=tiny,
        scratch_shapes=[pltpu.VMEM((count, LANES), f32)] * 3 + [pltpu.VMEM((2 * CHIPS, LANES), f32)],
        compiler_params=params,
        name="mix_rows",
    )(tok, lengths, cached, projected, local, staged_other, start, taps, *tables, out_wide)


def grow_states(tok, lengths, staged, staged_other, tables, near, columns):
    every = 2 * near
    requests = lengths.shape[1]
    chunk = 512

    def body(tok_ref, length_ref, own_ref, other_ref, left_ref, right_ref, bias_ref, out_ref):
        core, chip_y, chip_x = spot_of(tok_ref[0])
        lows, highs = spans(length_ref, requests)
        first_lane = core * columns
        row = lax.broadcasted_iota(jnp.int32, (64, LANES), 0)
        lane = lax.broadcasted_iota(jnp.int32, (64, LANES), 1)
        pick = ((lane == row + first_lane) & (row < columns)).astype(f32).astype(bf16)
        ones_row = (lax.broadcasted_iota(jnp.int32, (64, 1), 0) == columns).astype(f32)
        total = jnp.zeros((requests * 64, WIDE), f32)
        for k in range(every // chunk):
            if k * chunk < near:
                rows = own_ref[k * chunk : (k + 1) * chunk]
                at = rows_at(k * chunk, chunk, core, chip_y, chip_x)
            else:
                rows = other_ref[k * chunk - near : (k + 1) * chunk - near]
                at = rows_at(k * chunk - near, chunk, 1 - core, chip_y, chip_x)
            phi = features_of(rows, left_ref[...], right_ref[...], bias_ref[...])
            turned = lax.dot_general(pick, rows, (((1,), (1,)), ((), ())), preferred_element_type=f32) + ones_row
            parts = []
            for q in range(requests):
                member = (at >= lows[q]) & (at < highs[q])
                parts.append(jnp.where(member, turned, 0.0).astype(bf16))
            total = total + jnp.dot(jnp.concatenate(parts, axis=0), phi, preferred_element_type=f32)
        for q in range(requests):
            out_ref[q] = total[q * 64 : (q + 1) * 64]

    return pl.pallas_call(
        body,
        out_shape=jax.ShapeDtypeStruct((requests, 64, WIDE), f32),
        in_specs=[smem] * 2 + [vmem] * 5,
        cost_estimate=tiny,
        out_specs=vmem,
        compiler_params=params,
        name="grow_states",
    )(tok, lengths, staged, staged_other, *tables)


def on_device(
    tokens,
    norm_gains,
    qk_weight,
    mixer_weight,
    conv_weight,
    out_weight,
    ffn_weight,
    down_weight,
    cached_states,
    cached_norms,
    conv_cache,
    cached_lengths,
    new_lengths,
    state_source,
):
    tok_rows, width = tokens.shape
    requests, phi_size, columns = cached_states.shape
    head_count = cached_norms.shape[2]
    feature = qk_weight.shape[1] // head_count
    units = ffn_weight.shape[1]
    channels = CORES * columns
    rows_here = CHIPS * tok_rows
    group_now = lax.axis_index("group")
    tok_now = lax.axis_index("tok")
    core = tok_now % CORES
    chip = tok_now // CORES
    chip_y = chip // SIDE_X
    chip_x = chip % SIDE_X
    first_core = core == 0

    def both(own, other, axis):
        return jnp.where(
            first_core,
            jnp.concatenate([own, other], axis=axis),
            jnp.concatenate([other, own], axis=axis),
        )

    tok_here = tok_now[None].astype(jnp.int32)

    packed = pack_slots(
        tok_here, jnp.swapaxes(cached_states, 1, 2), jnp.swapaxes(cached_norms, 1, 2), conv_cache
    )
    normed_own = rms_scale(tokens, norm_gains[0]).astype(bf16)
    normed_own, packed = lax.optimization_barrier((normed_own, packed))
    gathered = lax.all_gather(packed, "group", axis=0, tiled=True)
    normed_pieces = line_gather(normed_own, 0)

    taps_high = conv_weight.astype(bf16)
    taps_low = (conv_weight - taps_high.astype(f32)).astype(bf16)
    taps_rows = jnp.concatenate([taps_high, taps_low, jnp.zeros((2, columns), bf16)], axis=0)
    mixer_rows = mixer_weight.reshape(3 * columns, width)
    early = jnp.concatenate(
        [
            mixer_rows,
            out_weight.reshape(2 * columns, width),
            jnp.concatenate([taps_rows, jnp.zeros((8, width - columns), bf16)], axis=1),
        ],
        axis=0,
    )
    early_other = swap_cores(early)
    normed_pieces, early_other = lax.optimization_barrier((normed_pieces, early_other))
    normed_parts = line_gather(jnp.concatenate(normed_pieces, axis=0), 1)
    early_low = jnp.where(first_core, early, early_other)
    early_high = jnp.where(first_core, early_other, early)

    def chip_rows(k):
        return [early_low[k * columns : (k + 1) * columns], early_high[k * columns : (k + 1) * columns]]

    head_qk = lax.dynamic_slice_in_dim(qk_weight, chip * feature, feature, 1)
    blank16 = jnp.zeros((16, width), bf16)
    in_rows = jnp.concatenate(
        chip_rows(0) + [head_qk[1]] + chip_rows(1) + [head_qk[0]] + chip_rows(2) + [blank16], axis=0
    )
    out_wide = jnp.concatenate(chip_rows(3) + [blank16] + chip_rows(4) + [blank16], axis=0)
    taps_both = jnp.concatenate(
        [early_low[5 * columns :, :columns], early_high[5 * columns :, :columns]], axis=1
    ).astype(f32)
    taps_both = taps_both[:3] + taps_both[3:6]

    lengths = new_lengths[0]
    tables = feature_tables(feature, channels)

    projected = [
        lax.dot_general(piece, in_rows, (((1,), (1,)), ((), ())), preferred_element_type=f32)
        for piece in normed_parts
    ]
    staged = stage_rows(tok_here, new_lengths, projected)
    staged_other = swap_cores(staged)
    added = grow_states(tok_here, new_lengths, staged, staged_other, tables, rows_here, columns)

    staged_other, ffn_weight, down_weight = lax.optimization_barrier((staged_other, ffn_weight, down_weight))
    late = jnp.concatenate([ffn_weight.reshape(2 * units, width), down_weight], axis=0)
    late_other = swap_cores(late)
    pad_units = -(-CORES * units // 128) * 128 - CORES * units
    blank_units = jnp.zeros((pad_units, width), bf16)
    ffn_wide = jnp.concatenate(
        [late[:units], late_other[:units], blank_units, late[units : 2 * units], late_other[units : 2 * units], blank_units], axis=0
    )
    down_wide = jnp.concatenate([late[2 * units :], late_other[2 * units :], blank_units], axis=0)

    local = attend_rows(tok_here, new_lengths, projected, staged, staged_other, channels)
    gathered, local = lax.optimization_barrier((gathered, local))
    own_sources = lax.dynamic_slice_in_dim(state_source[:, 0], group_now * requests, requests)
    wanted = own_sources * requests + jnp.arange(requests, dtype=jnp.int32)
    gathered = pltpu.with_memory_space_constraint(gathered, pltpu.HBM)
    slots = gather_slots(jnp.clip(wanted, 0, gathered.shape[0] - 1), gathered)
    start = unpack_slots(tok_here, cached_lengths, slots, swap_cores(slots), columns)

    taps_wide = jnp.concatenate([taps_both, jnp.zeros((3, LANES - channels), f32)], axis=1)
    mixed = [None] * 4
    last = None
    for k in (2, 1, 3, 0):
        rows = projected[k]
        if last is not None:
            rows = lax.optimization_barrier((rows, last))[0]
        last = mixed[k] = mix_rows(
            tok_here, new_lengths, cached_lengths, rows, local, staged_other, start, taps_wide, tables, out_wide, k, channels
        )
    residual = tokens.astype(f32) + scatter_chips([out for out, _ in mixed])

    grown = turn_slots(cached_lengths, slots, added)
    new_states = jnp.swapaxes(grown[:, :columns, :phi_size], 1, 2)
    norm_rows = jnp.concatenate(
        [grown[:, columns, :phi_size].astype(bf16), jnp.zeros((requests, width - phi_size), bf16)], axis=1
    )

    normed_ffn_own = rms_scale(residual, norm_gains[1]).astype(bf16)
    line = line_gather(jnp.concatenate([normed_ffn_own, norm_rows], axis=0), 0)
    line = jnp.concatenate([piece[:tok_rows] for piece in line] + [piece[tok_rows:] for piece in line], axis=0)
    wide_units = CORES * units + pad_units
    quarter = 4 * tok_rows

    def feed_forward(rows):
        both_parts = lax.dot_general(rows, ffn_wide, (((1,), (1,)), ((), ())), preferred_element_type=f32)
        hidden = (jax.nn.silu(both_parts[:, :wide_units]) * both_parts[:, wide_units:]).astype(bf16)
        return jnp.dot(hidden, down_wide, preferred_element_type=f32).astype(bf16)

    ffn_parts = line_gather(line, 1)
    ffn_partials = [feed_forward(line[:quarter]), None, None, None]
    ffn_parts[2] = lax.optimization_barrier((ffn_parts[2], ffn_partials[0]))[0]
    for k in (1, 2, 3):
        ffn_partials[k] = feed_forward(ffn_parts[k][:quarter])
    layer_out = (residual + scatter_chips(ffn_partials)).astype(bf16)
    stage = jnp.concatenate([piece[quarter:, :phi_size] for piece in ffn_parts], axis=0)
    stage = stage.reshape(CHIPS, requests, phi_size)
    head_index = jnp.arange(head_count, dtype=jnp.int32)
    head_dy = (head_index // SIDE_X - chip_y) % SIDE_Y
    head_dx = (head_index % SIDE_X - chip_x) % SIDE_X
    head_spot = jnp.where(first_core, head_dy * SIDE_X + head_dx, head_dx * SIDE_Y + head_dy)
    new_norms = jnp.transpose(stage[head_spot].astype(f32), (1, 2, 0))

    low_tail = rows_here + 2 * CHIPS
    tail = sum(own for _, own in mixed) + staged_other[low_tail:].astype(f32)
    tail = tail[:, :channels].reshape(2, requests, channels)
    penultimate = jnp.where((lengths >= 2)[:, None], tail[0], start[:, 281, :channels].astype(f32))
    cache = jnp.stack([penultimate, tail[1]], axis=1).astype(bf16)
    new_cache = jnp.where(first_core, cache[..., :columns], cache[..., columns:])
    return (layer_out, new_states, new_norms, new_cache)


def solution(mesh):
    in_specs = (
        P(("group", "tok"), None),
        P(),
        P(),
        P(None, "tok", None),
        P(None, "tok"),
        P(None, "tok", None),
        P(None, "tok", None),
        P("tok", None),
        P("group", None, "tok"),
        P("group", None, None),
        P("group", None, "tok"),
        P("group"),
        P("group", None),
        P(),
    )
    out_specs = (
        P(("group", "tok"), None),
        P("group", None, "tok"),
        P("group", None, None),
        P("group", None, "tok"),
    )
    return jax.shard_map(
        on_device, mesh=mesh, in_specs=in_specs, out_specs=out_specs, check_vma=False
    )
```

```python
import math

import jax
import jax.numpy as jnp
import numpy as np
from jax import lax
from jax.experimental import pallas as pl
from jax.experimental.pallas import tpu as pltpu
from jax.sharding import PartitionSpec as P

epsilon = 1e-05
quad_scale = 0.25 / math.sqrt(2.0)
SIDE_Y = 4
SIDE_X = 4
CORES = 2
CHIPS = SIDE_Y * SIDE_X
f32 = jnp.float32
bf16 = jnp.bfloat16


def tok_perm(move):
    pairs = []
    for y in range(SIDE_Y):
        for x in range(SIDE_X):
            for c in range(CORES):
                ty, tx, tc = move(y, x, c)
                source = (y * SIDE_X + x) * CORES + c
                target = (ty % SIDE_Y * SIDE_X + tx % SIDE_X) * CORES + tc % CORES
                pairs.append((source, target))
    return pairs


def permute(array, move):
    return lax.ppermute(array, "tok", tok_perm(move))


def swap_cores(array):
    return permute(array, lambda y, x, c: (y, x, 1 - c))


def shift(array, stage, step):
    def move(y, x, c):
        if c == stage:
            return (y, x + step, c)
        return (y + step, x, c)

    return permute(array, move)


def line_gather(own, stage):
    far = shift(own, stage, 2)
    from_next = shift(own, stage, -1)
    from_prev = shift(own, stage, 1)
    return [own, from_next, far, from_prev]


def line_reduce(parts, stage):
    far = shift(parts[2], stage, 2)
    from_prev = shift(parts[1], stage, 1)
    from_next = shift(parts[3], stage, -1)
    return parts[0].astype(f32) + far.astype(f32) + from_prev.astype(f32) + from_next.astype(f32)


def scatter_chips(partials):
    line = line_reduce(partials, 1).astype(bf16)
    rows = line.shape[0] // 4
    return line_reduce([line[k * rows : (k + 1) * rows] for k in range(4)], 0)


def rms_scale(inputs, gain_row):
    widened = inputs.astype(f32)
    mean_sq = jnp.mean(widened * widened, axis=-1, keepdims=True)
    return widened * lax.rsqrt(mean_sq + epsilon) * gain_row


WIDE = 288
HALF = 144
LANES = 128
smem = pl.BlockSpec(memory_space=pltpu.SMEM)
vmem = pl.BlockSpec(memory_space=pltpu.VMEM)
tiny = pl.CostEstimate(flops=2_000_000_000, bytes_accessed=8_000_000, transcendentals=0)
params = pltpu.CompilerParams(vmem_limit_bytes=20 * 1024 * 1024)


def feature_tables(feature, first_lane):
    left = np.zeros((LANES, WIDE), np.float32)
    right = np.zeros((LANES, WIDE), np.float32)
    bias = np.zeros((8, WIDE), np.float32)
    bias[:3, 0] = 1.0
    for a in range(feature):
        left[first_lane + a, 1 + a] = 1.0
        bias[1, 1 + a] = 1.0
        bias[2, 1 + a] = 0.5
        for b in range(feature):
            column = 1 + feature + a * feature + b
            left[first_lane + a, column] = 1.0
            right[first_lane + b, column] = 1.0
            bias[2, column] = quad_scale
    return jnp.asarray(left, bf16), jnp.asarray(right, bf16), jnp.asarray(bias)


def features_of(rows, left, right, bias):
    first = jnp.dot(rows, left, preferred_element_type=f32) + bias[0:1]
    second = jnp.dot(rows, right, preferred_element_type=f32) + bias[1:2]
    return (first * second * bias[2:3]).astype(bf16)


def spans(length_ref, requests):
    lows, highs, at = [], [], 0
    for q in range(requests):
        lows.append(at)
        at = at + length_ref[0, q]
        highs.append(at)
    return lows, highs


def spot_of(tok):
    return tok & 1, (tok >> 3) & 3, (tok >> 1) & 3


def block_first(block, core, chip_y, chip_x):
    dy = jnp.where(core == 0, block >> 2, block & 3)
    dx = jnp.where(core == 0, block & 3, block >> 2)
    return (((chip_y + dy) & 3) * 4 + ((chip_x + dx) & 3)) * 128 + core * 64


def rows_at(first, count, core, chip_y, chip_x):
    index = lax.broadcasted_iota(jnp.int32, (1, count), 1) + first
    return block_first(index >> 6, core, chip_y, chip_x) + (index & 63)


def gather_slots(wanted, gathered):
    requests = wanted.shape[0]

    def body(wanted_ref, all_ref, out_ref, sems):
        copies = [
            pltpu.make_async_copy(all_ref.at[wanted_ref[q]], out_ref.at[q], sems.at[q]) for q in range(requests)
        ]
        for copy in copies:
            copy.start()
        for copy in copies:
            copy.wait()

    return pl.pallas_call(
        body,
        out_shape=jax.ShapeDtypeStruct((requests,) + gathered.shape[1:], gathered.dtype),
        in_specs=[smem, pl.BlockSpec(memory_space=pltpu.HBM)],
        out_specs=vmem,
        scratch_shapes=[pltpu.SemaphoreType.DMA((requests,))],
        compiler_params=params,
        name="gather_slots",
    )(wanted, gathered)


def pack_slots(tok, states, norms, conv):
    requests, columns, phi_size = states.shape

    def body(tok_ref, states_ref, norms_ref, conv_ref, out_ref):
        head = tok_ref[0] >> 1
        for q in range(requests):
            whole = jnp.concatenate(
                [
                    states_ref[q],
                    jnp.broadcast_to(norms_ref[q, pl.ds(head, 1), :], (8, phi_size)),
                ],
                axis=0,
            )
            whole = jnp.concatenate([whole, jnp.zeros((64, 384 - phi_size), f32)], axis=1)
            turned = whole.T
            turned = jnp.concatenate([turned, jnp.zeros((384, 64), f32)], axis=1)
            upper = turned[HALF : 2 * HALF]
            packed = turned[:HALF] + pltpu.roll(upper, 64, axis=1)
            row = lax.broadcasted_iota(jnp.int32, (HALF, LANES), 0)
            lane = lax.broadcasted_iota(jnp.int32, (HALF, LANES), 1)
            slots = jnp.concatenate(
                [jnp.zeros((2, 64), f32), conv_ref[q].astype(f32), jnp.zeros((2, 64 - columns), f32)], axis=1
            )
            for k in range(2):
                packed = jnp.where((row == 136 + k) & (lane >= 64), slots[k : k + 1], packed)
            out_ref[q] = packed.astype(bf16)

    return pl.pallas_call(
        body,
        out_shape=jax.ShapeDtypeStruct((requests, HALF, LANES), bf16),
        in_specs=[smem, vmem, vmem, vmem],
        out_specs=vmem,
        compiler_params=params,
        name="pack_slots",
    )(tok, states, norms, conv)


def unpack_slots(tok, cached, own, other, columns):
    requests = own.shape[0]

    def body(tok_ref, cached_ref, own_ref, other_ref, start_ref):
        first = (tok_ref[0] & 1) == 0
        lane = lax.broadcasted_iota(jnp.int32, (HALF, LANES), 1)
        for q in range(requests):
            live = cached_ref[q] > 0
            mine = jnp.where(live, own_ref[q].astype(f32), 0.0)
            theirs = jnp.where(live, other_ref[q].astype(f32), 0.0)
            low = jnp.where(first, mine, theirs)
            high = jnp.where(first, theirs, mine)
            norm = lane == 2 * columns
            top = jnp.where(
                lane < columns,
                low,
                jnp.where(
                    lane < 2 * columns, pltpu.roll(high, columns, axis=1), jnp.where(norm, pltpu.roll(low, columns, axis=1), 0.0)
                ),
            )
            bottom = jnp.where(
                lane < columns,
                pltpu.roll(low, 64, axis=1),
                jnp.where(
                    lane < 2 * columns, pltpu.roll(high, 120, axis=1), jnp.where(norm, pltpu.roll(low, 120, axis=1), 0.0)
                ),
            )
            start_ref[q] = jnp.concatenate([top, bottom], axis=0).astype(bf16)

    return pl.pallas_call(
        body,
        out_shape=jax.ShapeDtypeStruct((requests, WIDE, LANES), bf16),
        in_specs=[smem, smem, vmem, vmem],
        out_specs=vmem,
        compiler_params=params,
        cost_estimate=tiny,
        name="unpack_slots",
    )(tok, cached, own, other)


def turn_slots(cached, own, added):
    requests = own.shape[0]

    def body(cached_ref, own_ref, added_ref, out_ref):
        for q in range(requests):
            mine = jnp.where(cached_ref[q] > 0, own_ref[q].astype(f32), 0.0)
            natural = jnp.concatenate([mine, pltpu.roll(mine, 64, axis=1)], axis=0)
            out_ref[q] = natural.T[:64] + added_ref[q]

    return pl.pallas_call(
        body,
        out_shape=jax.ShapeDtypeStruct((requests, 64, WIDE), f32),
        in_specs=[smem, vmem, vmem],
        out_specs=vmem,
        compiler_params=params,
        name="turn_slots",
    )(cached, own, added)


def stage_rows(tok, lengths, projected):
    count = projected[0].shape[0]
    parts = len(projected)
    blocks = count // 64
    rows = parts * count
    requests = lengths.shape[1]
    total = rows + 2 * parts * blocks + 2 * requests

    def body(tok_ref, length_ref, *refs):
        proj_refs = refs[:parts]
        out_ref = refs[parts]
        core, chip_y, chip_x = spot_of(tok_ref[0])
        lows, highs = spans(length_ref, requests)
        line = lax.broadcasted_iota(jnp.int32, (2 * requests, 1), 0)
        target = jnp.full((2 * requests, 1), -1, jnp.int32)
        for q in range(requests):
            before = jnp.where(highs[q] - lows[q] >= 2, highs[q] - 2, -1)
            target = jnp.where(line == q, before, jnp.where(line == requests + q, highs[q] - 1, target))
        tail = jnp.zeros((2 * requests, LANES), f32)
        bounds = []
        for p in range(parts):
            out_ref[p * count : (p + 1) * count] = proj_refs[p][:, :LANES].astype(bf16)
            conv_in = proj_refs[p][:, LANES : 2 * LANES]
            chosen = (target == rows_at(p * count, count, core, chip_y, chip_x)).astype(f32).astype(bf16)
            tail = tail + jnp.dot(chosen, conv_in.astype(bf16), preferred_element_type=f32)
            for j in range(blocks):
                bounds.append(conv_in[j * 64 + 62 : j * 64 + 64])
        out_ref[rows : rows + 2 * parts * blocks] = jnp.concatenate(bounds, axis=0).astype(bf16)
        out_ref[rows + 2 * parts * blocks :] = tail.astype(bf16)

    return pl.pallas_call(
        body,
        out_shape=jax.ShapeDtypeStruct((total, LANES), bf16),
        in_specs=[smem, smem] + [vmem] * parts,
        out_specs=vmem,
        compiler_params=params,
        cost_estimate=tiny,
        name="stage_rows",
    )(tok, lengths, *projected)


def attend_rows(tok, lengths, projected, staged, staged_other, channels):
    count = projected[0].shape[0]
    parts = len(projected)
    near = parts * count
    requests = lengths.shape[1]
    chunk = 512

    def body(tok_ref, length_ref, *refs):
        proj_refs = refs[:parts]
        own_ref, other_ref, out_ref = refs[parts:]
        core, chip_y, chip_x = spot_of(tok_ref[0])
        lows, highs = spans(length_ref, requests)
        lane = lax.broadcasted_iota(jnp.int32, (1, LANES), 1)
        keep = (lane < channels).astype(f32).astype(bf16)
        one_lane = (lane == channels).astype(f32).astype(bf16)
        for p in range(parts):
            query = jnp.where(lane >= channels, proj_refs[p][:, LANES : 2 * LANES], 0.0).astype(bf16)
            row = lax.broadcasted_iota(jnp.int32, (count, 1), 0) + p * count
            pos = block_first(row >> 6, core, chip_y, chip_x) + (row & 63)
            first_pos = jnp.zeros((count, 1), jnp.int32)
            for q in range(requests):
                first_pos = jnp.where((pos >= lows[q]) & (pos < highs[q]), lows[q], first_pos)
            total = jnp.zeros((count, LANES), f32)
            for k in range(2 * near // chunk):
                if k * chunk < near:
                    keys = own_ref[k * chunk : (k + 1) * chunk]
                    at = rows_at(k * chunk, chunk, core, chip_y, chip_x)
                else:
                    keys = other_ref[k * chunk - near : (k + 1) * chunk - near]
                    at = rows_at(k * chunk - near, chunk, 1 - core, chip_y, chip_x)
                scores = lax.dot_general(query, keys, (((1,), (1,)), ((), ())), preferred_element_type=f32)
                kernel = 1.0 + scores * (0.25 + scores * 0.03125)
                weights = jnp.where((at <= pos) & (at >= first_pos), kernel, 0.0).astype(bf16)
                total = total + jnp.dot(weights, keys * keep + one_lane, preferred_element_type=f32)
            out_ref[p * count : (p + 1) * count] = total

    return pl.pallas_call(
        body,
        out_shape=jax.ShapeDtypeStruct((near, LANES), f32),
        in_specs=[smem] * 2 + [vmem] * (parts + 2),
        out_specs=vmem,
        compiler_params=params,
        name="attend_rows",
    )(tok, lengths, *projected, staged, staged_other)


def mix_rows(tok, lengths, cached, projected, local, staged_other, start, taps, tables, out_wide, part, channels):
    count = projected.shape[0]
    near = 4 * count
    requests = start.shape[0]
    width = out_wide.shape[1]
    blocks = count // 64

    def body(
        tok_ref, length_ref, cached_ref, proj_ref, local_ref, other_ref, start_ref, taps_ref,
        left_ref, right_ref, bias_ref, out_w_ref, out_ref, tail_ref, acc_ref, one_ref, two_ref, bound_ref,
    ):
        lane = lax.broadcasted_iota(jnp.int32, (1, LANES), 1)
        conv_in = proj_ref[:, LANES : 2 * LANES]
        gate = proj_ref[:, 2 * LANES :]
        query = jnp.where(lane >= channels, conv_in, 0.0).astype(bf16)
        row = lax.broadcasted_iota(jnp.int32, (count, 1), 0)
        core, chip_y, chip_x = spot_of(tok_ref[0])
        lows, highs = spans(length_ref, requests)
        bases = [block_first(jnp.int32(part * blocks + j), core, chip_y, chip_x) for j in range(blocks)]
        pos = row % 64
        for j in range(blocks):
            pos = pos + jnp.where(row // 64 == j, bases[j], 0)
        first_pos = jnp.zeros((count, 1), jnp.int32)
        for q in range(requests):
            first_pos = jnp.where((pos >= lows[q]) & (pos < highs[q]), lows[q], first_pos)

        acc_ref[...] = local_ref[part * count : (part + 1) * count]
        one_ref[...] = jnp.zeros((count, LANES), f32)
        two_ref[...] = jnp.zeros((count, LANES), f32)
        phi = features_of(query, left_ref[...], right_ref[...], bias_ref[...])
        for q in range(requests):
            low, high = lows[q], highs[q]
            here = (bases[0] < high) & (bases[0] + 64 > low)
            for j in range(1, blocks):
                here = here | ((bases[j] < high) & (bases[j] + 64 > low))

            @pl.when(here)
            def _(q=q, low=low, high=high):
                member = (pos >= low) & (pos < high)
                carried = jnp.dot(phi, start_ref[q], preferred_element_type=f32)
                acc_ref[...] = acc_ref[...] + jnp.where(member, carried, 0.0)
                slots = start_ref[q, 272:288, :].astype(f32)
                newest = slots[9:10]
                older = jnp.where(cached_ref[q] >= 2, slots[8:9], 0.0)
                one_ref[...] = jnp.where(member, newest, one_ref[...])
                two_ref[...] = jnp.where(member, older, two_ref[...])

        attended = acc_ref[...] / acc_ref[:, channels : channels + 1]
        back_one = pltpu.roll(conv_in, 1, axis=0)
        back_two = pltpu.roll(conv_in, 2, axis=0)
        inner = row % 64
        bound_ref[...] = other_ref[near : near + 2 * CHIPS].astype(f32)
        for j in range(blocks):
            order = ((bases[j] >> 6) - 1) >> 1 & 15
            back_y = ((order >> 2) - chip_y) & 3
            back_x = ((order & 3) - chip_x) & 3
            spot = jnp.where(core == 1, back_y * 4 + back_x, back_x * 4 + back_y)
            older = bound_ref[pl.ds(2 * spot, 1), :]
            newest = bound_ref[pl.ds(2 * spot + 1, 1), :]
            mine = row // 64 == j
            back_one = jnp.where(mine & (inner == 0), newest, back_one)
            back_two = jnp.where(mine & (inner == 0), older, jnp.where(mine & (inner == 1), newest, back_two))
        within = pos - first_pos
        prev_one = jnp.where(within >= 1, back_one, one_ref[...])
        prev_two = jnp.where(within >= 2, back_two, jnp.where(within == 1, one_ref[...], two_ref[...]))
        conv_out = (taps_ref[0:1] * conv_in + taps_ref[1:2] * prev_one + taps_ref[2:3] * prev_two) * gate
        mixed = jnp.concatenate([attended.astype(bf16), conv_out.astype(bf16)], axis=1)
        out_ref[...] = jnp.dot(mixed, out_w_ref[...], preferred_element_type=f32).astype(bf16)
        line = lax.broadcasted_iota(jnp.int32, (2 * requests, 1), 0)
        target = jnp.full((2 * requests, 1), -1, jnp.int32)
        for q in range(requests):
            before = jnp.where(highs[q] - lows[q] >= 2, highs[q] - 2, -1)
            target = jnp.where(line == q, before, jnp.where(line == requests + q, highs[q] - 1, target))
        chosen = (target == rows_at(part * count, count, core, chip_y, chip_x)).astype(f32).astype(bf16)
        tail_ref[...] = jnp.dot(chosen, conv_in.astype(bf16), preferred_element_type=f32)

    return pl.pallas_call(
        body,
        out_shape=(
            jax.ShapeDtypeStruct((count, width), bf16),
            jax.ShapeDtypeStruct((2 * requests, LANES), f32),
        ),
        in_specs=[smem] * 3 + [vmem] * 9,
        out_specs=(vmem, vmem),
        cost_estimate=tiny,
        scratch_shapes=[pltpu.VMEM((count, LANES), f32)] * 3 + [pltpu.VMEM((2 * CHIPS, LANES), f32)],
        compiler_params=params,
        name="mix_rows",
    )(tok, lengths, cached, projected, local, staged_other, start, taps, *tables, out_wide)


def grow_states(tok, lengths, staged, staged_other, tables, near, columns):
    every = 2 * near
    requests = lengths.shape[1]
    chunk = 512

    def body(tok_ref, length_ref, own_ref, other_ref, left_ref, right_ref, bias_ref, out_ref):
        core, chip_y, chip_x = spot_of(tok_ref[0])
        lows, highs = spans(length_ref, requests)
        first_lane = core * columns
        row = lax.broadcasted_iota(jnp.int32, (64, LANES), 0)
        lane = lax.broadcasted_iota(jnp.int32, (64, LANES), 1)
        pick = ((lane == row + first_lane) & (row < columns)).astype(f32).astype(bf16)
        ones_row = (lax.broadcasted_iota(jnp.int32, (64, 1), 0) == columns).astype(f32)
        total = jnp.zeros((requests * 64, WIDE), f32)
        for k in range(every // chunk):
            if k * chunk < near:
                rows = own_ref[k * chunk : (k + 1) * chunk]
                at = rows_at(k * chunk, chunk, core, chip_y, chip_x)
            else:
                rows = other_ref[k * chunk - near : (k + 1) * chunk - near]
                at = rows_at(k * chunk - near, chunk, 1 - core, chip_y, chip_x)
            phi = features_of(rows, left_ref[...], right_ref[...], bias_ref[...])
            turned = lax.dot_general(pick, rows, (((1,), (1,)), ((), ())), preferred_element_type=f32) + ones_row
            parts = []
            for q in range(requests):
                member = (at >= lows[q]) & (at < highs[q])
                parts.append(jnp.where(member, turned, 0.0).astype(bf16))
            total = total + jnp.dot(jnp.concatenate(parts, axis=0), phi, preferred_element_type=f32)
        for q in range(requests):
            out_ref[q] = total[q * 64 : (q + 1) * 64]

    return pl.pallas_call(
        body,
        out_shape=jax.ShapeDtypeStruct((requests, 64, WIDE), f32),
        in_specs=[smem] * 2 + [vmem] * 5,
        cost_estimate=tiny,
        out_specs=vmem,
        compiler_params=params,
        name="grow_states",
    )(tok, lengths, staged, staged_other, *tables)


def on_device(
    tokens,
    norm_gains,
    qk_weight,
    mixer_weight,
    conv_weight,
    out_weight,
    ffn_weight,
    down_weight,
    cached_states,
    cached_norms,
    conv_cache,
    cached_lengths,
    new_lengths,
    state_source,
):
    tok_rows, width = tokens.shape
    requests, phi_size, columns = cached_states.shape
    head_count = cached_norms.shape[2]
    feature = qk_weight.shape[1] // head_count
    units = ffn_weight.shape[1]
    channels = CORES * columns
    rows_here = CHIPS * tok_rows
    group_now = lax.axis_index("group")
    tok_now = lax.axis_index("tok")
    core = tok_now % CORES
    chip = tok_now // CORES
    chip_y = chip // SIDE_X
    chip_x = chip % SIDE_X
    first_core = core == 0

    def both(own, other, axis):
        return jnp.where(
            first_core,
            jnp.concatenate([own, other], axis=axis),
            jnp.concatenate([other, own], axis=axis),
        )

    tok_here = tok_now[None].astype(jnp.int32)

    packed = pack_slots(
        tok_here, jnp.swapaxes(cached_states, 1, 2), jnp.swapaxes(cached_norms, 1, 2), conv_cache
    )
    normed_own = rms_scale(tokens, norm_gains[0]).astype(bf16)
    normed_own, packed = lax.optimization_barrier((normed_own, packed))
    gathered = lax.all_gather(packed, "group", axis=0, tiled=True)
    normed_pieces = line_gather(normed_own, 0)

    taps_high = conv_weight.astype(bf16)
    taps_low = (conv_weight - taps_high.astype(f32)).astype(bf16)
    taps_rows = jnp.concatenate([taps_high, taps_low, jnp.zeros((2, columns), bf16)], axis=0)
    mixer_rows = mixer_weight.reshape(3 * columns, width)
    early = jnp.concatenate(
        [
            mixer_rows,
            out_weight.reshape(2 * columns, width),
            jnp.concatenate([taps_rows, jnp.zeros((8, width - columns), bf16)], axis=1),
        ],
        axis=0,
    )
    early_other = swap_cores(early)
    normed_pieces, early_other = lax.optimization_barrier((normed_pieces, early_other))
    normed_parts = line_gather(jnp.concatenate(normed_pieces, axis=0), 1)
    early_low = jnp.where(first_core, early, early_other)
    early_high = jnp.where(first_core, early_other, early)

    def chip_rows(k):
        return [early_low[k * columns : (k + 1) * columns], early_high[k * columns : (k + 1) * columns]]

    head_qk = lax.dynamic_slice_in_dim(qk_weight, chip * feature, feature, 1)
    blank16 = jnp.zeros((16, width), bf16)
    in_rows = jnp.concatenate(
        chip_rows(0) + [head_qk[1]] + chip_rows(1) + [head_qk[0]] + chip_rows(2) + [blank16], axis=0
    )
    out_wide = jnp.concatenate(chip_rows(3) + [blank16] + chip_rows(4) + [blank16], axis=0)
    taps_both = jnp.concatenate(
        [early_low[5 * columns :, :columns], early_high[5 * columns :, :columns]], axis=1
    ).astype(f32)
    taps_both = taps_both[:3] + taps_both[3:6]

    lengths = new_lengths[0]
    tables = feature_tables(feature, channels)

    projected = [
        lax.dot_general(piece, in_rows, (((1,), (1,)), ((), ())), preferred_element_type=f32)
        for piece in normed_parts
    ]
    staged = stage_rows(tok_here, new_lengths, projected)
    staged_other = swap_cores(staged)
    added = grow_states(tok_here, new_lengths, staged, staged_other, tables, rows_here, columns)

    staged_other, ffn_weight, down_weight = lax.optimization_barrier((staged_other, ffn_weight, down_weight))
    late = jnp.concatenate([ffn_weight.reshape(2 * units, width), down_weight], axis=0)
    late_other = swap_cores(late)
    pad_units = -(-CORES * units // 128) * 128 - CORES * units
    blank_units = jnp.zeros((pad_units, width), bf16)
    ffn_wide = jnp.concatenate(
        [late[:units], late_other[:units], blank_units, late[units : 2 * units], late_other[units : 2 * units], blank_units], axis=0
    )
    down_wide = jnp.concatenate([late[2 * units :], late_other[2 * units :], blank_units], axis=0)

    local = attend_rows(tok_here, new_lengths, projected, staged, staged_other, channels)
    gathered, local = lax.optimization_barrier((gathered, local))
    own_sources = lax.dynamic_slice_in_dim(state_source[:, 0], group_now * requests, requests)
    wanted = own_sources * requests + jnp.arange(requests, dtype=jnp.int32)
    gathered = pltpu.with_memory_space_constraint(gathered, pltpu.HBM)
    slots = gather_slots(jnp.clip(wanted, 0, gathered.shape[0] - 1), gathered)
    start = unpack_slots(tok_here, cached_lengths, slots, swap_cores(slots), columns)

    taps_wide = jnp.concatenate([taps_both, jnp.zeros((3, LANES - channels), f32)], axis=1)
    mixed = [None] * 4
    last = None
    for k in (2, 1, 3, 0):
        rows = projected[k]
        if last is not None:
            rows = lax.optimization_barrier((rows, last))[0]
        last = mixed[k] = mix_rows(
            tok_here, new_lengths, cached_lengths, rows, local, staged_other, start, taps_wide, tables, out_wide, k, channels
        )
    residual = tokens.astype(f32) + scatter_chips([out for out, _ in mixed])

    grown = turn_slots(cached_lengths, slots, added)
    new_states = jnp.swapaxes(grown[:, :columns, :phi_size], 1, 2)
    norm_rows = jnp.concatenate(
        [grown[:, columns, :phi_size].astype(bf16), jnp.zeros((requests, width - phi_size), bf16)], axis=1
    )

    normed_ffn_own = rms_scale(residual, norm_gains[1]).astype(bf16)
    line = line_gather(jnp.concatenate([normed_ffn_own, norm_rows], axis=0), 0)
    line = jnp.concatenate([piece[:tok_rows] for piece in line] + [piece[tok_rows:] for piece in line], axis=0)
    wide_units = CORES * units + pad_units
    quarter = 4 * tok_rows

    def feed_forward(rows):
        both_parts = lax.dot_general(rows, ffn_wide, (((1,), (1,)), ((), ())), preferred_element_type=f32)
        hidden = (jax.nn.silu(both_parts[:, :wide_units]) * both_parts[:, wide_units:]).astype(bf16)
        return jnp.dot(hidden, down_wide, preferred_element_type=f32).astype(bf16)

    ffn_parts = line_gather(line, 1)
    ffn_partials = [feed_forward(line[:quarter]), None, None, None]
    ffn_parts[2] = lax.optimization_barrier((ffn_parts[2], ffn_partials[0]))[0]
    for k in (1, 2, 3):
        ffn_partials[k] = feed_forward(ffn_parts[k][:quarter])
    layer_out = (residual + scatter_chips(ffn_partials)).astype(bf16)
    stage = jnp.concatenate([piece[quarter:, :phi_size] for piece in ffn_parts], axis=0)
    stage = stage.reshape(CHIPS, requests, phi_size)
    head_index = jnp.arange(head_count, dtype=jnp.int32)
    head_dy = (head_index // SIDE_X - chip_y) % SIDE_Y
    head_dx = (head_index % SIDE_X - chip_x) % SIDE_X
    head_spot = jnp.where(first_core, head_dy * SIDE_X + head_dx, head_dx * SIDE_Y + head_dy)
    new_norms = jnp.transpose(stage[head_spot].astype(f32), (1, 2, 0))

    low_tail = rows_here + 2 * CHIPS
    tail = sum(own for _, own in mixed) + staged_other[low_tail:].astype(f32)
    tail = tail[:, :channels].reshape(2, requests, channels)
    penultimate = jnp.where((lengths >= 2)[:, None], tail[0], start[:, 281, :channels].astype(f32))
    cache = jnp.stack([penultimate, tail[1]], axis=1).astype(bf16)
    new_cache = jnp.where(first_core, cache[..., :columns], cache[..., columns:])
    return (layer_out, new_states, new_norms, new_cache)


def solution(mesh):
    in_specs = (
        P(("group", "tok"), None),
        P(),
        P(),
        P(None, "tok", None),
        P(None, "tok"),
        P(None, "tok", None),
        P(None, "tok", None),
        P("tok", None),
        P("group", None, "tok"),
        P("group", None, None),
        P("group", None, "tok"),
        P("group"),
        P("group", None),
        P(),
    )
    out_specs = (
        P(("group", "tok"), None),
        P("group", None, "tok"),
        P("group", None, None),
        P("group", None, "tok"),
    )
    return jax.shard_map(
        on_device, mesh=mesh, in_specs=in_specs, out_specs=out_specs, check_vma=False
    )
```
